512 devices in a mesh: frames: 8 (over x_hi, y), queries: 64 (over x_lo, z, core).
Axes of the slice: x: 4 (x_hi: 2, x_lo: 2; x = x_hi * 2 + x_lo), y: 4, z: 16, core: 2. Of those that a mesh axis runs over, the one named last changes fastest.
Arguments:
- frame_maps: bfloat16 [16, 4096, 256], P('frames', 'queries'), may hold values from -6 to 6
- query_table: bfloat16 [8, 4096, 256], P('frames', 'queries'), may hold values from -6 to 6
- start_frame: int32 [4096], P('queries'), may hold values from 0 to 15
- row_ids: int32 [4096], P('queries'), may hold values from 0 to 63
- conv1_w: bfloat16 [3, 3, 1, 16], replicated, may hold values from -2 to 2
- conv1_b: float32 [16], replicated, may hold values from -3 to 3
- conv2_w: bfloat16 [3, 3, 16, 32], replicated, may hold values from -0.5 to 0.5
- conv2_b: float32 [32], replicated, may hold values from -3 to 3
- proj_w: bfloat16 [32, 512], replicated, may hold values from -1 to 1
- proj_b: float32 [512], replicated, may hold values from -3 to 3
- time_w: float32 [3, 512], replicated, may hold values from -3 to 3
- time_b: float32 [512], replicated, may hold values from -3 to 3
Outputs:
- track_feats: bfloat16 [4096, 16, 512], P('queries', 'frames')
The draws below stay inside these ranges and needn't reach their ends.
Inputs may be any that keep to these rules, and one draw needn't show every extreme that they name: `start_frame`: the frame in which the query was picked, one of the 16 frames. `row_ids`: a row index within the query's own block of 64 rows.
All inputs are finite; a program needn't handle non-finite values.
Results may differ from the reference program's by a relative error of at most 0.001.
The reference program's roundings to bfloat16 on the way count: a program that leaves them out, or rounds other values in their place, can miss the bound.
Values may be sent and summed in bfloat16 or wider, within the bound.
No kernel may reach another device: no remote copies, remote signals or barrier semaphores. Data moves between devices by JAX's collectives and lax.ppermute only.
A program may use at most 64 MiB of HBM per device.

```python
import jax
import jax.numpy as jnp
from jax import lax

C = 256
MAP = 64
CH1 = 16
CH2 = 32
D = 512
FR_DEV = 2
Q_DEV = 64
WINDOW = 16
QUERY_ALL = 4096
N_FRAMES = 8


def plant(array, own_key, least, high):
    shape = array.shape
    index_at = [jax.random.randint(jax.random.fold_in(own_key, axis), (), 0, shape[axis]) for axis in range(len(shape))]
    array = array.at[tuple(index_at)].set(least)
    longest = shape.index(max(shape))
    index_at[longest] = (index_at[longest] + 1) % shape[longest]
    return array.at[tuple(index_at)].set(high)


def steps_of(own_key, dims, shards, low, largest):
    def one(position, parts):
        steps = jax.random.uniform(jax.random.fold_in(jax.random.fold_in(own_key, 6), position), (parts,), jnp.float32, low / len(shards), largest / len(shards))
        return jnp.repeat(jnp.exp(steps), dims[position] // parts).reshape((-1,) + (1,) * (len(dims) - position - 1))

    loudness = one(*shards[0])
    for cut in shards[1:]:
        loudness = loudness * one(*cut)
    return loudness


def bell_draw(rng, dims, spread, limit, shards=(), kind=jnp.bfloat16):
    values = jax.random.normal(rng, dims, jnp.float32) * spread
    if len(shards) > 0:
        values = steps_of(rng, dims, shards, -0.22, 0.18) * values
    return jnp.clip(values, min=-limit, max=limit).astype(kind)


def setup_inputs(seed: int = 0) -> dict:
    arg_keys = jax.random.split(jax.random.key(seed), 13)
    frame_maps = bell_draw(arg_keys[0], (WINDOW, MAP * MAP, C), 1.0, 6.0, ((0, 8), (1, 64)))
    query_table = bell_draw(arg_keys[1], (N_FRAMES, QUERY_ALL, C), 1.0, 6.0, ((0, 8), (1, 64)))
    start_frame = plant(jax.random.randint(arg_keys[2], (QUERY_ALL,), 0, WINDOW), jax.random.fold_in(arg_keys[2], 1), 0, WINDOW - 1).astype(jnp.int32)
    row_ids = plant(jax.random.randint(arg_keys[3], (QUERY_ALL,), 0, Q_DEV), jax.random.fold_in(arg_keys[3], 1), 0, Q_DEV - 1).astype(jnp.int32)
    conv1_w = bell_draw(arg_keys[4], (3, 3, 1, CH1), 9 ** -0.5, 2.0)
    conv1_b = bell_draw(arg_keys[5], (CH1,), 0.5, 3.0, (), jnp.float32)
    conv2_w = bell_draw(arg_keys[6], (3, 3, CH1, CH2), (9 * CH1) ** -0.5, 0.5)
    conv2_b = bell_draw(arg_keys[7], (CH2,), 0.5, 3.0, (), jnp.float32)
    proj_w = bell_draw(arg_keys[8], (CH2, D), CH2 ** -0.5, 1.0)
    proj_b = bell_draw(arg_keys[9], (D,), 0.5, 3.0, (), jnp.float32)
    time_w = bell_draw(arg_keys[10], (3, D), 0.6, 3.0, (), jnp.float32)
    time_b = bell_draw(arg_keys[11], (D,), 0.5, 3.0, (), jnp.float32)
    return {"frame_maps": frame_maps, "query_table": query_table, "start_frame": start_frame, "row_ids": row_ids, "conv1_w": conv1_w, "conv1_b": conv1_b, "conv2_w": conv2_w, "conv2_b": conv2_b, "proj_w": proj_w, "proj_b": proj_b, "time_w": time_w, "time_b": time_b}


def cost_block(query_rows, maps_one, conv1_w, conv1_b, conv2_w, conv2_b):
    corr = (jnp.dot(query_rows, maps_one.T, preferred_element_type=jnp.float32) * 0.0625).astype(jnp.bfloat16)
    images = corr.reshape(query_rows.shape[0], 1, MAP, MAP)
    layer_one = lax.conv_general_dilated(images, conv1_w, (2, 2), ((1, 1), (1, 1)), dimension_numbers=("NCHW", "HWIO", "NCHW"), preferred_element_type=jnp.float32)
    layer_one = jax.nn.relu(layer_one + conv1_b[None, :, None, None]).astype(jnp.bfloat16)
    layer_two = lax.conv_general_dilated(layer_one, conv2_w, (2, 2), ((1, 1), (1, 1)), dimension_numbers=("NCHW", "HWIO", "NCHW"), preferred_element_type=jnp.float32)
    layer_two = jax.nn.relu(layer_two + conv2_b[None, :, None, None])
    return jnp.mean(layer_two, axis=(2, 3)).astype(jnp.bfloat16)


def reference(frame_maps, query_table, start_frame, row_ids, conv1_w, conv1_b, conv2_w, conv2_b, proj_w, proj_b, time_w, time_b):
    owner = (start_frame // FR_DEV).astype(jnp.int32)
    table_row = (jnp.arange(QUERY_ALL, dtype=jnp.int32) // Q_DEV * Q_DEV + row_ids).astype(jnp.int32)
    qfeat = query_table[owner, table_row]
    row_block = min(1024, QUERY_ALL)
    query_blocks = qfeat.reshape(QUERY_ALL // row_block, row_block, C)

    def per_frame(maps_one):
        def per_block(query_rows):
            return cost_block(query_rows, maps_one, conv1_w, conv1_b, conv2_w, conv2_b)
        return lax.map(per_block, query_blocks).reshape(QUERY_ALL, CH2)

    pooled = lax.map(per_frame, frame_maps)
    proj = (jnp.dot(pooled.reshape(WINDOW * QUERY_ALL, CH2), proj_w, preferred_element_type=jnp.float32) + proj_b).astype(jnp.bfloat16)
    proj = proj.reshape(WINDOW, QUERY_ALL, D).astype(jnp.float32)
    padded = jnp.pad(proj, ((1, 1), (0, 0), (0, 0)))
    mixed = time_w[0] * padded[:-2] + time_w[1] * padded[1:-1] + time_w[2] * padded[2:] + time_b
    return jnp.transpose(mixed, (1, 0, 2)).astype(jnp.bfloat16)
```

```python
import functools

import jax
import jax.numpy as jnp
from jax import lax
from jax.experimental import pallas as pl
from jax.experimental.pallas import tpu as pltpu
from jax.sharding import Mesh, PartitionSpec as P

MAP = 64
CH1 = 16
CH2 = 32
HALF1 = MAP // 2
HALF2 = MAP // 4
ROW1 = HALF1 * CH1
ROW2 = HALF2 * CH2
BF = jnp.bfloat16
F32 = jnp.float32
INTERPRET = False


def weights_kernel(w1_ref, w2_ref, a_ref, b_ref):
    def iota(shape, dim):
        return lax.broadcasted_iota(jnp.int32, shape, dim)

    pick = (iota((CH1, ROW1), 1) % CH1 == iota((CH1, ROW1), 0)).astype(BF)
    w1_wide = jnp.dot(w1_ref[...], pick, preferred_element_type=F32)
    in_x = iota((MAP, ROW1), 0)
    out_x = iota((MAP, ROW1), 1) // CH1
    a_ref[0:MAP, :] = jnp.zeros((MAP, ROW1), BF)
    for dy in range(3):
        block = jnp.zeros((MAP, ROW1), F32)
        for dx in range(3):
            tap = w1_wide[3 * dy + dx : 3 * dy + dx + 1, :]
            block = jnp.where(in_x == 2 * out_x + dx - 1, tap, block)
        a_ref[MAP * (dy + 1) : MAP * (dy + 2), :] = block.astype(BF)

    rows = (iota((ROW1, CH1), 0) % CH1 == iota((ROW1, CH1), 1)).astype(BF)
    cols = (iota((CH2, ROW2), 1) % CH2 == iota((CH2, ROW2), 0)).astype(BF)
    in_x = iota((ROW1, ROW2), 0) // CH1
    out_x = iota((ROW1, ROW2), 1) // CH2
    for dy in range(3):
        block = jnp.zeros((ROW1, ROW2), F32)
        for dx in range(3):
            wide = jnp.dot(w2_ref[3 * dy + dx], cols, preferred_element_type=F32).astype(BF)
            tall = jnp.dot(rows, wide, preferred_element_type=F32)
            block = jnp.where(in_x == 2 * out_x + dx - 1, tall, block)
        b_ref[ROW1 * dy : ROW1 * (dy + 1), :] = block.astype(BF)


def banded_weights(conv1_w, conv2_w):
    return pl.pallas_call(
        weights_kernel,
        out_shape=(
            jax.ShapeDtypeStruct((4 * MAP, ROW1), BF),
            jax.ShapeDtypeStruct((3 * ROW1, ROW2), BF),
        ),
        cost_estimate=pl.CostEstimate(flops=400_000_000, bytes_accessed=2_000_000, transcendentals=0),
        interpret=INTERPRET,
    )(conv1_w.reshape(9, CH1), conv2_w.reshape(9, CH1, CH2))


def cost_kernel(z_count, where_ref, q_ref, own_ref, *refs):
    far_refs = refs[:-9]
    a_ref, b_ref, bias1_ref, bias2_ref, kept_ref, sent_ref, corr, hid, acc = refs[-9:]
    x, z = where_ref[0], where_ref[1]
    n = q_ref.shape[0]
    corr[0, :, 0:128] = jnp.zeros((n, 128), BF)
    hid[0, :, 0:ROW1] = jnp.zeros((n, ROW1), BF)
    q = q_ref[...]

    def put(low, high, chip):
        cells = jnp.concatenate([low[0:MAP], high[0:MAP], low[MAP:], high[MAP:]], axis=0)
        got = lax.dot_general(q, cells, (((1,), (1,)), ((), ())), preferred_element_type=F32)
        got = (got * 0.0625).astype(BF)
        for side in range(2):
            part = got[:, 128 * side : 128 * (side + 1)]
            y = (x if side == 0 else 1 - x) * z_count + chip
            corr[y, :, 128:256] = part
            corr[y + 1, :, 0:128] = part

    put(own_ref[0], own_ref[1], z)
    distance = 0
    for ref in far_refs:
        per = ref.shape[0] // 4
        for i in range(per):
            distance += 1
            k = 2 * i
            put(ref[k], ref[k + 1], lax.rem(z + z_count - distance, z_count))
            if 2 * distance < z_count:
                k += 2 * per
                put(ref[k], ref[k + 1], lax.rem(z + distance, z_count))

    bias1 = bias1_ref[...]
    rows1 = 8
    for t in range(HALF1 // rows1):
        lhs = corr[rows1 * t : rows1 * (t + 1)].reshape(rows1 * n, 256)
        got = jnp.dot(lhs, a_ref[...], preferred_element_type=F32)
        got = jnp.maximum(got + bias1, 0.0).astype(BF).reshape(rows1, n, ROW1)
        for s in range(rows1):
            y = rows1 * t + s
            j = y // 2
            if y % 2 == 0:
                hid[j, :, ROW1 : 2 * ROW1] = got[s]
            else:
                hid[j, :, 2 * ROW1 : 3 * ROW1] = got[s]
                hid[j + 1, :, 0:ROW1] = got[s]

    bias2 = bias2_ref[...]
    half = ROW2 // 2
    rows2 = 4
    acc[...] = jnp.zeros(acc.shape, F32)
    for t in range(HALF2 // rows2):
        tile = slice(rows2 * t, rows2 * (t + 1))
        left = jnp.zeros((rows2 * n, half), F32)
        for dy in range(3):
            k = slice(ROW1 * dy, ROW1 * dy + ROW1 // 2)
            left += jnp.dot(
                hid[tile, :, k].reshape(rows2 * n, ROW1 // 2),
                b_ref[k, 0:half],
                preferred_element_type=F32,
            )
        right = jnp.dot(
            hid[tile].reshape(rows2 * n, 3 * ROW1), b_ref[:, half:], preferred_element_type=F32
        )
        left = jnp.maximum(left + bias2[:, :half], 0.0).reshape(rows2, n, half)
        right = jnp.maximum(right + bias2[:, half:], 0.0).reshape(rows2, n, half)
        acc[:, :half] += jnp.sum(left, axis=0)
        acc[:, half:] += jnp.sum(right, axis=0)
    total = acc[:, 0:128]
    for k in range(1, ROW2 // 128):
        total = total + acc[:, 128 * k : 128 * (k + 1)]
    total = (total[:, 0:32] + total[:, 32:64]) + (total[:, 64:96] + total[:, 96:128])
    pooled = (total * (1.0 / (HALF2 * HALF2))).astype(BF)
    kept_ref[...] = pooled[: n // 2]
    sent_ref[...] = pooled[n // 2 :]


def pooled_costs(where, queries, own, far, a, b, bias1, bias2):
    n = queries.shape[0]
    z_count = MAP // 4
    vmem = pl.BlockSpec(memory_space=pltpu.VMEM)

    return pl.pallas_call(
        functools.partial(cost_kernel, z_count),
        out_shape=(jax.ShapeDtypeStruct((n // 2, CH2), BF),) * 2,
        in_specs=[pl.BlockSpec(memory_space=pltpu.SMEM)] + [vmem] * (6 + len(far)),
        out_specs=(vmem, vmem),
        scratch_shapes=[
            pltpu.VMEM((HALF1 + 1, n, 256), BF),
            pltpu.VMEM((HALF2 + 1, n, 3 * ROW1), BF),
            pltpu.VMEM((n, ROW2), F32),
        ],
        cost_estimate=pl.CostEstimate(
            flops=5_000_000_000, bytes_accessed=4_000_000, transcendentals=0
        ),
        interpret=INTERPRET,
    )(where, queries, own, *far, a, b, bias1, bias2)


def per_device(
    sizes,
    frame_maps,
    query_table,
    start_frame,
    row_ids,
    conv1_w,
    conv1_b,
    conv2_w,
    conv2_b,
    proj_w,
    proj_b,
    time_w,
    time_b,
):
    xh_count, y_count, _, z_count, _ = sizes
    frame_count = xh_count * y_count
    x = lax.axis_index("xl")
    z = lax.axis_index("z")
    frame_block = lax.axis_index("xh") * y_count + lax.axis_index("y")
    where = jnp.stack([x, z]).astype(jnp.int32)
    swap = [(0, 1), (1, 0)]

    a, b = banded_weights(conv1_w, conv2_w)
    bias1 = jnp.tile(conv1_b, HALF1)[None, :]
    bias2 = jnp.tile(conv2_b, HALF2)[None, :]

    mine = jnp.where(x == 0, frame_maps[0], frame_maps[1])
    other = jnp.where(x == 0, frame_maps[1], frame_maps[0])

    cells_here = query_table.shape[1]
    owned = start_frame // frame_maps.shape[0] == frame_block
    chosen = (row_ids[:, None] == jnp.arange(cells_here)[None, :]) & owned[:, None]
    queries = jnp.dot(chosen.astype(BF), query_table[0], preferred_element_type=F32).astype(BF)
    other, queries = lax.optimization_barrier((other, queries))

    def flip(axis, count, step):
        return lambda v: lax.ppermute(v, axis, [(i, i ^ step) for i in range(count)])

    def along(block, distance):
        pairs = []
        for i in range(z_count):
            pairs.append((2 * i, 2 * ((i + distance) % z_count)))
            pairs.append((2 * i + 1, 2 * ((i - distance) % z_count) + 1))
        return lax.ppermute(block, ("z", "c"), pairs)

    def both(block):
        return lax.all_gather(block, "c", axis=0, tiled=True)

    theirs = lax.ppermute(other, "xl", swap)
    got = flip("y", y_count, 1)(queries)
    theirs, queries = lax.optimization_barrier((theirs, queries + got))

    own = lax.all_gather(jnp.concatenate([mine, theirs], axis=0), "c", axis=0)
    near, next_near = along(own, 1), along(own, 2)
    if y_count > 2:
        queries = queries + flip("y", y_count, 2)(queries)
    near, next_near, queries = lax.optimization_barrier((near, next_near, queries))

    moving = jnp.concatenate([near, next_near], axis=0)
    far = [both(moving)]
    moving = along(moving, 2)
    if xh_count > 1:
        queries = queries + flip("xh", xh_count, 1)(queries)
    moving, queries = lax.optimization_barrier((moving, queries))

    far.append(both(moving))
    moving = along(moving, 2)
    queries = jnp.concatenate([queries, lax.ppermute(queries, "xl", swap)], axis=0)
    moving, queries = lax.optimization_barrier((moving, queries))

    far.append(both(moving))
    moving = along(moving, 2)
    far.append(both(moving))

    kept, sent = pooled_costs(where, queries, own, far, a, b, bias1, bias2)

    def frame_pairs(cross):
        pairs = []
        for f in range(frame_count):
            if f > 0:
                pairs.append((2 * (f - 1) + 1, 2 * f + (0 if cross else 1)))
            if f < frame_count - 1:
                pairs.append((2 * (f + 1), 2 * f + (1 if cross else 0)))
        return pairs

    partner = lax.ppermute(sent, "xl", swap)
    straight = lax.ppermute(kept, ("xh", "y", "xl"), frame_pairs(False))
    crossed = lax.ppermute(sent, ("xh", "y", "xl"), frame_pairs(True))
    first = x == 0
    around = jnp.stack(
        [
            jnp.where(first, crossed, straight),
            jnp.where(first, kept, partner),
            jnp.where(first, partner, kept),
            jnp.where(first, straight, crossed),
        ]
    )
    projected = lax.reduce_precision(
        jnp.einsum("fqc,cd->fqd", around, proj_w, preferred_element_type=F32) + proj_b, 8, 7
    )
    index = jnp.arange(4)
    valid = ((index > 0) | (frame_block > 0)) & ((index < 3) | (frame_block < frame_count - 1))
    wide = jnp.where(valid[:, None, None], projected, 0.0)
    mixed = time_w[0] * wide[:-2] + time_w[1] * wide[1:-1] + time_w[2] * wide[2:] + time_b
    return jnp.transpose(mixed, (1, 0, 2)).astype(BF)


def solution(mesh):

    frames, _ = mesh.devices.shape
    sizes = (frames // 4 or 1, min(frames, 4), 2, MAP // 4, 2)
    fine = Mesh(mesh.devices.reshape(sizes), ("xh", "y", "xl", "z", "c"))
    fr = ("xh", "y")
    qs = ("xl", "z", "c")
    placed = (P(fr, qs, None), P(fr, qs, None), P(qs), P(qs)) + (P(),) * 8
    return jax.shard_map(
        functools.partial(per_device, sizes),
        mesh=fine,
        in_specs=placed,
        out_specs=P(qs, fr, None),
        check_vma=False,
    )
```

```python
import functools

import jax
import jax.numpy as jnp
from jax import lax
from jax.experimental import pallas as pl
from jax.experimental.pallas import tpu as pltpu
from jax.sharding import Mesh, PartitionSpec as P

MAP = 64
CH1 = 16
CH2 = 32
HALF1 = MAP // 2
HALF2 = MAP // 4
ROW1 = HALF1 * CH1
ROW2 = HALF2 * CH2
BF = jnp.bfloat16
F32 = jnp.float32
INTERPRET = False


def iota(shape, dim):
    return lax.broadcasted_iota(jnp.int32, shape, dim)


def first_kernel(where_ref, maps_ref, table_ref, start_ref, rows_ref, out_ref, mine_ref):
    x, frame_block = where_ref[0], where_ref[2]
    cells = table_ref.shape[1]
    frames_here = maps_ref.shape[0]
    mine_ref[...] = maps_ref[x]
    out_ref[0:cells, :] = maps_ref[1 - x]
    low = frame_block * frames_here
    owned = (start_ref[...] >= low) & (start_ref[...] < low + frames_here)
    row = jnp.where(owned, rows_ref[...], -1)
    chosen = (iota((cells, row.shape[1]), 0) == row).astype(BF)
    got = lax.dot_general(
        chosen, table_ref[0], (((0,), (0,)), ((), ())), preferred_element_type=F32
    )
    out_ref[cells:, :] = got.astype(BF)


def first_message(where, frame_maps, query_table, start_frame, row_ids):
    cells, channels = frame_maps.shape[1:]
    count = start_frame.shape[0]
    vmem = pl.BlockSpec(memory_space=pltpu.VMEM)
    return pl.pallas_call(
        first_kernel,
        out_shape=(
            jax.ShapeDtypeStruct((cells + count, channels), BF),
            jax.ShapeDtypeStruct((cells, channels), BF),
        ),
        in_specs=[pl.BlockSpec(memory_space=pltpu.SMEM)] + [vmem] * 4,
        out_specs=(vmem, vmem),
        cost_estimate=pl.CostEstimate(flops=2_000_000, bytes_accessed=200_000, transcendentals=0),
        compiler_params=pltpu.CompilerParams(vmem_limit_bytes=4 << 20),
        interpret=INTERPRET,
    )(where, frame_maps, query_table, start_frame[None, :], row_ids[None, :])


def merge_kernel(message_ref, mine_ref, theirs_ref, block_ref, queries_ref):
    cells = mine_ref.shape[0]
    block_ref[0:cells, :] = mine_ref[...]
    block_ref[cells:, :] = theirs_ref[0:cells, :]
    count = message_ref.shape[0] - cells
    queries_ref[0:count, :] = message_ref[cells:, :]
    queries_ref[count:, :] = theirs_ref[cells:, :]


def merged(message, mine, theirs):
    cells, channels = mine.shape
    count = message.shape[0] - cells
    vmem = pl.BlockSpec(memory_space=pltpu.VMEM)
    return pl.pallas_call(
        merge_kernel,
        out_shape=(
            jax.ShapeDtypeStruct((2 * cells, channels), BF),
            jax.ShapeDtypeStruct((2 * count, channels), BF),
        ),
        in_specs=[vmem] * 3,
        out_specs=(vmem, vmem),
        cost_estimate=pl.CostEstimate(flops=0, bytes_accessed=300_000, transcendentals=0),
        compiler_params=pltpu.CompilerParams(vmem_limit_bytes=4 << 20),
        interpret=INTERPRET,
    )(message, mine, theirs)


def weights_kernel(w1_ref, w2_ref, bias1_ref, bias2_ref, a_ref, b_ref, wide1_ref, wide2_ref):
    spread = (iota((CH1, ROW1), 1) % CH1 == iota((CH1, ROW1), 0)).astype(BF)
    wide1_ref[...] = jnp.concatenate([bias1_ref[...]] * HALF1, axis=1)
    wide2_ref[...] = jnp.concatenate([bias2_ref[...]] * HALF2, axis=1)

    in_x = iota((MAP, ROW1), 0)
    out_x = iota((MAP, ROW1), 1) // CH1
    a_ref[0:MAP, :] = jnp.zeros((MAP, ROW1), BF)
    for dy in range(3):
        wide = jnp.dot(w1_ref[dy], spread, preferred_element_type=F32)
        block = jnp.zeros((MAP, ROW1), F32)
        for dx in range(3):
            block = jnp.where(in_x == 2 * out_x + dx - 1, wide[dx : dx + 1, :], block)
        a_ref[MAP * (dy + 1) : MAP * (dy + 2), :] = block.astype(BF)

    b_ref[...] = jnp.zeros(b_ref.shape, BF)
    for dy in range(3):
        taps = jnp.concatenate([w2_ref[3 * dy + dx] for dx in range(3)], axis=0)
        taps = jnp.concatenate([taps] * (128 // CH2), axis=1)
        for out_x in range(HALF2):
            low = 2 * out_x - 1
            skip = max(0, -low)
            lane = CH2 * out_x
            part = lane % 128
            b_ref[
                ROW1 * dy + CH1 * (low + skip) : ROW1 * dy + CH1 * (low + 3), lane : lane + CH2
            ] = taps[CH1 * skip :, part : part + CH2]


def banded_weights(conv1_w, conv1_b, conv2_w, conv2_b):
    return pl.pallas_call(
        weights_kernel,
        out_shape=(
            jax.ShapeDtypeStruct((4 * MAP, ROW1), BF),
            jax.ShapeDtypeStruct((3 * ROW1, ROW2), BF),
            jax.ShapeDtypeStruct((1, ROW1), F32),
            jax.ShapeDtypeStruct((1, ROW2), F32),
        ),
        cost_estimate=pl.CostEstimate(flops=50_000_000, bytes_accessed=2_000_000, transcendentals=0),
        compiler_params=pltpu.CompilerParams(vmem_limit_bytes=8 << 20),
        interpret=INTERPRET,
    )(
        jnp.transpose(conv1_w, (0, 2, 1, 3)).reshape(3, 3, CH1),
        conv2_w.reshape(9, CH1, CH2),
        conv1_b[None, :],
        conv2_b[None, :],
    )


def cost_kernel(z_count, where_ref, q_ref, own_ref, *refs):
    far_refs = refs[:-9]
    a_ref, b_ref, bias1_ref, bias2_ref, kept_ref, sent_ref, corr, hid, acc = refs[-9:]
    x, z = where_ref[0], where_ref[1]
    n = q_ref.shape[0]
    corr[0, :, 0:128] = jnp.zeros((n, 128), BF)
    hid[0, :, 0:ROW1] = jnp.zeros((n, ROW1), BF)
    q = q_ref[...]

    def put(low, high, chip):
        cells = jnp.concatenate([low[0:MAP], high[0:MAP], low[MAP:], high[MAP:]], axis=0)
        got = lax.dot_general(q, cells, (((1,), (1,)), ((), ())), preferred_element_type=F32)
        got = (got * 0.0625).astype(BF)
        for side in range(2):
            part = got[:, 128 * side : 128 * (side + 1)]
            y = (x if side == 0 else 1 - x) * z_count + chip
            corr[y, :, 128:256] = part
            corr[y + 1, :, 0:128] = part

    put(own_ref[0], own_ref[1], z)
    distance = 0
    for ref in far_refs:
        per = ref.shape[0] // 4
        for i in range(per):
            distance += 1
            k = 2 * i
            put(ref[k], ref[k + 1], lax.rem(z + z_count - distance, z_count))
            if 2 * distance < z_count:
                k += 2 * per
                put(ref[k], ref[k + 1], lax.rem(z + distance, z_count))

    bias1 = bias1_ref[...]
    rows1 = 8
    for t in range(HALF1 // rows1):
        lhs = corr[rows1 * t : rows1 * (t + 1)].reshape(rows1 * n, 256)
        got = jnp.dot(lhs, a_ref[...], preferred_element_type=F32)
        got = jnp.maximum(got + bias1, 0.0).astype(BF).reshape(rows1, n, ROW1)
        for s in range(rows1):
            y = rows1 * t + s
            j = y // 2
            if y % 2 == 0:
                hid[j, :, ROW1 : 2 * ROW1] = got[s]
            else:
                hid[j, :, 2 * ROW1 : 3 * ROW1] = got[s]
                hid[j + 1, :, 0:ROW1] = got[s]

    bias2 = bias2_ref[...]
    half = ROW2 // 2
    rows2 = 4
    acc[...] = jnp.zeros(acc.shape, F32)
    for t in range(HALF2 // rows2):
        tile = slice(rows2 * t, rows2 * (t + 1))
        left = jnp.zeros((rows2 * n, half), F32)
        for dy in range(3):
            k = slice(ROW1 * dy, ROW1 * dy + ROW1 // 2)
            left += jnp.dot(
                hid[tile, :, k].reshape(rows2 * n, ROW1 // 2),
                b_ref[k, 0:half],
                preferred_element_type=F32,
            )
        right = jnp.dot(
            hid[tile].reshape(rows2 * n, 3 * ROW1), b_ref[:, half:], preferred_element_type=F32
        )
        left = jnp.maximum(left + bias2[:, :half], 0.0).reshape(rows2, n, half)
        right = jnp.maximum(right + bias2[:, half:], 0.0).reshape(rows2, n, half)
        acc[:, :half] += jnp.sum(left, axis=0)
        acc[:, half:] += jnp.sum(right, axis=0)
    total = acc[:, 0:128]
    for k in range(1, ROW2 // 128):
        total = total + acc[:, 128 * k : 128 * (k + 1)]
    total = (total[:, 0:32] + total[:, 32:64]) + (total[:, 64:96] + total[:, 96:128])
    pooled = (total * (1.0 / (HALF2 * HALF2))).astype(BF)
    kept_ref[...] = pooled[: n // 2]
    sent_ref[...] = pooled[n // 2 :]


def pooled_costs(where, queries, own, far, a, b, bias1, bias2):
    n = queries.shape[0]
    z_count = MAP // 4
    vmem = pl.BlockSpec(memory_space=pltpu.VMEM)

    return pl.pallas_call(
        functools.partial(cost_kernel, z_count),
        out_shape=(jax.ShapeDtypeStruct((n // 2, CH2), BF),) * 2,
        in_specs=[pl.BlockSpec(memory_space=pltpu.SMEM)] + [vmem] * (6 + len(far)),
        out_specs=(vmem, vmem),
        scratch_shapes=[
            pltpu.VMEM((HALF1 + 1, n, 256), BF),
            pltpu.VMEM((HALF2 + 1, n, 3 * ROW1), BF),
            pltpu.VMEM((n, ROW2), F32),
        ],
        cost_estimate=pl.CostEstimate(
            flops=5_000_000_000, bytes_accessed=4_000_000, transcendentals=0
        ),
        compiler_params=pltpu.CompilerParams(vmem_limit_bytes=28 << 20),
        interpret=INTERPRET,
    )(where, queries, own, *far, a, b, bias1, bias2)


def tail_kernel(
    frame_count,
    where_ref,
    kept_ref,
    partner_ref,
    straight_ref,
    crossed_ref,
    proj_w_ref,
    proj_b_ref,
    time_w_ref,
    time_b_ref,
    out_ref,
):
    x, frame_block = where_ref[0], where_ref[2]
    first = x == 0
    kept, partner = kept_ref[...], partner_ref[...]
    straight, crossed = straight_ref[...], crossed_ref[...]
    around = [
        jnp.where(first, crossed, straight),
        jnp.where(first, kept, partner),
        jnp.where(first, partner, kept),
        jnp.where(first, straight, crossed),
    ]
    valid = [frame_block > 0, None, None, frame_block < frame_count - 1]
    wide = []
    for pooled, there in zip(around, valid):
        got = jnp.dot(pooled, proj_w_ref[...], preferred_element_type=F32) + proj_b_ref[...]
        got = got.astype(BF).astype(F32)
        if there is not None:
            got = jnp.where(there, got, 0.0)
        wide.append(got)
    for t in range(2):
        mixed = (
            time_w_ref[0:1, :] * wide[t]
            + time_w_ref[1:2, :] * wide[t + 1]
            + time_w_ref[2:3, :] * wide[t + 2]
            + time_b_ref[...]
        )
        out_ref[:, t, :] = mixed.astype(BF)


def tail(frame_count, where, pooled, proj_w, proj_b, time_w, time_b):
    count, width = pooled[0].shape[0], proj_w.shape[1]
    vmem = pl.BlockSpec(memory_space=pltpu.VMEM)
    return pl.pallas_call(
        functools.partial(tail_kernel, frame_count),
        out_shape=jax.ShapeDtypeStruct((count, 2, width), BF),
        in_specs=[pl.BlockSpec(memory_space=pltpu.SMEM)] + [vmem] * 8,
        out_specs=vmem,
        compiler_params=pltpu.CompilerParams(vmem_limit_bytes=8 << 20),
        interpret=INTERPRET,
    )(where, *pooled, proj_w, proj_b[None, :], time_w, time_b[None, :])


def per_device(
    sizes,
    frame_maps,
    query_table,
    start_frame,
    row_ids,
    conv1_w,
    conv1_b,
    conv2_w,
    conv2_b,
    proj_w,
    proj_b,
    time_w,
    time_b,
):
    xh_count, y_count, _, z_count, _ = sizes
    frame_count = xh_count * y_count
    x = lax.axis_index("xl")
    z = lax.axis_index("z")
    frame_block = lax.axis_index("xh") * y_count + lax.axis_index("y")
    where = jnp.stack([x, z, frame_block]).astype(jnp.int32)
    swap = [(0, 1), (1, 0)]

    def flip(axis, count, step):
        return lambda v: lax.ppermute(v, axis, [(i, i ^ step) for i in range(count)])

    def along(block, distance):
        pairs = []
        for i in range(z_count):
            pairs.append((2 * i, 2 * ((i + distance) % z_count)))
            pairs.append((2 * i + 1, 2 * ((i - distance) % z_count) + 1))
        return lax.ppermute(block, ("z", "c"), pairs)

    def both(block):
        return lax.all_gather(block, "c", axis=0, tiled=True)

    message, mine = first_message(where, frame_maps, query_table, start_frame, row_ids)
    theirs = lax.ppermute(message, "xl", swap)
    weights = banded_weights(conv1_w, conv1_b, conv2_w, conv2_b)
    theirs, weights = lax.optimization_barrier((theirs, weights))

    block, queries = merged(message, mine, theirs)
    own = lax.all_gather(block, "c", axis=0)
    own, queries = lax.optimization_barrier((own, queries))
    near, next_near = along(own, 1), along(own, 2)
    queries = queries + flip("y", y_count, 1)(queries)
    near, next_near, queries = lax.optimization_barrier((near, next_near, queries))

    moving = [jnp.concatenate([near, next_near], axis=0)]
    moving.append(along(moving[-1], 2))
    if y_count > 2:
        queries = queries + flip("y", y_count, 2)(queries)
    moving, queries = lax.optimization_barrier((moving, queries))

    moving.append(along(moving[-1], 2))
    if xh_count > 1:
        queries = queries + flip("xh", xh_count, 1)(queries)
    moving, queries = lax.optimization_barrier((moving, queries))

    last = along(moving[-1], 2)
    far = [both(v) for v in moving]
    last, far = lax.optimization_barrier((last, far))
    far.append(both(last))

    kept, sent = pooled_costs(where, queries, own, far, *weights)

    def frame_pairs(cross):
        pairs = []
        for f in range(frame_count):
            if f > 0:
                pairs.append((2 * (f - 1) + 1, 2 * f + (0 if cross else 1)))
            if f < frame_count - 1:
                pairs.append((2 * (f + 1), 2 * f + (1 if cross else 0)))
        return pairs

    partner = lax.ppermute(sent, "xl", swap)
    straight = lax.ppermute(kept, ("xh", "y", "xl"), frame_pairs(False))
    crossed = lax.ppermute(sent, ("xh", "y", "xl"), frame_pairs(True))
    pooled = (kept, partner, straight, crossed)
    return tail(frame_count, where, pooled, proj_w, proj_b, time_w, time_b)


def solution(mesh):

    frames, _ = mesh.devices.shape
    sizes = (frames // 4 or 1, min(frames, 4), 2, MAP // 4, 2)
    fine = Mesh(mesh.devices.reshape(sizes), ("xh", "y", "xl", "z", "c"))
    fr = ("xh", "y")
    qs = ("xl", "z", "c")
    placed = (P(fr, qs, None), P(fr, qs, None), P(qs), P(qs)) + (P(),) * 8
    return jax.shard_map(
        functools.partial(per_device, sizes),
        mesh=fine,
        in_specs=placed,
        out_specs=P(qs, fr, None),
        check_vma=False,
    )
```

```python
import functools

import jax
import jax.numpy as jnp
from jax import lax
from jax.experimental import pallas as pl
from jax.experimental.pallas import tpu as pltpu
from jax.sharding import Mesh, PartitionSpec as P


MAP = 64
CH1 = 16
CH2 = 32
HALF1 = MAP // 2
HALF2 = MAP // 4
ROW1 = HALF1 * CH1
ROW2 = HALF2 * CH2
BF = jnp.bfloat16
F32 = jnp.float32
INTERPRET = False


def iota(shape, dim):
    return lax.broadcasted_iota(jnp.int32, shape, dim)


def in_hbm(array):
    if INTERPRET:
        return array
    return pltpu.with_memory_space_constraint(array, pltpu.HBM)


def query_kernel(where_ref, table_hbm, start_hbm, rows_hbm, out_ref, table, start, rows, sems):
    frames_here = 2
    copies = [
        pltpu.make_async_copy(table_hbm, table, sems.at[0]),
        pltpu.make_async_copy(start_hbm, start, sems.at[1]),
        pltpu.make_async_copy(rows_hbm, rows, sems.at[2]),
    ]
    for copy in copies:
        copy.start()
    for copy in copies:
        copy.wait()
    low = where_ref[2] * frames_here
    owned = (start[...] >= low) & (start[...] < low + frames_here)
    row = jnp.where(owned, rows[...], -1)
    chosen = (iota((table.shape[1], row.shape[1]), 0) == row).astype(BF)
    got = lax.dot_general(chosen, table[0], (((0,), (0,)), ((), ())), preferred_element_type=F32)
    out_ref[...] = got.astype(BF)


def own_queries(where, query_table, start_frame, row_ids):
    count = start_frame.shape[0]
    hbm = pl.BlockSpec(memory_space=pltpu.HBM)
    return pl.pallas_call(
        query_kernel,
        out_shape=jax.ShapeDtypeStruct((count, query_table.shape[2]), BF),
        in_specs=[pl.BlockSpec(memory_space=pltpu.SMEM)] + [hbm] * 3,
        out_specs=pl.BlockSpec(memory_space=pltpu.VMEM),
        scratch_shapes=[
            pltpu.VMEM(query_table.shape, BF),
            pltpu.VMEM((1, count), jnp.int32),
            pltpu.VMEM((1, count), jnp.int32),
            pltpu.SemaphoreType.DMA((3,)),
        ],
        cost_estimate=pl.CostEstimate(flops=2_000_000, bytes_accessed=200_000, transcendentals=0),
        compiler_params=pltpu.CompilerParams(vmem_limit_bytes=4 << 20),
        interpret=INTERPRET,
    )(where, *map(in_hbm, (query_table, start_frame[None, :], row_ids[None, :])))


def pick_kernel(where_ref, all_ref, out_ref):
    x = where_ref[0]
    cells = all_ref.shape[2]
    for core in range(2):
        for side in range(2):
            out_ref[core, cells * side : cells * (side + 1), :] = all_ref[2 * side + core, x]


def picked(where, gathered):
    cells, channels = gathered.shape[2:]
    vmem = pl.BlockSpec(memory_space=pltpu.VMEM)
    return pl.pallas_call(
        pick_kernel,
        out_shape=jax.ShapeDtypeStruct((2, 2 * cells, channels), BF),
        in_specs=[pl.BlockSpec(memory_space=pltpu.SMEM), vmem],
        out_specs=vmem,
        cost_estimate=pl.CostEstimate(flops=0, bytes_accessed=300_000, transcendentals=0),
        compiler_params=pltpu.CompilerParams(vmem_limit_bytes=4 << 20),
        interpret=INTERPRET,
    )(where, gathered)


def weights_kernel(*refs):
    a_ref, b_ref, wide1_ref, wide2_ref, w1_ref, w2_ref, bias1_ref, bias2_ref, sems = refs[4:]
    copies = [
        pltpu.make_async_copy(refs[k], refs[8 + k], sems.at[k]) for k in range(4)
    ]
    for copy in copies:
        copy.start()
    b_ref[...] = jnp.zeros(b_ref.shape, BF)
    for copy in copies:
        copy.wait()
    spread = (iota((CH1, ROW1), 1) % CH1 == iota((CH1, ROW1), 0)).astype(BF)
    wide1_ref[...] = jnp.concatenate([bias1_ref[...]] * HALF1, axis=1)
    wide2_ref[...] = jnp.concatenate([bias2_ref[...]] * HALF2, axis=1)

    in_x = iota((MAP, ROW1), 0)
    out_x = iota((MAP, ROW1), 1) // CH1
    a_ref[0:MAP, :] = jnp.zeros((MAP, ROW1), BF)
    for dy in range(3):
        wide = jnp.dot(w1_ref[dy], spread, preferred_element_type=F32)
        block = jnp.zeros((MAP, ROW1), F32)
        for dx in range(3):
            block = jnp.where(in_x == 2 * out_x + dx - 1, wide[dx : dx + 1, :], block)
        a_ref[MAP * (dy + 1) : MAP * (dy + 2), :] = block.astype(BF)

    for dy in range(3):
        taps = jnp.concatenate([w2_ref[3 * dy + dx] for dx in range(3)], axis=0)
        taps = jnp.concatenate([taps] * (128 // CH2), axis=1)
        for out_x in range(HALF2):
            low = 2 * out_x - 1
            skip = max(0, -low)
            lane = CH2 * out_x
            part = lane % 128
            b_ref[
                ROW1 * dy + CH1 * (low + skip) : ROW1 * dy + CH1 * (low + 3), lane : lane + CH2
            ] = taps[CH1 * skip :, part : part + CH2]


def banded_weights(conv1_w, conv1_b, conv2_w, conv2_b):
    return pl.pallas_call(
        weights_kernel,
        out_shape=(
            jax.ShapeDtypeStruct((4 * MAP, ROW1), BF),
            jax.ShapeDtypeStruct((3 * ROW1, ROW2), BF),
            jax.ShapeDtypeStruct((1, ROW1), F32),
            jax.ShapeDtypeStruct((1, ROW2), F32),
        ),
        in_specs=[pl.BlockSpec(memory_space=pltpu.HBM)] * 4,
        scratch_shapes=[
            pltpu.VMEM((3, 3, CH1), BF),
            pltpu.VMEM((9, CH1, CH2), BF),
            pltpu.VMEM((1, CH1), F32),
            pltpu.VMEM((1, CH2), F32),
            pltpu.SemaphoreType.DMA((4,)),
        ],
        cost_estimate=pl.CostEstimate(flops=50_000_000, bytes_accessed=2_000_000, transcendentals=0),
        compiler_params=pltpu.CompilerParams(vmem_limit_bytes=8 << 20),
        interpret=INTERPRET,
    )(
        *map(
            in_hbm,
            (
                jnp.transpose(conv1_w, (0, 2, 1, 3)).reshape(3, 3, CH1),
                conv2_w.reshape(9, CH1, CH2),
                conv1_b[None, :],
                conv2_b[None, :],
            ),
        )
    )


def cost_kernel(z_count, where_ref, kept_q_ref, sent_q_ref, own_ref, *refs):
    far_refs = refs[:-9]
    a_ref, b_ref, bias1_ref, bias2_ref, kept_ref, sent_ref, corr, hid, acc = refs[-9:]
    z = where_ref[1]
    n = 2 * kept_q_ref.shape[0]
    corr[0, :, 0:128] = jnp.zeros((n, 128), BF)
    hid[0, :, 0:ROW1] = jnp.zeros((n, ROW1), BF)
    q = jnp.concatenate([kept_q_ref[...], sent_q_ref[...]], axis=0)

    def put(low, high, chip):
        cells = jnp.concatenate([low[0:MAP], high[0:MAP], low[MAP:], high[MAP:]], axis=0)
        got = lax.dot_general(q, cells, (((1,), (1,)), ((), ())), preferred_element_type=F32)
        got = (got * 0.0625).astype(BF)
        for side in range(2):
            part = got[:, 128 * side : 128 * (side + 1)]
            y = side * z_count + chip
            corr[y, :, 128:256] = part
            corr[y + 1, :, 0:128] = part

    put(own_ref[0], own_ref[1], z)
    distance = 0
    for ref in far_refs:
        per = ref.shape[0] // 4
        for i in range(per):
            distance += 1
            k = 2 * i
            put(ref[k], ref[k + 1], lax.rem(z + z_count - distance, z_count))
            if 2 * distance < z_count:
                k += 2 * per
                put(ref[k], ref[k + 1], lax.rem(z + distance, z_count))

    bias1 = bias1_ref[...]
    rows1 = 8
    for t in range(HALF1 // rows1):
        lhs = corr[rows1 * t : rows1 * (t + 1)].reshape(rows1 * n, 256)
        got = jnp.dot(lhs, a_ref[...], preferred_element_type=F32)
        got = jnp.maximum(got + bias1, 0.0).astype(BF).reshape(rows1, n, ROW1)
        for s in range(rows1):
            y = rows1 * t + s
            j = y // 2
            if y % 2 == 0:
                hid[j, :, ROW1 : 2 * ROW1] = got[s]
            else:
                hid[j, :, 2 * ROW1 : 3 * ROW1] = got[s]
                hid[j + 1, :, 0:ROW1] = got[s]

    bias2 = bias2_ref[...]
    half = ROW2 // 2
    rows2 = 4
    acc[...] = jnp.zeros(acc.shape, F32)
    for t in range(HALF2 // rows2):
        tile = slice(rows2 * t, rows2 * (t + 1))
        left = jnp.zeros((rows2 * n, half), F32)
        for dy in range(3):
            k = slice(ROW1 * dy, ROW1 * dy + ROW1 // 2)
            left += jnp.dot(
                hid[tile, :, k].reshape(rows2 * n, ROW1 // 2),
                b_ref[k, 0:half],
                preferred_element_type=F32,
            )
        right = jnp.dot(
            hid[tile].reshape(rows2 * n, 3 * ROW1), b_ref[:, half:], preferred_element_type=F32
        )
        left = jnp.maximum(left + bias2[:, :half], 0.0).reshape(rows2, n, half)
        right = jnp.maximum(right + bias2[:, half:], 0.0).reshape(rows2, n, half)
        acc[:, :half] += jnp.sum(left, axis=0)
        acc[:, half:] += jnp.sum(right, axis=0)
    total = acc[:, 0:128]
    for k in range(1, ROW2 // 128):
        total = total + acc[:, 128 * k : 128 * (k + 1)]
    total = (total[:, 0:32] + total[:, 32:64]) + (total[:, 64:96] + total[:, 96:128])
    pooled = (total * (1.0 / (HALF2 * HALF2))).astype(BF)
    kept_ref[...] = pooled[: n // 2]
    sent_ref[...] = pooled[n // 2 :]


def pooled_costs(where, kept_q, sent_q, own, far, a, b, bias1, bias2):
    n = 2 * kept_q.shape[0]
    z_count = MAP // 4
    vmem = pl.BlockSpec(memory_space=pltpu.VMEM)

    return pl.pallas_call(
        functools.partial(cost_kernel, z_count),
        out_shape=(jax.ShapeDtypeStruct((n // 2, CH2), BF),) * 2,
        in_specs=[pl.BlockSpec(memory_space=pltpu.SMEM)] + [vmem] * (7 + len(far)),
        out_specs=(vmem, vmem),
        scratch_shapes=[
            pltpu.VMEM((HALF1 + 1, n, 256), BF),
            pltpu.VMEM((HALF2 + 1, n, 3 * ROW1), BF),
            pltpu.VMEM((n, ROW2), F32),
        ],
        cost_estimate=pl.CostEstimate(
            flops=5_000_000_000, bytes_accessed=4_000_000, transcendentals=0
        ),
        compiler_params=pltpu.CompilerParams(vmem_limit_bytes=28 << 20),
        interpret=INTERPRET,
    )(where, kept_q, sent_q, own, *far, a, b, bias1, bias2)


def tail_kernel(
    frame_count,
    where_ref,
    kept_ref,
    partner_ref,
    straight_ref,
    crossed_ref,
    proj_w_ref,
    proj_b_ref,
    time_w_ref,
    time_b_ref,
    out_ref,
):
    x, frame_block = where_ref[0], where_ref[2]
    first = x == 0
    kept, partner = kept_ref[...], partner_ref[...]
    straight, crossed = straight_ref[...], crossed_ref[...]
    around = [
        jnp.where(first, crossed, straight),
        jnp.where(first, kept, partner),
        jnp.where(first, partner, kept),
        jnp.where(first, straight, crossed),
    ]
    valid = [frame_block > 0, None, None, frame_block < frame_count - 1]
    wide = []
    for pooled, there in zip(around, valid):
        got = jnp.dot(pooled, proj_w_ref[...], preferred_element_type=F32) + proj_b_ref[...]
        got = got.astype(BF).astype(F32)
        if there is not None:
            got = jnp.where(there, got, 0.0)
        wide.append(got)
    for t in range(2):
        mixed = (
            time_w_ref[0:1, :] * wide[t]
            + time_w_ref[1:2, :] * wide[t + 1]
            + time_w_ref[2:3, :] * wide[t + 2]
            + time_b_ref[...]
        )
        out_ref[:, t, :] = mixed.astype(BF)


def tail(frame_count, where, pooled, proj_w, proj_b, time_w, time_b):
    count, width = pooled[0].shape[0], proj_w.shape[1]
    vmem = pl.BlockSpec(memory_space=pltpu.VMEM)
    return pl.pallas_call(
        functools.partial(tail_kernel, frame_count),
        out_shape=jax.ShapeDtypeStruct((count, 2, width), BF),
        in_specs=[pl.BlockSpec(memory_space=pltpu.SMEM)] + [vmem] * 8,
        out_specs=vmem,
        compiler_params=pltpu.CompilerParams(vmem_limit_bytes=8 << 20),
        interpret=INTERPRET,
    )(where, *pooled, proj_w, proj_b[None, :], time_w, time_b[None, :])


def one_device(
    sizes,
    frame_maps,
    query_table,
    start_frame,
    row_ids,
    conv1_w,
    conv1_b,
    conv2_w,
    conv2_b,
    proj_w,
    proj_b,
    time_w,
    time_b,
):
    xh_count, y_count, _, z_count, _ = sizes
    frame_count = xh_count * y_count
    x = lax.axis_index("xl")
    z = lax.axis_index("z")
    frame_block = lax.axis_index("xh") * y_count + lax.axis_index("y")
    where = jnp.stack([x, z, frame_block]).astype(jnp.int32)
    swap = [(0, 1), (1, 0)]

    def flip(axis, count, step):
        return lambda v: lax.ppermute(v, axis, [(i, i ^ step) for i in range(count)])

    def along(block, distance):
        pairs = []
        for i in range(z_count):
            pairs.append((2 * i, 2 * ((i + distance) % z_count)))
            pairs.append((2 * i + 1, 2 * ((i - distance) % z_count) + 1))
        return lax.ppermute(block, ("z", "c"), pairs)

    def both(block):
        return lax.all_gather(block, "c", axis=0, tiled=True)

    def behind(value, earlier):
        return lax.optimization_barrier((value, earlier))[0]

    gathered = lax.all_gather(frame_maps, ("xl", "c"), axis=0)
    own = picked(where, gathered)
    weights = banded_weights(conv1_w, conv1_b, conv2_w, conv2_b)
    near = along(own, 1)
    next_near = along(own, 2)
    queries = own_queries(where, query_table, start_frame, row_ids)
    queries = queries + flip("y", y_count, 1)(behind(queries, own))
    near, next_near, weights = lax.optimization_barrier((near, next_near, weights))

    far = []
    moving = jnp.concatenate([near, next_near], axis=0)
    if y_count > 2:
        queries = queries + flip("y", y_count, 2)(behind(queries, moving))
    far.append(both(moving))
    moving = along(moving, 2)
    moving, far = lax.optimization_barrier((moving, far))

    if xh_count > 1:
        queries = queries + flip("xh", xh_count, 1)(behind(queries, moving))
    far.append(both(moving))
    moving = along(moving, 2)
    moving, far = lax.optimization_barrier((moving, far))

    kept_q = queries
    sent_q = lax.ppermute(behind(queries, moving), "xl", swap)
    far.append(both(moving))
    moving = along(moving, 2)
    moving, far = lax.optimization_barrier((moving, far))
    far.append(both(moving))

    kept, sent = pooled_costs(where, kept_q, sent_q, own, far, *weights)

    def frame_pairs(cross):
        pairs = []
        for f in range(frame_count):
            if f > 0:
                pairs.append((2 * (f - 1) + 1, 2 * f + (0 if cross else 1)))
            if f < frame_count - 1:
                pairs.append((2 * (f + 1), 2 * f + (1 if cross else 0)))
        return pairs

    partner = lax.ppermute(sent, "xl", swap)
    straight = lax.ppermute(kept, ("xh", "y", "xl"), frame_pairs(False))
    crossed = lax.ppermute(sent, ("xh", "y", "xl"), frame_pairs(True))
    pooled = (kept, partner, straight, crossed)
    return tail(frame_count, where, pooled, proj_w, proj_b, time_w, time_b)


def solution(mesh):

    frames, _ = mesh.devices.shape
    sizes = (frames // 4 or 1, min(frames, 4), 2, MAP // 4, 2)
    fine = Mesh(mesh.devices.reshape(sizes), ("xh", "y", "xl", "z", "c"))
    fr = ("xh", "y")
    qs = ("xl", "z", "c")
    placed = (P(fr, qs, None), P(fr, qs, None), P(qs), P(qs)) + (P(),) * 8
    return jax.shard_map(
        functools.partial(one_device, sizes),
        mesh=fine,
        in_specs=placed,
        out_specs=P(qs, fr, None),
        check_vma=False,
    )
```

```python
import functools

import jax
import jax.numpy as jnp
from jax import lax
from jax.experimental import pallas as pl
from jax.experimental.pallas import tpu as pltpu
from jax.sharding import Mesh, PartitionSpec as P


MAP = 64
CH1 = 16
CH2 = 32
HALF1 = MAP // 2
HALF2 = MAP // 4
ROW1 = HALF1 * CH1
ROW2 = HALF2 * CH2
BF = jnp.bfloat16
F32 = jnp.float32
INTERPRET = False


def iota(shape, dim):
    return lax.broadcasted_iota(jnp.int32, shape, dim)


def in_hbm(array):
    if INTERPRET:
        return array
    return pltpu.with_memory_space_constraint(array, pltpu.HBM)


def opening_kernel(
    where_ref, maps_hbm, table_hbm, start_hbm, rows_hbm, out_ref, table, start, rows, sems
):
    frames_here, cells = maps_hbm.shape[0], maps_hbm.shape[1]
    copies = [
        pltpu.make_async_copy(start_hbm, start, sems.at[0]),
        pltpu.make_async_copy(rows_hbm, rows, sems.at[1]),
        pltpu.make_async_copy(table_hbm, table, sems.at[2]),
    ]
    for f in range(frames_here):
        part = out_ref.at[pl.ds(cells * f, cells)]
        copies.append(pltpu.make_async_copy(maps_hbm.at[f], part, sems.at[3 + f]))
    for copy in copies:
        copy.start()
    for copy in copies[:3]:
        copy.wait()
    low = where_ref[2] * frames_here
    owned = (start[...] >= low) & (start[...] < low + frames_here)
    row = jnp.where(owned, rows[...], -1)
    chosen = (iota((table.shape[1], row.shape[1]), 0) == row).astype(BF)
    got = lax.dot_general(chosen, table[0], (((0,), (0,)), ((), ())), preferred_element_type=F32)
    out_ref[frames_here * cells :, :] = got.astype(BF)
    for copy in copies[3:]:
        copy.wait()


def opening(where, frame_maps, query_table, start_frame, row_ids):
    frames_here, cells, channels = frame_maps.shape
    count = start_frame.shape[0]
    hbm = pl.BlockSpec(memory_space=pltpu.HBM)
    arrays = (frame_maps, query_table, start_frame[None, :], row_ids[None, :])
    return pl.pallas_call(
        opening_kernel,
        out_shape=jax.ShapeDtypeStruct((frames_here * cells + count, channels), BF),
        in_specs=[pl.BlockSpec(memory_space=pltpu.SMEM)] + [hbm] * 4,
        out_specs=pl.BlockSpec(memory_space=pltpu.VMEM),
        scratch_shapes=[
            pltpu.VMEM(query_table.shape, BF),
            pltpu.VMEM((1, count), jnp.int32),
            pltpu.VMEM((1, count), jnp.int32),
            pltpu.SemaphoreType.DMA((5,)),
        ],
        cost_estimate=pl.CostEstimate(flops=2_000_000, bytes_accessed=200_000, transcendentals=0),
        compiler_params=pltpu.CompilerParams(vmem_limit_bytes=4 << 20),
        interpret=INTERPRET,
    )(where, *map(in_hbm, arrays))


def pick_kernel(where_ref, all_ref, block_ref, queries_ref):
    x, core = where_ref[0], where_ref[3]
    cells = block_ref.shape[1] // 2
    frame = pl.ds(pl.multiple_of(cells * x, cells), cells)
    for c in range(2):
        for side in range(2):
            block_ref[c, cells * side : cells * (side + 1), :] = all_ref[2 * side + c, frame, :]
    count = queries_ref.shape[0] // 2
    first = 2 * cells
    queries_ref[0:count, :] = all_ref[2 * x + core, first : first + count, :]
    queries_ref[count:, :] = all_ref[2 * (1 - x) + core, first : first + count, :]


def picked(where, gathered, cells):
    channels = gathered.shape[2]
    count = gathered.shape[1] - 2 * cells
    vmem = pl.BlockSpec(memory_space=pltpu.VMEM)
    return pl.pallas_call(
        pick_kernel,
        out_shape=(
            jax.ShapeDtypeStruct((2, 2 * cells, channels), BF),
            jax.ShapeDtypeStruct((2 * count, channels), BF),
        ),
        in_specs=[pl.BlockSpec(memory_space=pltpu.SMEM), vmem],
        out_specs=(vmem, vmem),
        cost_estimate=pl.CostEstimate(flops=0, bytes_accessed=300_000, transcendentals=0),
        compiler_params=pltpu.CompilerParams(vmem_limit_bytes=4 << 20),
        interpret=INTERPRET,
    )(where, gathered)


def weights_kernel(*refs):
    a_ref, b_ref, wide1_ref, wide2_ref, w1_ref, w2_ref, bias1_ref, bias2_ref, sems = refs[4:]
    copies = [
        pltpu.make_async_copy(refs[k], refs[8 + k], sems.at[k]) for k in range(4)
    ]
    for copy in copies:
        copy.start()
    b_ref[...] = jnp.zeros(b_ref.shape, BF)
    for copy in copies:
        copy.wait()
    spread = (iota((CH1, ROW1), 1) % CH1 == iota((CH1, ROW1), 0)).astype(BF)
    wide1_ref[...] = jnp.concatenate([bias1_ref[...]] * HALF1, axis=1)
    wide2_ref[...] = jnp.concatenate([bias2_ref[...]] * HALF2, axis=1)

    in_x = iota((MAP, ROW1), 0)
    out_x = iota((MAP, ROW1), 1) // CH1
    a_ref[0:MAP, :] = jnp.zeros((MAP, ROW1), BF)
    for dy in range(3):
        wide = jnp.dot(w1_ref[dy], spread, preferred_element_type=F32)
        block = jnp.zeros((MAP, ROW1), F32)
        for dx in range(3):
            block = jnp.where(in_x == 2 * out_x + dx - 1, wide[dx : dx + 1, :], block)
        a_ref[MAP * (dy + 1) : MAP * (dy + 2), :] = block.astype(BF)

    for dy in range(3):
        taps = jnp.concatenate([w2_ref[3 * dy + dx] for dx in range(3)], axis=0)
        taps = jnp.concatenate([taps] * (128 // CH2), axis=1)
        for out_x in range(HALF2):
            low = 2 * out_x - 1
            skip = max(0, -low)
            lane = CH2 * out_x
            part = lane % 128
            b_ref[
                ROW1 * dy + CH1 * (low + skip) : ROW1 * dy + CH1 * (low + 3), lane : lane + CH2
            ] = taps[CH1 * skip :, part : part + CH2]


def banded_weights(conv1_w, conv1_b, conv2_w, conv2_b):
    return pl.pallas_call(
        weights_kernel,
        out_shape=(
            jax.ShapeDtypeStruct((4 * MAP, ROW1), BF),
            jax.ShapeDtypeStruct((3 * ROW1, ROW2), BF),
            jax.ShapeDtypeStruct((1, ROW1), F32),
            jax.ShapeDtypeStruct((1, ROW2), F32),
        ),
        in_specs=[pl.BlockSpec(memory_space=pltpu.HBM)] * 4,
        scratch_shapes=[
            pltpu.VMEM((3, 3, CH1), BF),
            pltpu.VMEM((9, CH1, CH2), BF),
            pltpu.VMEM((1, CH1), F32),
            pltpu.VMEM((1, CH2), F32),
            pltpu.SemaphoreType.DMA((4,)),
        ],
        cost_estimate=pl.CostEstimate(flops=50_000_000, bytes_accessed=2_000_000, transcendentals=0),
        compiler_params=pltpu.CompilerParams(vmem_limit_bytes=8 << 20),
        interpret=INTERPRET,
    )(
        *map(
            in_hbm,
            (
                jnp.transpose(conv1_w, (0, 2, 1, 3)).reshape(3, 3, CH1),
                conv2_w.reshape(9, CH1, CH2),
                conv1_b[None, :],
                conv2_b[None, :],
            ),
        )
    )


def cost_kernel(z_count, where_ref, q_ref, own_ref, *refs):
    far_refs = refs[:-9]
    a_ref, b_ref, bias1_ref, bias2_ref, kept_ref, sent_ref, corr, hid, acc = refs[-9:]
    z = where_ref[1]
    n = q_ref.shape[0]
    corr[0, :, 0:128] = jnp.zeros((n, 128), BF)
    hid[0, :, 0:ROW1] = jnp.zeros((n, ROW1), BF)
    q = q_ref[...]

    def put(low, high, chip):
        cells = jnp.concatenate([low[0:MAP], high[0:MAP], low[MAP:], high[MAP:]], axis=0)
        got = lax.dot_general(q, cells, (((1,), (1,)), ((), ())), preferred_element_type=F32)
        got = (got * 0.0625).astype(BF)
        for side in range(2):
            part = got[:, 128 * side : 128 * (side + 1)]
            y = side * z_count + chip
            corr[y, :, 128:256] = part
            corr[y + 1, :, 0:128] = part

    put(own_ref[0], own_ref[1], z)
    distance = 0
    for ref in far_refs:
        per = ref.shape[0] // 4
        for i in range(per):
            distance += 1
            k = 2 * i
            put(ref[k], ref[k + 1], lax.rem(z + z_count - distance, z_count))
            if 2 * distance < z_count:
                k += 2 * per
                put(ref[k], ref[k + 1], lax.rem(z + distance, z_count))

    bias1 = bias1_ref[...]
    rows1 = 8
    for t in range(HALF1 // rows1):
        lhs = corr[rows1 * t : rows1 * (t + 1)].reshape(rows1 * n, 256)
        got = jnp.dot(lhs, a_ref[...], preferred_element_type=F32)
        got = jnp.maximum(got + bias1, 0.0).astype(BF).reshape(rows1, n, ROW1)
        for s in range(rows1):
            y = rows1 * t + s
            j = y // 2
            if y % 2 == 0:
                hid[j, :, ROW1 : 2 * ROW1] = got[s]
            else:
                hid[j, :, 2 * ROW1 : 3 * ROW1] = got[s]
                hid[j + 1, :, 0:ROW1] = got[s]

    bias2 = bias2_ref[...]
    half = ROW2 // 2
    rows2 = 4
    acc[...] = jnp.zeros(acc.shape, F32)
    for t in range(HALF2 // rows2):
        tile = slice(rows2 * t, rows2 * (t + 1))
        left = jnp.zeros((rows2 * n, half), F32)
        for dy in range(3):
            k = slice(ROW1 * dy, ROW1 * dy + ROW1 // 2)
            left += jnp.dot(
                hid[tile, :, k].reshape(rows2 * n, ROW1 // 2),
                b_ref[k, 0:half],
                preferred_element_type=F32,
            )
        right = jnp.dot(
            hid[tile].reshape(rows2 * n, 3 * ROW1), b_ref[:, half:], preferred_element_type=F32
        )
        left = jnp.maximum(left + bias2[:, :half], 0.0).reshape(rows2, n, half)
        right = jnp.maximum(right + bias2[:, half:], 0.0).reshape(rows2, n, half)
        acc[:, :half] += jnp.sum(left, axis=0)
        acc[:, half:] += jnp.sum(right, axis=0)
    total = acc[:, 0:128]
    for k in range(1, ROW2 // 128):
        total = total + acc[:, 128 * k : 128 * (k + 1)]
    total = (total[:, 0:32] + total[:, 32:64]) + (total[:, 64:96] + total[:, 96:128])
    pooled = (total * (1.0 / (HALF2 * HALF2))).astype(BF)
    kept_ref[...] = pooled[: n // 2]
    sent_ref[...] = pooled[n // 2 :]


def pooled_costs(where, queries, own, far, a, b, bias1, bias2):
    n = queries.shape[0]
    z_count = MAP // 4
    vmem = pl.BlockSpec(memory_space=pltpu.VMEM)

    return pl.pallas_call(
        functools.partial(cost_kernel, z_count),
        out_shape=(jax.ShapeDtypeStruct((n // 2, CH2), BF),) * 2,
        in_specs=[pl.BlockSpec(memory_space=pltpu.SMEM)] + [vmem] * (6 + len(far)),
        out_specs=(vmem, vmem),
        scratch_shapes=[
            pltpu.VMEM((HALF1 + 1, n, 256), BF),
            pltpu.VMEM((HALF2 + 1, n, 3 * ROW1), BF),
            pltpu.VMEM((n, ROW2), F32),
        ],
        cost_estimate=pl.CostEstimate(
            flops=5_000_000_000, bytes_accessed=4_000_000, transcendentals=0
        ),
        compiler_params=pltpu.CompilerParams(vmem_limit_bytes=28 << 20),
        interpret=INTERPRET,
    )(where, queries, own, *far, a, b, bias1, bias2)


def tail_kernel(
    frame_count,
    where_ref,
    kept_ref,
    partner_ref,
    straight_ref,
    crossed_ref,
    proj_w_ref,
    proj_b_ref,
    time_w_ref,
    time_b_ref,
    out_ref,
):
    x, frame_block = where_ref[0], where_ref[2]
    first = x == 0
    kept, partner = kept_ref[...], partner_ref[...]
    straight, crossed = straight_ref[...], crossed_ref[...]
    around = [
        jnp.where(first, crossed, straight),
        jnp.where(first, kept, partner),
        jnp.where(first, partner, kept),
        jnp.where(first, straight, crossed),
    ]
    valid = [frame_block > 0, None, None, frame_block < frame_count - 1]
    wide = []
    for pooled, there in zip(around, valid):
        got = jnp.dot(pooled, proj_w_ref[...], preferred_element_type=F32) + proj_b_ref[...]
        got = got.astype(BF).astype(F32)
        if there is not None:
            got = jnp.where(there, got, 0.0)
        wide.append(got)
    for t in range(2):
        mixed = (
            time_w_ref[0:1, :] * wide[t]
            + time_w_ref[1:2, :] * wide[t + 1]
            + time_w_ref[2:3, :] * wide[t + 2]
            + time_b_ref[...]
        )
        out_ref[:, t, :] = mixed.astype(BF)


def tail(frame_count, where, pooled, proj_w, proj_b, time_w, time_b):
    count, width = pooled[0].shape[0], proj_w.shape[1]
    vmem = pl.BlockSpec(memory_space=pltpu.VMEM)
    return pl.pallas_call(
        functools.partial(tail_kernel, frame_count),
        out_shape=jax.ShapeDtypeStruct((count, 2, width), BF),
        in_specs=[pl.BlockSpec(memory_space=pltpu.SMEM)] + [vmem] * 8,
        out_specs=vmem,
        compiler_params=pltpu.CompilerParams(vmem_limit_bytes=8 << 20),
        interpret=INTERPRET,
    )(where, *pooled, proj_w, proj_b[None, :], time_w, time_b[None, :])


def one_device(
    sizes,
    frame_maps,
    query_table,
    start_frame,
    row_ids,
    conv1_w,
    conv1_b,
    conv2_w,
    conv2_b,
    proj_w,
    proj_b,
    time_w,
    time_b,
):
    xh_count, y_count, _, z_count, _ = sizes
    frame_count = xh_count * y_count
    x = lax.axis_index("xl")
    z = lax.axis_index("z")
    frame_block = lax.axis_index("xh") * y_count + lax.axis_index("y")
    where = jnp.stack([x, z, frame_block, lax.axis_index("c")]).astype(jnp.int32)
    swap = [(0, 1), (1, 0)]

    def flip(axis, count, step):
        return lambda v: lax.ppermute(v, axis, [(i, i ^ step) for i in range(count)])

    def along(block, distance):
        pairs = []
        for i in range(z_count):
            pairs.append((2 * i, 2 * ((i + distance) % z_count)))
            pairs.append((2 * i + 1, 2 * ((i - distance) % z_count) + 1))
        return lax.ppermute(block, ("z", "c"), pairs)

    def both(block):
        return lax.all_gather(block, "c", axis=0, tiled=True)

    def behind(value, earlier):
        return lax.optimization_barrier((value, earlier))[0]

    message = opening(where, frame_maps, query_table, start_frame, row_ids)
    gathered = lax.all_gather(message, ("xl", "c"), axis=0)
    own, queries = picked(where, gathered, frame_maps.shape[1])
    weights = banded_weights(conv1_w, conv1_b, conv2_w, conv2_b)
    near = []
    for distance in (1, 2, 3):
        near.append(along(own, distance))
    queries = queries + flip("y", y_count, 1)(queries)
    near[1], near[2] = lax.optimization_barrier((near[1], near[2]))

    pair = jnp.concatenate([near[1], near[2]], axis=0)
    far5 = along(pair, 3)
    far4 = along(near[0], 3)
    if y_count > 2:
        queries = queries + flip("y", y_count, 2)(behind(queries, pair))
    near1 = both(near[0])
    far5, near1, weights = lax.optimization_barrier((far5, near1, weights))

    far7 = along(far5, 2)
    if xh_count > 1:
        queries = queries + flip("xh", xh_count, 1)(behind(queries, far5))
    spread = [near1, both(behind(pair, far5)), both(behind(far4, far5)), both(far5)]
    far7, spread, queries = lax.optimization_barrier((far7, spread, queries))
    spread.append(both(far7))

    kept, sent = pooled_costs(where, queries, own, spread, *weights)

    def frame_pairs(cross):
        pairs = []
        for f in range(frame_count):
            if f > 0:
                pairs.append((2 * (f - 1) + 1, 2 * f + (0 if cross else 1)))
            if f < frame_count - 1:
                pairs.append((2 * (f + 1), 2 * f + (1 if cross else 0)))
        return pairs

    partner = lax.ppermute(sent, "xl", swap)
    straight = lax.ppermute(kept, ("xh", "y", "xl"), frame_pairs(False))
    crossed = lax.ppermute(sent, ("xh", "y", "xl"), frame_pairs(True))
    pooled = (kept, partner, straight, crossed)
    return tail(frame_count, where, pooled, proj_w, proj_b, time_w, time_b)


def solution(mesh):

    frames, _ = mesh.devices.shape
    sizes = (frames // 4 or 1, min(frames, 4), 2, MAP // 4, 2)
    fine = Mesh(mesh.devices.reshape(sizes), ("xh", "y", "xl", "z", "c"))
    fr = ("xh", "y")
    qs = ("xl", "z", "c")
    placed = (P(fr, qs, None), P(fr, qs, None), P(qs), P(qs)) + (P(),) * 8
    return jax.shard_map(
        functools.partial(one_device, sizes),
        mesh=fine,
        in_specs=placed,
        out_specs=P(qs, fr, None),
        check_vma=False,
    )
```

```python
import functools

import jax
import jax.numpy as jnp
from jax import lax
from jax.experimental import pallas as pl
from jax.experimental.pallas import tpu as pltpu
from jax.sharding import Mesh, PartitionSpec as P


MAP = 64
CH1 = 16
CH2 = 32
HALF1 = MAP // 2
HALF2 = MAP // 4
ROW1 = HALF1 * CH1
ROW2 = HALF2 * CH2
BF = jnp.bfloat16
F32 = jnp.float32
INTERPRET = False


def iota(shape, dim):
    return lax.broadcasted_iota(jnp.int32, shape, dim)


def in_hbm(array):
    if INTERPRET:
        return array
    return pltpu.with_memory_space_constraint(array, pltpu.HBM)


def opening_kernel(
    where_ref, maps_hbm, table_hbm, start_hbm, rows_hbm, out_ref, table, start, rows, sems
):
    frames_here, cells = maps_hbm.shape[0], maps_hbm.shape[1]
    copies = [
        pltpu.make_async_copy(start_hbm, start, sems.at[0]),
        pltpu.make_async_copy(rows_hbm, rows, sems.at[1]),
        pltpu.make_async_copy(table_hbm, table, sems.at[2]),
    ]
    for f in range(frames_here):
        part = out_ref.at[pl.ds(cells * f, cells)]
        copies.append(pltpu.make_async_copy(maps_hbm.at[f], part, sems.at[3 + f]))
    for copy in copies:
        copy.start()
    for copy in copies[:3]:
        copy.wait()
    low = where_ref[2] * frames_here
    owned = (start[...] >= low) & (start[...] < low + frames_here)
    row = jnp.where(owned, rows[...], -1)
    chosen = (iota((table.shape[1], row.shape[1]), 0) == row).astype(BF)
    got = lax.dot_general(chosen, table[0], (((0,), (0,)), ((), ())), preferred_element_type=F32)
    out_ref[frames_here * cells :, :] = got.astype(BF)
    for copy in copies[3:]:
        copy.wait()


def opening(where, frame_maps, query_table, start_frame, row_ids):
    frames_here, cells, channels = frame_maps.shape
    count = start_frame.shape[0]
    hbm = pl.BlockSpec(memory_space=pltpu.HBM)
    arrays = (frame_maps, query_table, start_frame[None, :], row_ids[None, :])
    return pl.pallas_call(
        opening_kernel,
        out_shape=jax.ShapeDtypeStruct((frames_here * cells + count, channels), BF),
        in_specs=[pl.BlockSpec(memory_space=pltpu.SMEM)] + [hbm] * 4,
        out_specs=pl.BlockSpec(memory_space=pltpu.VMEM),
        scratch_shapes=[
            pltpu.VMEM(query_table.shape, BF),
            pltpu.VMEM((1, count), jnp.int32),
            pltpu.VMEM((1, count), jnp.int32),
            pltpu.SemaphoreType.DMA((5,)),
        ],
        cost_estimate=pl.CostEstimate(flops=2_000_000, bytes_accessed=200_000, transcendentals=0),
        compiler_params=pltpu.CompilerParams(vmem_limit_bytes=4 << 20),
        interpret=INTERPRET,
    )(where, *map(in_hbm, arrays))


def pick_kernel(where_ref, all_ref, block_ref, queries_ref):
    x, core = where_ref[0], where_ref[3]
    cells = block_ref.shape[1] // 2
    frame = pl.ds(pl.multiple_of(cells * x, cells), cells)
    for c in range(2):
        for side in range(2):
            block_ref[c, cells * side : cells * (side + 1), :] = all_ref[2 * side + c, frame, :]
    count = queries_ref.shape[0] // 2
    first = 2 * cells
    queries_ref[0:count, :] = all_ref[2 * x + core, first : first + count, :]
    queries_ref[count:, :] = all_ref[2 * (1 - x) + core, first : first + count, :]


def picked(where, gathered, cells):
    channels = gathered.shape[2]
    count = gathered.shape[1] - 2 * cells
    vmem = pl.BlockSpec(memory_space=pltpu.VMEM)
    return pl.pallas_call(
        pick_kernel,
        out_shape=(
            jax.ShapeDtypeStruct((2, 2 * cells, channels), BF),
            jax.ShapeDtypeStruct((2 * count, channels), BF),
        ),
        in_specs=[pl.BlockSpec(memory_space=pltpu.SMEM), vmem],
        out_specs=(vmem, vmem),
        cost_estimate=pl.CostEstimate(flops=0, bytes_accessed=300_000, transcendentals=0),
        compiler_params=pltpu.CompilerParams(vmem_limit_bytes=4 << 20),
        interpret=INTERPRET,
    )(where, gathered)


def weights_kernel(*refs):
    a_ref, b_ref, wide1_ref, wide2_ref, w1_ref, w2_ref, bias1_ref, bias2_ref, sems = refs[4:]
    copies = [
        pltpu.make_async_copy(refs[k], refs[8 + k], sems.at[k]) for k in range(4)
    ]
    for copy in copies:
        copy.start()
    b_ref[...] = jnp.zeros(b_ref.shape, BF)
    for copy in copies:
        copy.wait()
    spread = (iota((CH1, ROW1), 1) % CH1 == iota((CH1, ROW1), 0)).astype(BF)
    wide1_ref[...] = jnp.concatenate([bias1_ref[...]] * HALF1, axis=1)
    wide2_ref[...] = jnp.concatenate([bias2_ref[...]] * HALF2, axis=1)

    in_x = iota((MAP, ROW1), 0)
    out_x = iota((MAP, ROW1), 1) // CH1
    a_ref[0:MAP, :] = jnp.zeros((MAP, ROW1), BF)
    for dy in range(3):
        wide = jnp.dot(w1_ref[dy], spread, preferred_element_type=F32)
        block = jnp.zeros((MAP, ROW1), F32)
        for dx in range(3):
            block = jnp.where(in_x == 2 * out_x + dx - 1, wide[dx : dx + 1, :], block)
        a_ref[MAP * (dy + 1) : MAP * (dy + 2), :] = block.astype(BF)

    for dy in range(3):
        taps = jnp.concatenate([w2_ref[3 * dy + dx] for dx in range(3)], axis=0)
        taps = jnp.concatenate([taps] * (128 // CH2), axis=1)
        for out_x in range(HALF2):
            low = 2 * out_x - 1
            skip = max(0, -low)
            lane = CH2 * out_x
            part = lane % 128
            b_ref[
                ROW1 * dy + CH1 * (low + skip) : ROW1 * dy + CH1 * (low + 3), lane : lane + CH2
            ] = taps[CH1 * skip :, part : part + CH2]


def banded_weights(conv1_w, conv1_b, conv2_w, conv2_b):
    return pl.pallas_call(
        weights_kernel,
        out_shape=(
            jax.ShapeDtypeStruct((4 * MAP, ROW1), BF),
            jax.ShapeDtypeStruct((3 * ROW1, ROW2), BF),
            jax.ShapeDtypeStruct((1, ROW1), F32),
            jax.ShapeDtypeStruct((1, ROW2), F32),
        ),
        in_specs=[pl.BlockSpec(memory_space=pltpu.HBM)] * 4,
        scratch_shapes=[
            pltpu.VMEM((3, 3, CH1), BF),
            pltpu.VMEM((9, CH1, CH2), BF),
            pltpu.VMEM((1, CH1), F32),
            pltpu.VMEM((1, CH2), F32),
            pltpu.SemaphoreType.DMA((4,)),
        ],
        cost_estimate=pl.CostEstimate(flops=50_000_000, bytes_accessed=2_000_000, transcendentals=0),
        compiler_params=pltpu.CompilerParams(vmem_limit_bytes=8 << 20),
        interpret=INTERPRET,
    )(
        *map(
            in_hbm,
            (
                jnp.transpose(conv1_w, (0, 2, 1, 3)).reshape(3, 3, CH1),
                conv2_w.reshape(9, CH1, CH2),
                conv1_b[None, :],
                conv2_b[None, :],
            ),
        )
    )


def join_kernel(*refs):
    low = 0
    for ref in refs[:-1]:
        high = low + ref.shape[0]
        refs[-1][low:high] = ref[...]
        low = high


def joined(*blocks):
    count = sum(block.shape[0] for block in blocks)
    vmem = pl.BlockSpec(memory_space=pltpu.VMEM)
    shape = (count,) + blocks[0].shape[1:]
    return pl.pallas_call(
        join_kernel,
        out_shape=jax.ShapeDtypeStruct(shape, BF),
        in_specs=[vmem] * len(blocks),
        out_specs=vmem,
        cost_estimate=pl.CostEstimate(flops=0, bytes_accessed=300_000, transcendentals=0),
        compiler_params=pltpu.CompilerParams(vmem_limit_bytes=4 << 20),
        interpret=INTERPRET,
    )(*blocks)


def cost_kernel(z_count, where_ref, q_ref, own_ref, *refs):
    *mine_refs, cross_ref, last_ref = refs[:-9]
    a_ref, b_ref, bias1_ref, bias2_ref, kept_ref, sent_ref, corr, hid, acc = refs[-9:]
    z = where_ref[1]
    toward = 2 * where_ref[3] - 1
    n = q_ref.shape[0]
    corr[0, :, 0:128] = jnp.zeros((n, 128), BF)
    hid[0, :, 0:ROW1] = jnp.zeros((n, ROW1), BF)
    q = q_ref[...]

    def put(ref, k, shift):
        low, high = ref[k], ref[k + 1]
        chip = lax.rem(z + z_count + shift, z_count)
        cells = jnp.concatenate([low[0:MAP], high[0:MAP], low[MAP:], high[MAP:]], axis=0)
        got = lax.dot_general(q, cells, (((1,), (1,)), ((), ())), preferred_element_type=F32)
        got = (got * 0.0625).astype(BF)
        for side in range(2):
            part = got[:, 128 * side : 128 * (side + 1)]
            y = side * z_count + chip
            corr[y, :, 128:256] = part
            corr[y + 1, :, 0:128] = part

    put(own_ref, 0, 0)
    distance = 0
    for ref in mine_refs:
        for k in range(0, ref.shape[0], 2):
            distance += 1
            put(ref, k, toward * distance)
            put(cross_ref, 2 * distance - 2, -toward * distance)
    half = last_ref.shape[0] // 2
    for k in range(0, half, 2):
        distance += 1
        put(last_ref, k, -distance)
        if 2 * distance < z_count:
            put(last_ref, half + k, distance)

    bias1 = bias1_ref[...]
    rows1 = 8
    for t in range(HALF1 // rows1):
        lhs = corr[rows1 * t : rows1 * (t + 1)].reshape(rows1 * n, 256)
        got = jnp.dot(lhs, a_ref[...], preferred_element_type=F32)
        got = jnp.maximum(got + bias1, 0.0).astype(BF).reshape(rows1, n, ROW1)
        for s in range(rows1):
            y = rows1 * t + s
            j = y // 2
            if y % 2 == 0:
                hid[j, :, ROW1 : 2 * ROW1] = got[s]
            else:
                hid[j, :, 2 * ROW1 : 3 * ROW1] = got[s]
                hid[j + 1, :, 0:ROW1] = got[s]

    bias2 = bias2_ref[...]
    half = ROW2 // 2
    rows2 = 4
    acc[...] = jnp.zeros(acc.shape, F32)
    for t in range(HALF2 // rows2):
        tile = slice(rows2 * t, rows2 * (t + 1))
        left = jnp.zeros((rows2 * n, half), F32)
        for dy in range(3):
            k = slice(ROW1 * dy, ROW1 * dy + ROW1 // 2)
            left += jnp.dot(
                hid[tile, :, k].reshape(rows2 * n, ROW1 // 2),
                b_ref[k, 0:half],
                preferred_element_type=F32,
            )
        right = jnp.dot(
            hid[tile].reshape(rows2 * n, 3 * ROW1), b_ref[:, half:], preferred_element_type=F32
        )
        left = jnp.maximum(left + bias2[:, :half], 0.0).reshape(rows2, n, half)
        right = jnp.maximum(right + bias2[:, half:], 0.0).reshape(rows2, n, half)
        acc[:, :half] += jnp.sum(left, axis=0)
        acc[:, half:] += jnp.sum(right, axis=0)
    total = acc[:, 0:128]
    for k in range(1, ROW2 // 128):
        total = total + acc[:, 128 * k : 128 * (k + 1)]
    total = (total[:, 0:32] + total[:, 32:64]) + (total[:, 64:96] + total[:, 96:128])
    pooled = (total * (1.0 / (HALF2 * HALF2))).astype(BF)
    kept_ref[...] = pooled[: n // 2]
    sent_ref[...] = pooled[n // 2 :]


def pooled_costs(where, queries, own, far, a, b, bias1, bias2):
    n = queries.shape[0]
    z_count = MAP // 4
    vmem = pl.BlockSpec(memory_space=pltpu.VMEM)

    return pl.pallas_call(
        functools.partial(cost_kernel, z_count),
        out_shape=(jax.ShapeDtypeStruct((n // 2, CH2), BF),) * 2,
        in_specs=[pl.BlockSpec(memory_space=pltpu.SMEM)] + [vmem] * (6 + len(far)),
        out_specs=(vmem, vmem),
        scratch_shapes=[
            pltpu.VMEM((HALF1 + 1, n, 256), BF),
            pltpu.VMEM((HALF2 + 1, n, 3 * ROW1), BF),
            pltpu.VMEM((n, ROW2), F32),
        ],
        cost_estimate=pl.CostEstimate(
            flops=5_000_000_000, bytes_accessed=4_000_000, transcendentals=0
        ),
        compiler_params=pltpu.CompilerParams(vmem_limit_bytes=28 << 20),
        interpret=INTERPRET,
    )(where, queries, own, *far, a, b, bias1, bias2)


def tail_kernel(
    frame_count,
    where_ref,
    kept_ref,
    partner_ref,
    straight_ref,
    crossed_ref,
    proj_w_ref,
    proj_b_ref,
    time_w_ref,
    time_b_ref,
    out_ref,
):
    x, frame_block = where_ref[0], where_ref[2]
    first = x == 0
    kept, partner = kept_ref[...], partner_ref[...]
    straight, crossed = straight_ref[...], crossed_ref[...]
    around = [
        jnp.where(first, crossed, straight),
        jnp.where(first, kept, partner),
        jnp.where(first, partner, kept),
        jnp.where(first, straight, crossed),
    ]
    valid = [frame_block > 0, None, None, frame_block < frame_count - 1]
    wide = []
    for pooled, there in zip(around, valid):
        got = jnp.dot(pooled, proj_w_ref[...], preferred_element_type=F32) + proj_b_ref[...]
        got = got.astype(BF).astype(F32)
        if there is not None:
            got = jnp.where(there, got, 0.0)
        wide.append(got)
    for t in range(2):
        mixed = (
            time_w_ref[0:1, :] * wide[t]
            + time_w_ref[1:2, :] * wide[t + 1]
            + time_w_ref[2:3, :] * wide[t + 2]
            + time_b_ref[...]
        )
        out_ref[:, t, :] = mixed.astype(BF)


def tail(frame_count, where, pooled, proj_w, proj_b, time_w, time_b):
    count, width = pooled[0].shape[0], proj_w.shape[1]
    vmem = pl.BlockSpec(memory_space=pltpu.VMEM)
    return pl.pallas_call(
        functools.partial(tail_kernel, frame_count),
        out_shape=jax.ShapeDtypeStruct((count, 2, width), BF),
        in_specs=[pl.BlockSpec(memory_space=pltpu.SMEM)] + [vmem] * 8,
        out_specs=vmem,
        compiler_params=pltpu.CompilerParams(vmem_limit_bytes=8 << 20),
        interpret=INTERPRET,
    )(where, *pooled, proj_w, proj_b[None, :], time_w, time_b[None, :])


def one_device(
    sizes,
    frame_maps,
    query_table,
    start_frame,
    row_ids,
    conv1_w,
    conv1_b,
    conv2_w,
    conv2_b,
    proj_w,
    proj_b,
    time_w,
    time_b,
):
    xh_count, y_count, _, z_count, _ = sizes
    frame_count = xh_count * y_count
    x = lax.axis_index("xl")
    z = lax.axis_index("z")
    frame_block = lax.axis_index("xh") * y_count + lax.axis_index("y")
    where = jnp.stack([x, z, frame_block, lax.axis_index("c")]).astype(jnp.int32)
    swap = [(0, 1), (1, 0)]

    def flip(axis, count, step):
        return lambda v: lax.ppermute(v, axis, [(i, i ^ step) for i in range(count)])

    def along(block, distance):
        pairs = []
        for i in range(z_count):
            pairs.append((2 * i, 2 * ((i + distance) % z_count)))
            pairs.append((2 * i + 1, 2 * ((i - distance) % z_count) + 1))
        return lax.ppermute(block, ("z", "c"), pairs)

    def both(block):
        return lax.all_gather(block, "c", axis=0, tiled=True)

    def behind(value, earlier):
        return lax.optimization_barrier((value, earlier))[0]

    message = opening(where, frame_maps, query_table, start_frame, row_ids)
    gathered = lax.all_gather(message, ("xl", "c"), axis=0)
    own, queries = picked(where, gathered, frame_maps.shape[1])
    weights = banded_weights(conv1_w, conv1_b, conv2_w, conv2_b)
    near = []
    for distance in (1, 2, 3):
        near.append(along(own, distance))
    queries = queries + flip("y", y_count, 1)(queries)
    near[1], near[2] = lax.optimization_barrier((near[1], near[2]))

    pair = joined(near[1], near[2])
    far5 = along(pair, 3)
    far4 = along(near[0], 3)
    if y_count > 2:
        queries = queries + flip("y", y_count, 2)(behind(queries, pair))
    far5, weights = lax.optimization_barrier((far5, weights))

    far7 = along(far5, 2)
    if xh_count > 1:
        queries = queries + flip("xh", xh_count, 1)(behind(queries, far5))
    mine = [near[0], pair, far4, far5]
    cross = lax.ppermute(joined(*mine), "c", swap)
    far7, cross, queries = lax.optimization_barrier((far7, cross, queries))
    spread = mine + [cross, both(far7)]

    kept, sent = pooled_costs(where, queries, own, spread, *weights)

    def frame_pairs(cross):
        pairs = []
        for f in range(frame_count):
            if f > 0:
                pairs.append((2 * (f - 1) + 1, 2 * f + (0 if cross else 1)))
            if f < frame_count - 1:
                pairs.append((2 * (f + 1), 2 * f + (1 if cross else 0)))
        return pairs

    partner = lax.ppermute(sent, "xl", swap)
    straight = lax.ppermute(kept, ("xh", "y", "xl"), frame_pairs(False))
    crossed = lax.ppermute(sent, ("xh", "y", "xl"), frame_pairs(True))
    pooled = (kept, partner, straight, crossed)
    return tail(frame_count, where, pooled, proj_w, proj_b, time_w, time_b)


def solution(mesh):

    frames, _ = mesh.devices.shape
    sizes = (frames // 4 or 1, min(frames, 4), 2, MAP // 4, 2)
    fine = Mesh(mesh.devices.reshape(sizes), ("xh", "y", "xl", "z", "c"))
    fr = ("xh", "y")
    qs = ("xl", "z", "c")
    placed = (P(fr, qs, None), P(fr, qs, None), P(qs), P(qs)) + (P(),) * 8
    return jax.shard_map(
        functools.partial(one_device, sizes),
        mesh=fine,
        in_specs=placed,
        out_specs=P(qs, fr, None),
        check_vma=False,
    )
```

```python
import functools

import jax
import jax.numpy as jnp
from jax import lax
from jax.experimental import pallas as pl
from jax.experimental.pallas import tpu as pltpu
from jax.sharding import Mesh, PartitionSpec as P


MAP = 64
CH1 = 16
CH2 = 32
HALF1 = MAP // 2
HALF2 = MAP // 4
ROW1 = HALF1 * CH1
ROW2 = HALF2 * CH2
BF = jnp.bfloat16
F32 = jnp.float32
INTERPRET = False


def iota(shape, dim):
    return lax.broadcasted_iota(jnp.int32, shape, dim)


def in_hbm(array):
    if INTERPRET:
        return array
    return pltpu.with_memory_space_constraint(array, pltpu.HBM)


def opening_kernel(
    where_ref, maps_hbm, table_hbm, start_hbm, rows_hbm, out_ref, table, start, rows, sems
):
    frames_here, cells = maps_hbm.shape[0], maps_hbm.shape[1]
    copies = [
        pltpu.make_async_copy(start_hbm, start, sems.at[0]),
        pltpu.make_async_copy(rows_hbm, rows, sems.at[1]),
        pltpu.make_async_copy(table_hbm, table, sems.at[2]),
    ]
    for f in range(frames_here):
        part = out_ref.at[pl.ds(cells * f, cells)]
        copies.append(pltpu.make_async_copy(maps_hbm.at[f], part, sems.at[3 + f]))
    for copy in copies:
        copy.start()
    for copy in copies[:3]:
        copy.wait()
    low = where_ref[2] * frames_here
    owned = (start[...] >= low) & (start[...] < low + frames_here)
    row = jnp.where(owned, rows[...], -1)
    chosen = (iota((table.shape[1], row.shape[1]), 0) == row).astype(BF)
    got = lax.dot_general(chosen, table[0], (((0,), (0,)), ((), ())), preferred_element_type=F32)
    out_ref[frames_here * cells :, :] = got.astype(BF)
    for copy in copies[3:]:
        copy.wait()


def opening(where, frame_maps, query_table, start_frame, row_ids):
    frames_here, cells, channels = frame_maps.shape
    count = start_frame.shape[0]
    hbm = pl.BlockSpec(memory_space=pltpu.HBM)
    arrays = (frame_maps, query_table, start_frame[None, :], row_ids[None, :])
    return pl.pallas_call(
        opening_kernel,
        out_shape=jax.ShapeDtypeStruct((frames_here * cells + count, channels), BF),
        in_specs=[pl.BlockSpec(memory_space=pltpu.SMEM)] + [hbm] * 4,
        out_specs=pl.BlockSpec(memory_space=pltpu.VMEM),
        scratch_shapes=[
            pltpu.VMEM(query_table.shape, BF),
            pltpu.VMEM((1, count), jnp.int32),
            pltpu.VMEM((1, count), jnp.int32),
            pltpu.SemaphoreType.DMA((5,)),
        ],
        cost_estimate=pl.CostEstimate(flops=2_000_000, bytes_accessed=200_000, transcendentals=0),
        compiler_params=pltpu.CompilerParams(vmem_limit_bytes=4 << 20),
        interpret=INTERPRET,
    )(where, *map(in_hbm, arrays))


def pick_kernel(where_ref, all_ref, block_ref, queries_ref):
    x, core = where_ref[0], where_ref[3]
    cells = block_ref.shape[1] // 2
    frame = pl.ds(pl.multiple_of(cells * x, cells), cells)
    for c in range(2):
        for side in range(2):
            block_ref[c, cells * side : cells * (side + 1), :] = all_ref[2 * side + c, frame, :]
    count = queries_ref.shape[0] // 2
    first = 2 * cells
    queries_ref[0:count, :] = all_ref[2 * x + core, first : first + count, :]
    queries_ref[count:, :] = all_ref[2 * (1 - x) + core, first : first + count, :]


def picked(where, gathered, cells):
    channels = gathered.shape[2]
    count = gathered.shape[1] - 2 * cells
    vmem = pl.BlockSpec(memory_space=pltpu.VMEM)
    return pl.pallas_call(
        pick_kernel,
        out_shape=(
            jax.ShapeDtypeStruct((2, 2 * cells, channels), BF),
            jax.ShapeDtypeStruct((2 * count, channels), BF),
        ),
        in_specs=[pl.BlockSpec(memory_space=pltpu.SMEM), vmem],
        out_specs=(vmem, vmem),
        cost_estimate=pl.CostEstimate(flops=0, bytes_accessed=300_000, transcendentals=0),
        compiler_params=pltpu.CompilerParams(vmem_limit_bytes=4 << 20),
        interpret=INTERPRET,
    )(where, gathered)


def weights_kernel(*refs):
    a_ref, b_ref, wide1_ref, wide2_ref, w1_ref, w2_ref, bias1_ref, bias2_ref, sems = refs[4:]
    copies = [
        pltpu.make_async_copy(refs[k], refs[8 + k], sems.at[k]) for k in range(4)
    ]
    for copy in copies:
        copy.start()
    b_ref[...] = jnp.zeros(b_ref.shape, BF)
    for copy in copies:
        copy.wait()
    spread = (iota((CH1, ROW1), 1) % CH1 == iota((CH1, ROW1), 0)).astype(BF)
    wide1_ref[...] = jnp.concatenate([bias1_ref[...]] * HALF1, axis=1)
    wide2_ref[...] = jnp.concatenate([bias2_ref[...]] * HALF2, axis=1)

    in_x = iota((MAP, ROW1), 0)
    out_x = iota((MAP, ROW1), 1) // CH1
    a_ref[0:MAP, :] = jnp.zeros((MAP, ROW1), BF)
    for dy in range(3):
        wide = jnp.dot(w1_ref[dy], spread, preferred_element_type=F32)
        block = jnp.zeros((MAP, ROW1), F32)
        for dx in range(3):
            block = jnp.where(in_x == 2 * out_x + dx - 1, wide[dx : dx + 1, :], block)
        a_ref[MAP * (dy + 1) : MAP * (dy + 2), :] = block.astype(BF)

    for dy in range(3):
        taps = jnp.concatenate([w2_ref[3 * dy + dx] for dx in range(3)], axis=0)
        taps = jnp.concatenate([taps] * (128 // CH2), axis=1)
        for out_x in range(HALF2):
            low = 2 * out_x - 1
            skip = max(0, -low)
            lane = CH2 * out_x
            part = lane % 128
            b_ref[
                ROW1 * dy + CH1 * (low + skip) : ROW1 * dy + CH1 * (low + 3), lane : lane + CH2
            ] = taps[CH1 * skip :, part : part + CH2]


def banded_weights(conv1_w, conv1_b, conv2_w, conv2_b):
    return pl.pallas_call(
        weights_kernel,
        out_shape=(
            jax.ShapeDtypeStruct((4 * MAP, ROW1), BF),
            jax.ShapeDtypeStruct((3 * ROW1, ROW2), BF),
            jax.ShapeDtypeStruct((1, ROW1), F32),
            jax.ShapeDtypeStruct((1, ROW2), F32),
        ),
        in_specs=[pl.BlockSpec(memory_space=pltpu.HBM)] * 4,
        scratch_shapes=[
            pltpu.VMEM((3, 3, CH1), BF),
            pltpu.VMEM((9, CH1, CH2), BF),
            pltpu.VMEM((1, CH1), F32),
            pltpu.VMEM((1, CH2), F32),
            pltpu.SemaphoreType.DMA((4,)),
        ],
        cost_estimate=pl.CostEstimate(flops=50_000_000, bytes_accessed=2_000_000, transcendentals=0),
        compiler_params=pltpu.CompilerParams(vmem_limit_bytes=8 << 20),
        interpret=INTERPRET,
    )(
        *map(
            in_hbm,
            (
                jnp.transpose(conv1_w, (0, 2, 1, 3)).reshape(3, 3, CH1),
                conv2_w.reshape(9, CH1, CH2),
                conv1_b[None, :],
                conv2_b[None, :],
            ),
        )
    )


def join_kernel(*refs):
    low = 0
    for ref in refs[:-1]:
        high = low + ref.shape[0]
        refs[-1][low:high] = ref[...]
        low = high


def joined(*blocks):
    count = sum(block.shape[0] for block in blocks)
    vmem = pl.BlockSpec(memory_space=pltpu.VMEM)
    shape = (count,) + blocks[0].shape[1:]
    return pl.pallas_call(
        join_kernel,
        out_shape=jax.ShapeDtypeStruct(shape, BF),
        in_specs=[vmem] * len(blocks),
        out_specs=vmem,
        cost_estimate=pl.CostEstimate(flops=0, bytes_accessed=300_000, transcendentals=0),
        compiler_params=pltpu.CompilerParams(vmem_limit_bytes=4 << 20),
        interpret=INTERPRET,
    )(*blocks)


def cost_kernel(z_count, where_ref, q_ref, own_ref, *refs):
    *mine_refs, cross_ref, last_ref = refs[:-9]
    a_ref, b_ref, bias1_ref, bias2_ref, kept_ref, sent_ref, corr, hid, acc = refs[-9:]
    z = where_ref[1]
    toward = 2 * where_ref[3] - 1
    n = q_ref.shape[0]
    corr[0, :, 0:128] = jnp.zeros((n, 128), BF)
    hid[0, :, 0:ROW1] = jnp.zeros((n, ROW1), BF)
    q = q_ref[...]

    def put(ref, k, shift):
        low, high = ref[k], ref[k + 1]
        chip = lax.rem(z + z_count + shift, z_count)
        cells = jnp.concatenate([low[0:MAP], high[0:MAP], low[MAP:], high[MAP:]], axis=0)
        got = lax.dot_general(q, cells, (((1,), (1,)), ((), ())), preferred_element_type=F32)
        got = (got * 0.0625).astype(BF)
        for side in range(2):
            part = got[:, 128 * side : 128 * (side + 1)]
            y = side * z_count + chip
            corr[y, :, 128:256] = part
            corr[y + 1, :, 0:128] = part

    put(own_ref, 0, 0)
    distance = 0
    for ref in mine_refs:
        for k in range(0, ref.shape[0], 2):
            distance += 1
            put(ref, k, toward * distance)
            put(cross_ref, 2 * distance - 2, -toward * distance)
    half = last_ref.shape[0] // 2
    for k in range(0, half, 2):
        distance += 1
        put(last_ref, k, -distance)
        if 2 * distance < z_count:
            put(last_ref, half + k, distance)

    bias1 = bias1_ref[...]
    rows1 = 8
    for t in range(HALF1 // rows1):
        lhs = corr[rows1 * t : rows1 * (t + 1)].reshape(rows1 * n, 256)
        got = jnp.dot(lhs, a_ref[...], preferred_element_type=F32)
        got = jnp.maximum(got + bias1, 0.0).astype(BF).reshape(rows1, n, ROW1)
        for s in range(rows1):
            y = rows1 * t + s
            j = y // 2
            if y % 2 == 0:
                hid[j, :, ROW1 : 2 * ROW1] = got[s]
            else:
                hid[j, :, 2 * ROW1 : 3 * ROW1] = got[s]
                hid[j + 1, :, 0:ROW1] = got[s]

    bias2 = bias2_ref[...]
    half = ROW2 // 2
    rows2 = 4
    acc[...] = jnp.zeros(acc.shape, F32)
    for t in range(HALF2 // rows2):
        tile = slice(rows2 * t, rows2 * (t + 1))
        left = jnp.zeros((rows2 * n, half), F32)
        for dy in range(3):
            k = slice(ROW1 * dy, ROW1 * dy + ROW1 // 2)
            left += jnp.dot(
                hid[tile, :, k].reshape(rows2 * n, ROW1 // 2),
                b_ref[k, 0:half],
                preferred_element_type=F32,
            )
        right = jnp.dot(
            hid[tile].reshape(rows2 * n, 3 * ROW1), b_ref[:, half:], preferred_element_type=F32
        )
        left = jnp.maximum(left + bias2[:, :half], 0.0).reshape(rows2, n, half)
        right = jnp.maximum(right + bias2[:, half:], 0.0).reshape(rows2, n, half)
        acc[:, :half] += jnp.sum(left, axis=0)
        acc[:, half:] += jnp.sum(right, axis=0)
    total = acc[:, 0:128]
    for k in range(1, ROW2 // 128):
        total = total + acc[:, 128 * k : 128 * (k + 1)]
    total = (total[:, 0:32] + total[:, 32:64]) + (total[:, 64:96] + total[:, 96:128])
    pooled = (total * (1.0 / (HALF2 * HALF2))).astype(BF)
    kept_ref[...] = pooled[: n // 2]
    sent_ref[...] = pooled[n // 2 :]


def pooled_costs(where, queries, own, far, a, b, bias1, bias2):
    n = queries.shape[0]
    z_count = MAP // 4
    vmem = pl.BlockSpec(memory_space=pltpu.VMEM)

    return pl.pallas_call(
        functools.partial(cost_kernel, z_count),
        out_shape=(jax.ShapeDtypeStruct((n // 2, CH2), BF),) * 2,
        in_specs=[pl.BlockSpec(memory_space=pltpu.SMEM)] + [vmem] * (6 + len(far)),
        out_specs=(vmem, vmem),
        scratch_shapes=[
            pltpu.VMEM((HALF1 + 1, n, 256), BF),
            pltpu.VMEM((HALF2 + 1, n, 3 * ROW1), BF),
            pltpu.VMEM((n, ROW2), F32),
        ],
        cost_estimate=pl.CostEstimate(
            flops=5_000_000_000, bytes_accessed=4_000_000, transcendentals=0
        ),
        compiler_params=pltpu.CompilerParams(vmem_limit_bytes=28 << 20),
        interpret=INTERPRET,
    )(where, queries, own, *far, a, b, bias1, bias2)


def tail_kernel(
    frame_count,
    where_ref,
    kept_ref,
    partner_ref,
    straight_ref,
    crossed_ref,
    proj_w_ref,
    proj_b_ref,
    time_w_ref,
    time_b_ref,
    out_ref,
):
    x, frame_block = where_ref[0], where_ref[2]
    first = x == 0
    kept, partner = kept_ref[...], partner_ref[...]
    straight, crossed = straight_ref[...], crossed_ref[...]
    around = [
        jnp.where(first, crossed, straight),
        jnp.where(first, kept, partner),
        jnp.where(first, partner, kept),
        jnp.where(first, straight, crossed),
    ]
    valid = [frame_block > 0, None, None, frame_block < frame_count - 1]
    wide = []
    for pooled, there in zip(around, valid):
        got = jnp.dot(pooled, proj_w_ref[...], preferred_element_type=F32) + proj_b_ref[...]
        got = got.astype(BF).astype(F32)
        if there is not None:
            got = jnp.where(there, got, 0.0)
        wide.append(got)
    for t in range(2):
        mixed = (
            time_w_ref[0:1, :] * wide[t]
            + time_w_ref[1:2, :] * wide[t + 1]
            + time_w_ref[2:3, :] * wide[t + 2]
            + time_b_ref[...]
        )
        out_ref[:, t, :] = mixed.astype(BF)


def tail(frame_count, where, pooled, proj_w, proj_b, time_w, time_b):
    count, width = pooled[0].shape[0], proj_w.shape[1]
    vmem = pl.BlockSpec(memory_space=pltpu.VMEM)
    return pl.pallas_call(
        functools.partial(tail_kernel, frame_count),
        out_shape=jax.ShapeDtypeStruct((count, 2, width), BF),
        in_specs=[pl.BlockSpec(memory_space=pltpu.SMEM)] + [vmem] * 8,
        out_specs=vmem,
        compiler_params=pltpu.CompilerParams(vmem_limit_bytes=8 << 20),
        interpret=INTERPRET,
    )(where, *pooled, proj_w, proj_b[None, :], time_w, time_b[None, :])


def one_device(
    sizes,
    frame_maps,
    query_table,
    start_frame,
    row_ids,
    conv1_w,
    conv1_b,
    conv2_w,
    conv2_b,
    proj_w,
    proj_b,
    time_w,
    time_b,
):
    xh_count, y_count, _, z_count, _ = sizes
    frame_count = xh_count * y_count
    x = lax.axis_index("xl")
    z = lax.axis_index("z")
    frame_block = lax.axis_index("xh") * y_count + lax.axis_index("y")
    where = jnp.stack([x, z, frame_block, lax.axis_index("c")]).astype(jnp.int32)
    swap = [(0, 1), (1, 0)]

    def flip(axis, count, step):
        return lambda v: lax.ppermute(v, axis, [(i, i ^ step) for i in range(count)])

    def along(block, distance):
        pairs = []
        for i in range(z_count):
            pairs.append((2 * i, 2 * ((i + distance) % z_count)))
            pairs.append((2 * i + 1, 2 * ((i - distance) % z_count) + 1))
        return lax.ppermute(block, ("z", "c"), pairs)

    def both(block):
        return lax.all_gather(block, "c", axis=0, tiled=True)

    def behind(value, earlier):
        return lax.optimization_barrier((value, earlier))[0]

    message = opening(where, frame_maps, query_table, start_frame, row_ids)
    gathered = lax.all_gather(message, ("xl", "c"), axis=0)
    own, queries = picked(where, gathered, frame_maps.shape[1])
    weights = banded_weights(conv1_w, conv1_b, conv2_w, conv2_b)
    near = []
    for distance in (1, 2):
        near.append(along(own, distance))
    queries = queries + flip("y", y_count, 1)(queries)
    near = lax.optimization_barrier(near)

    ring = [joined(*near)]
    ring.append(along(ring[0], 2))
    if y_count > 2:
        queries = queries + flip("y", y_count, 2)(behind(queries, ring[0]))
    ring[1], weights = lax.optimization_barrier((ring[1], weights))

    ring.append(along(ring[1], 2))
    if xh_count > 1:
        queries = queries + flip("xh", xh_count, 1)(behind(queries, ring[1]))
    ring[2] = lax.optimization_barrier(ring[2])

    last = along(ring[2], 2)
    cross = lax.ppermute(joined(*ring), "c", swap)
    last, cross, queries = lax.optimization_barrier((last, cross, queries))
    spread = ring + [cross, both(last)]

    kept, sent = pooled_costs(where, queries, own, spread, *weights)

    def frame_pairs(cross):
        pairs = []
        for f in range(frame_count):
            if f > 0:
                pairs.append((2 * (f - 1) + 1, 2 * f + (0 if cross else 1)))
            if f < frame_count - 1:
                pairs.append((2 * (f + 1), 2 * f + (1 if cross else 0)))
        return pairs

    partner = lax.ppermute(sent, "xl", swap)
    straight = lax.ppermute(kept, ("xh", "y", "xl"), frame_pairs(False))
    crossed = lax.ppermute(sent, ("xh", "y", "xl"), frame_pairs(True))
    pooled = (kept, partner, straight, crossed)
    return tail(frame_count, where, pooled, proj_w, proj_b, time_w, time_b)


def solution(mesh):

    frames, _ = mesh.devices.shape
    sizes = (frames // 4 or 1, min(frames, 4), 2, MAP // 4, 2)
    fine = Mesh(mesh.devices.reshape(sizes), ("xh", "y", "xl", "z", "c"))
    fr = ("xh", "y")
    qs = ("xl", "z", "c")
    placed = (P(fr, qs, None), P(fr, qs, None), P(qs), P(qs)) + (P(),) * 8
    return jax.shard_map(
        functools.partial(one_device, sizes),
        mesh=fine,
        in_specs=placed,
        out_specs=P(qs, fr, None),
        check_vma=False,
    )
```

```python
import functools

import jax
import jax.numpy as jnp
from jax import lax
from jax.experimental import pallas as pl
from jax.experimental.pallas import tpu as pltpu
from jax.sharding import Mesh, PartitionSpec as P


MAP = 64
CH1 = 16
CH2 = 32
HALF1 = MAP // 2
HALF2 = MAP // 4
ROW1 = HALF1 * CH1
ROW2 = HALF2 * CH2
BF = jnp.bfloat16
F32 = jnp.float32
INTERPRET = False


def iota(shape, dim):
    return lax.broadcasted_iota(jnp.int32, shape, dim)


def in_hbm(array):
    if INTERPRET:
        return array
    return pltpu.with_memory_space_constraint(array, pltpu.HBM)


def opening_kernel(
    where_ref, maps_hbm, table_hbm, start_hbm, rows_hbm, out_ref, table, start, rows, sems
):
    frames_here, cells = maps_hbm.shape[0], maps_hbm.shape[1]
    copies = [
        pltpu.make_async_copy(start_hbm, start, sems.at[0]),
        pltpu.make_async_copy(rows_hbm, rows, sems.at[1]),
        pltpu.make_async_copy(table_hbm, table, sems.at[2]),
    ]
    for f in range(frames_here):
        part = out_ref.at[pl.ds(cells * f, cells)]
        copies.append(pltpu.make_async_copy(maps_hbm.at[f], part, sems.at[3 + f]))
    for copy in copies:
        copy.start()
    for copy in copies[:3]:
        copy.wait()
    low = where_ref[2] * frames_here
    owned = (start[...] >= low) & (start[...] < low + frames_here)
    row = jnp.where(owned, rows[...], -1)
    chosen = (iota((table.shape[1], row.shape[1]), 0) == row).astype(BF)
    got = lax.dot_general(chosen, table[0], (((0,), (0,)), ((), ())), preferred_element_type=F32)
    out_ref[frames_here * cells :, :] = got.astype(BF)
    for copy in copies[3:]:
        copy.wait()


def opening(where, frame_maps, query_table, start_frame, row_ids):
    frames_here, cells, channels = frame_maps.shape
    count = start_frame.shape[0]
    hbm = pl.BlockSpec(memory_space=pltpu.HBM)
    arrays = (frame_maps, query_table, start_frame[None, :], row_ids[None, :])
    return pl.pallas_call(
        opening_kernel,
        out_shape=jax.ShapeDtypeStruct((frames_here * cells + count, channels), BF),
        in_specs=[pl.BlockSpec(memory_space=pltpu.SMEM)] + [hbm] * 4,
        out_specs=pl.BlockSpec(memory_space=pltpu.VMEM),
        scratch_shapes=[
            pltpu.VMEM(query_table.shape, BF),
            pltpu.VMEM((1, count), jnp.int32),
            pltpu.VMEM((1, count), jnp.int32),
            pltpu.SemaphoreType.DMA((5,)),
        ],
        cost_estimate=pl.CostEstimate(flops=2_000_000, bytes_accessed=200_000, transcendentals=0),
        compiler_params=pltpu.CompilerParams(vmem_limit_bytes=4 << 20),
        interpret=INTERPRET,
    )(where, *map(in_hbm, arrays))


def pick_kernel(where_ref, all_ref, block_ref, queries_ref):
    x, core = where_ref[0], where_ref[3]
    cells = block_ref.shape[1] // 2
    frame = pl.ds(pl.multiple_of(cells * x, cells), cells)
    for c in range(2):
        for side in range(2):
            block_ref[c, cells * side : cells * (side + 1), :] = all_ref[2 * side + c, frame, :]
    count = queries_ref.shape[0] // 2
    first = 2 * cells
    queries_ref[0:count, :] = all_ref[2 * x + core, first : first + count, :]
    queries_ref[count:, :] = all_ref[2 * (1 - x) + core, first : first + count, :]


def picked(where, gathered, cells):
    channels = gathered.shape[2]
    count = gathered.shape[1] - 2 * cells
    vmem = pl.BlockSpec(memory_space=pltpu.VMEM)
    return pl.pallas_call(
        pick_kernel,
        out_shape=(
            jax.ShapeDtypeStruct((2, 2 * cells, channels), BF),
            jax.ShapeDtypeStruct((2 * count, channels), BF),
        ),
        in_specs=[pl.BlockSpec(memory_space=pltpu.SMEM), vmem],
        out_specs=(vmem, vmem),
        cost_estimate=pl.CostEstimate(flops=0, bytes_accessed=300_000, transcendentals=0),
        compiler_params=pltpu.CompilerParams(vmem_limit_bytes=4 << 20),
        interpret=INTERPRET,
    )(where, gathered)


def weights_kernel(*refs):
    a_ref, b_ref, wide1_ref, wide2_ref, w1_ref, w2_ref, bias1_ref, bias2_ref, sems = refs[4:]
    copies = [
        pltpu.make_async_copy(refs[k], refs[8 + k], sems.at[k]) for k in range(4)
    ]
    for copy in copies:
        copy.start()
    b_ref[...] = jnp.zeros(b_ref.shape, BF)
    for copy in copies:
        copy.wait()
    spread = (iota((CH1, ROW1), 1) % CH1 == iota((CH1, ROW1), 0)).astype(BF)
    wide1_ref[...] = jnp.concatenate([bias1_ref[...]] * HALF1, axis=1)
    wide2_ref[...] = jnp.concatenate([bias2_ref[...]] * HALF2, axis=1)

    in_x = iota((MAP, ROW1), 0)
    out_x = iota((MAP, ROW1), 1) // CH1
    a_ref[0:MAP, :] = jnp.zeros((MAP, ROW1), BF)
    for dy in range(3):
        wide = jnp.dot(w1_ref[dy], spread, preferred_element_type=F32)
        block = jnp.zeros((MAP, ROW1), F32)
        for dx in range(3):
            block = jnp.where(in_x == 2 * out_x + dx - 1, wide[dx : dx + 1, :], block)
        a_ref[MAP * (dy + 1) : MAP * (dy + 2), :] = block.astype(BF)

    for dy in range(3):
        taps = jnp.concatenate([w2_ref[3 * dy + dx] for dx in range(3)], axis=0)
        taps = jnp.concatenate([taps] * (128 // CH2), axis=1)
        for out_x in range(HALF2):
            low = 2 * out_x - 1
            skip = max(0, -low)
            lane = CH2 * out_x
            part = lane % 128
            b_ref[
                ROW1 * dy + CH1 * (low + skip) : ROW1 * dy + CH1 * (low + 3), lane : lane + CH2
            ] = taps[CH1 * skip :, part : part + CH2]


def banded_weights(conv1_w, conv1_b, conv2_w, conv2_b):
    return pl.pallas_call(
        weights_kernel,
        out_shape=(
            jax.ShapeDtypeStruct((4 * MAP, ROW1), BF),
            jax.ShapeDtypeStruct((3 * ROW1, ROW2), BF),
            jax.ShapeDtypeStruct((1, ROW1), F32),
            jax.ShapeDtypeStruct((1, ROW2), F32),
        ),
        in_specs=[pl.BlockSpec(memory_space=pltpu.HBM)] * 4,
        scratch_shapes=[
            pltpu.VMEM((3, 3, CH1), BF),
            pltpu.VMEM((9, CH1, CH2), BF),
            pltpu.VMEM((1, CH1), F32),
            pltpu.VMEM((1, CH2), F32),
            pltpu.SemaphoreType.DMA((4,)),
        ],
        cost_estimate=pl.CostEstimate(flops=50_000_000, bytes_accessed=2_000_000, transcendentals=0),
        compiler_params=pltpu.CompilerParams(vmem_limit_bytes=8 << 20),
        interpret=INTERPRET,
    )(
        *map(
            in_hbm,
            (
                jnp.transpose(conv1_w, (0, 2, 1, 3)).reshape(3, 3, CH1),
                conv2_w.reshape(9, CH1, CH2),
                conv1_b[None, :],
                conv2_b[None, :],
            ),
        )
    )


def join_kernel(*refs):
    low = 0
    for ref in refs[:-1]:
        high = low + ref.shape[0]
        refs[-1][low:high] = ref[...]
        low = high


def joined(*blocks):
    count = sum(block.shape[0] for block in blocks)
    vmem = pl.BlockSpec(memory_space=pltpu.VMEM)
    shape = (count,) + blocks[0].shape[1:]
    return pl.pallas_call(
        join_kernel,
        out_shape=jax.ShapeDtypeStruct(shape, BF),
        in_specs=[vmem] * len(blocks),
        out_specs=vmem,
        cost_estimate=pl.CostEstimate(flops=0, bytes_accessed=300_000, transcendentals=0),
        compiler_params=pltpu.CompilerParams(vmem_limit_bytes=4 << 20),
        interpret=INTERPRET,
    )(*blocks)


def cost_kernel(z_count, where_ref, q_ref, own_ref, *refs):
    *mine_refs, cross_ref, seven_ref, eight_ref = refs[:-9]
    a_ref, b_ref, bias1_ref, bias2_ref, kept_ref, sent_ref, corr, hid, acc = refs[-9:]
    z = where_ref[1]
    toward = 2 * where_ref[3] - 1
    n = q_ref.shape[0]
    corr[0, :, 0:128] = jnp.zeros((n, 128), BF)
    hid[0, :, 0:ROW1] = jnp.zeros((n, ROW1), BF)
    q = q_ref[...]

    def put(ref, k, shift):
        low, high = ref[k], ref[k + 1]
        chip = lax.rem(z + z_count + shift, z_count)
        cells = jnp.concatenate([low[0:MAP], high[0:MAP], low[MAP:], high[MAP:]], axis=0)
        got = lax.dot_general(q, cells, (((1,), (1,)), ((), ())), preferred_element_type=F32)
        got = (got * 0.0625).astype(BF)
        for side in range(2):
            part = got[:, 128 * side : 128 * (side + 1)]
            y = side * z_count + chip
            corr[y, :, 128:256] = part
            corr[y + 1, :, 0:128] = part

    put(own_ref, 0, 0)
    distance = 0
    for ref in mine_refs:
        for k in range(0, ref.shape[0], 2):
            distance += 1
            put(ref, k, toward * distance)
            put(cross_ref, 2 * distance - 2, -toward * distance)
    put(seven_ref, 0, -distance - 1)
    put(seven_ref, 2, distance + 1)
    put(eight_ref, 0, distance + 2)

    bias1 = bias1_ref[...]
    rows1 = 8
    for t in range(HALF1 // rows1):
        lhs = corr[rows1 * t : rows1 * (t + 1)].reshape(rows1 * n, 256)
        got = jnp.dot(lhs, a_ref[...], preferred_element_type=F32)
        got = jnp.maximum(got + bias1, 0.0).astype(BF).reshape(rows1, n, ROW1)
        for s in range(rows1):
            y = rows1 * t + s
            j = y // 2
            if y % 2 == 0:
                hid[j, :, ROW1 : 2 * ROW1] = got[s]
            else:
                hid[j, :, 2 * ROW1 : 3 * ROW1] = got[s]
                hid[j + 1, :, 0:ROW1] = got[s]

    bias2 = bias2_ref[...]
    half = ROW2 // 2
    rows2 = 4
    acc[...] = jnp.zeros(acc.shape, F32)
    for t in range(HALF2 // rows2):
        tile = slice(rows2 * t, rows2 * (t + 1))
        left = jnp.zeros((rows2 * n, half), F32)
        for dy in range(3):
            k = slice(ROW1 * dy, ROW1 * dy + ROW1 // 2)
            left += jnp.dot(
                hid[tile, :, k].reshape(rows2 * n, ROW1 // 2),
                b_ref[k, 0:half],
                preferred_element_type=F32,
            )
        right = jnp.dot(
            hid[tile].reshape(rows2 * n, 3 * ROW1), b_ref[:, half:], preferred_element_type=F32
        )
        left = jnp.maximum(left + bias2[:, :half], 0.0).reshape(rows2, n, half)
        right = jnp.maximum(right + bias2[:, half:], 0.0).reshape(rows2, n, half)
        acc[:, :half] += jnp.sum(left, axis=0)
        acc[:, half:] += jnp.sum(right, axis=0)
    total = acc[:, 0:128]
    for k in range(1, ROW2 // 128):
        total = total + acc[:, 128 * k : 128 * (k + 1)]
    total = (total[:, 0:32] + total[:, 32:64]) + (total[:, 64:96] + total[:, 96:128])
    pooled = (total * (1.0 / (HALF2 * HALF2))).astype(BF)
    kept_ref[...] = pooled[: n // 2]
    sent_ref[...] = pooled[n // 2 :]


def pooled_costs(where, queries, own, far, a, b, bias1, bias2):
    n = queries.shape[0]
    z_count = MAP // 4
    vmem = pl.BlockSpec(memory_space=pltpu.VMEM)

    return pl.pallas_call(
        functools.partial(cost_kernel, z_count),
        out_shape=(jax.ShapeDtypeStruct((n // 2, CH2), BF),) * 2,
        in_specs=[pl.BlockSpec(memory_space=pltpu.SMEM)] + [vmem] * (6 + len(far)),
        out_specs=(vmem, vmem),
        scratch_shapes=[
            pltpu.VMEM((HALF1 + 1, n, 256), BF),
            pltpu.VMEM((HALF2 + 1, n, 3 * ROW1), BF),
            pltpu.VMEM((n, ROW2), F32),
        ],
        cost_estimate=pl.CostEstimate(
            flops=5_000_000_000, bytes_accessed=4_000_000, transcendentals=0
        ),
        compiler_params=pltpu.CompilerParams(vmem_limit_bytes=28 << 20),
        interpret=INTERPRET,
    )(where, queries, own, *far, a, b, bias1, bias2)


def tail_kernel(
    frame_count,
    where_ref,
    kept_ref,
    partner_ref,
    straight_ref,
    crossed_ref,
    proj_w_ref,
    proj_b_ref,
    time_w_ref,
    time_b_ref,
    out_ref,
):
    x, frame_block = where_ref[0], where_ref[2]
    first = x == 0
    kept, partner = kept_ref[...], partner_ref[...]
    straight, crossed = straight_ref[...], crossed_ref[...]
    around = [
        jnp.where(first, crossed, straight),
        jnp.where(first, kept, partner),
        jnp.where(first, partner, kept),
        jnp.where(first, straight, crossed),
    ]
    valid = [frame_block > 0, None, None, frame_block < frame_count - 1]
    wide = []
    for pooled, there in zip(around, valid):
        got = jnp.dot(pooled, proj_w_ref[...], preferred_element_type=F32) + proj_b_ref[...]
        got = got.astype(BF).astype(F32)
        if there is not None:
            got = jnp.where(there, got, 0.0)
        wide.append(got)
    for t in range(2):
        mixed = (
            time_w_ref[0:1, :] * wide[t]
            + time_w_ref[1:2, :] * wide[t + 1]
            + time_w_ref[2:3, :] * wide[t + 2]
            + time_b_ref[...]
        )
        out_ref[:, t, :] = mixed.astype(BF)


def tail(frame_count, where, pooled, proj_w, proj_b, time_w, time_b):
    count, width = pooled[0].shape[0], proj_w.shape[1]
    vmem = pl.BlockSpec(memory_space=pltpu.VMEM)
    return pl.pallas_call(
        functools.partial(tail_kernel, frame_count),
        out_shape=jax.ShapeDtypeStruct((count, 2, width), BF),
        in_specs=[pl.BlockSpec(memory_space=pltpu.SMEM)] + [vmem] * 8,
        out_specs=vmem,
        compiler_params=pltpu.CompilerParams(vmem_limit_bytes=8 << 20),
        interpret=INTERPRET,
    )(where, *pooled, proj_w, proj_b[None, :], time_w, time_b[None, :])


def one_device(
    sizes,
    frame_maps,
    query_table,
    start_frame,
    row_ids,
    conv1_w,
    conv1_b,
    conv2_w,
    conv2_b,
    proj_w,
    proj_b,
    time_w,
    time_b,
):
    xh_count, y_count, _, z_count, _ = sizes
    frame_count = xh_count * y_count
    x = lax.axis_index("xl")
    z = lax.axis_index("z")
    frame_block = lax.axis_index("xh") * y_count + lax.axis_index("y")
    where = jnp.stack([x, z, frame_block, lax.axis_index("c")]).astype(jnp.int32)
    swap = [(0, 1), (1, 0)]

    def flip(axis, count, step):
        return lambda v: lax.ppermute(v, axis, [(i, i ^ step) for i in range(count)])

    def along(block, distance):
        pairs = []
        for i in range(z_count):
            pairs.append((2 * i, 2 * ((i + distance) % z_count)))
            pairs.append((2 * i + 1, 2 * ((i - distance) % z_count) + 1))
        return lax.ppermute(block, ("z", "c"), pairs)

    def both(block):
        return lax.all_gather(block, "c", axis=0, tiled=True)

    message = opening(where, frame_maps, query_table, start_frame, row_ids)
    gathered = lax.all_gather(message, ("xl", "c"), axis=0)
    own, queries = picked(where, gathered, frame_maps.shape[1])
    weights = banded_weights(conv1_w, conv1_b, conv2_w, conv2_b)
    ring = {}
    for distance in range(1, 9):
        if distance <= 2:
            ring[distance] = along(own, distance)
        else:
            ring[distance] = along(ring[distance - 2], 2)
    queries = queries + flip("y", y_count, 1)(queries)
    if y_count > 2:
        queries = queries + flip("y", y_count, 2)(queries)
    if xh_count > 1:
        queries = queries + flip("xh", xh_count, 1)(queries)
    mine = [ring[distance] for distance in range(1, 7)]
    cross = lax.ppermute(joined(*mine), "c", swap)
    seven = both(ring[7])
    eight, seven, cross, weights = lax.optimization_barrier((ring[8], seven, cross, weights))
    spread = mine + [cross, seven, eight]

    kept, sent = pooled_costs(where, queries, own, spread, *weights)

    def frame_pairs(cross):
        pairs = []
        for f in range(frame_count):
            if f > 0:
                pairs.append((2 * (f - 1) + 1, 2 * f + (0 if cross else 1)))
            if f < frame_count - 1:
                pairs.append((2 * (f + 1), 2 * f + (1 if cross else 0)))
        return pairs

    partner = lax.ppermute(sent, "xl", swap)
    straight = lax.ppermute(kept, ("xh", "y", "xl"), frame_pairs(False))
    crossed = lax.ppermute(sent, ("xh", "y", "xl"), frame_pairs(True))
    pooled = (kept, partner, straight, crossed)
    return tail(frame_count, where, pooled, proj_w, proj_b, time_w, time_b)


def solution(mesh):

    frames, _ = mesh.devices.shape
    sizes = (frames // 4 or 1, min(frames, 4), 2, MAP // 4, 2)
    fine = Mesh(mesh.devices.reshape(sizes), ("xh", "y", "xl", "z", "c"))
    fr = ("xh", "y")
    qs = ("xl", "z", "c")
    placed = (P(fr, qs, None), P(fr, qs, None), P(qs), P(qs)) + (P(),) * 8
    return jax.shard_map(
        functools.partial(one_device, sizes),
        mesh=fine,
        in_specs=placed,
        out_specs=P(qs, fr, None),
        check_vma=False,
    )
```

```python
import functools

import jax
import jax.numpy as jnp
from jax import lax
from jax.experimental import pallas as pl
from jax.experimental.pallas import tpu as pltpu
from jax.sharding import Mesh, PartitionSpec as P


MAP = 64
CH1 = 16
CH2 = 32
HALF1 = MAP // 2
HALF2 = MAP // 4
ROW1 = HALF1 * CH1
ROW2 = HALF2 * CH2
BF = jnp.bfloat16
F32 = jnp.float32
INTERPRET = False


def iota(shape, dim):
    return lax.broadcasted_iota(jnp.int32, shape, dim)


def in_hbm(array):
    if INTERPRET:
        return array
    return pltpu.with_memory_space_constraint(array, pltpu.HBM)


def query_kernel(where_ref, table_hbm, start_hbm, rows_hbm, out_ref, table, start, rows, sems):
    frames_here = 2
    copies = [
        pltpu.make_async_copy(table_hbm, table, sems.at[0]),
        pltpu.make_async_copy(start_hbm, start, sems.at[1]),
        pltpu.make_async_copy(rows_hbm, rows, sems.at[2]),
    ]
    for copy in copies:
        copy.start()
    for copy in copies:
        copy.wait()
    low = where_ref[3] * frames_here
    owned = (start[...] >= low) & (start[...] < low + frames_here)
    row = jnp.where(owned, rows[...], -1)
    chosen = (iota((table.shape[1], row.shape[1]), 0) == row).astype(BF)
    got = lax.dot_general(chosen, table[0], (((0,), (0,)), ((), ())), preferred_element_type=F32)
    out_ref[...] = got.astype(BF)


def own_queries(where, query_table, start_frame, row_ids):
    count = start_frame.shape[0]
    hbm = pl.BlockSpec(memory_space=pltpu.HBM)
    return pl.pallas_call(
        query_kernel,
        out_shape=jax.ShapeDtypeStruct((count, query_table.shape[2]), BF),
        in_specs=[pl.BlockSpec(memory_space=pltpu.SMEM)] + [hbm] * 3,
        out_specs=pl.BlockSpec(memory_space=pltpu.VMEM),
        scratch_shapes=[
            pltpu.VMEM(query_table.shape, BF),
            pltpu.VMEM((1, count), jnp.int32),
            pltpu.VMEM((1, count), jnp.int32),
            pltpu.SemaphoreType.DMA((3,)),
        ],
        cost_estimate=pl.CostEstimate(flops=2_000_000, bytes_accessed=200_000, transcendentals=0),
        compiler_params=pltpu.CompilerParams(vmem_limit_bytes=4 << 20),
        interpret=INTERPRET,
    )(where, *map(in_hbm, (query_table, start_frame[None, :], row_ids[None, :])))


def pick_kernel(where_ref, all_ref, out_ref):
    x = where_ref[0]
    cells = all_ref.shape[2]
    for core in range(2):
        for side in range(2):
            out_ref[core, cells * side : cells * (side + 1), :] = all_ref[2 * side + core, x]


def picked(where, gathered):
    cells, channels = gathered.shape[2:]
    vmem = pl.BlockSpec(memory_space=pltpu.VMEM)
    return pl.pallas_call(
        pick_kernel,
        out_shape=jax.ShapeDtypeStruct((2, 2 * cells, channels), BF),
        in_specs=[pl.BlockSpec(memory_space=pltpu.SMEM), vmem],
        out_specs=vmem,
        cost_estimate=pl.CostEstimate(flops=0, bytes_accessed=300_000, transcendentals=0),
        compiler_params=pltpu.CompilerParams(vmem_limit_bytes=4 << 20),
        interpret=INTERPRET,
    )(where, gathered)


def weights_kernel(*refs):
    a_ref, b_ref, wide1_ref, wide2_ref, w1_ref, w2_ref, bias1_ref, bias2_ref, sems = refs[4:]
    copies = [
        pltpu.make_async_copy(refs[k], refs[8 + k], sems.at[k]) for k in range(4)
    ]
    for copy in copies:
        copy.start()
    b_ref[...] = jnp.zeros(b_ref.shape, BF)
    for copy in copies:
        copy.wait()
    spread = (iota((CH1, ROW1), 1) % CH1 == iota((CH1, ROW1), 0)).astype(BF)
    wide1_ref[...] = jnp.concatenate([bias1_ref[...]] * HALF1, axis=1)
    wide2_ref[...] = jnp.concatenate([bias2_ref[...]] * HALF2, axis=1)

    in_x = iota((MAP, ROW1), 0)
    out_x = iota((MAP, ROW1), 1) // CH1
    a_ref[0:MAP, :] = jnp.zeros((MAP, ROW1), BF)
    for dy in range(3):
        wide = jnp.dot(w1_ref[dy], spread, preferred_element_type=F32)
        block = jnp.zeros((MAP, ROW1), F32)
        for dx in range(3):
            block = jnp.where(in_x == 2 * out_x + dx - 1, wide[dx : dx + 1, :], block)
        a_ref[MAP * (dy + 1) : MAP * (dy + 2), :] = block.astype(BF)

    for dy in range(3):
        taps = jnp.concatenate([w2_ref[3 * dy + dx] for dx in range(3)], axis=0)
        taps = jnp.concatenate([taps] * (128 // CH2), axis=1)
        for out_x in range(HALF2):
            low = 2 * out_x - 1
            skip = max(0, -low)
            lane = CH2 * out_x
            part = lane % 128
            b_ref[
                ROW1 * dy + CH1 * (low + skip) : ROW1 * dy + CH1 * (low + 3), lane : lane + CH2
            ] = taps[CH1 * skip :, part : part + CH2]


def banded_weights(conv1_w, conv1_b, conv2_w, conv2_b):
    return pl.pallas_call(
        weights_kernel,
        out_shape=(
            jax.ShapeDtypeStruct((4 * MAP, ROW1), BF),
            jax.ShapeDtypeStruct((3 * ROW1, ROW2), BF),
            jax.ShapeDtypeStruct((1, ROW1), F32),
            jax.ShapeDtypeStruct((1, ROW2), F32),
        ),
        in_specs=[pl.BlockSpec(memory_space=pltpu.HBM)] * 4,
        scratch_shapes=[
            pltpu.VMEM((3, 3, CH1), BF),
            pltpu.VMEM((9, CH1, CH2), BF),
            pltpu.VMEM((1, CH1), F32),
            pltpu.VMEM((1, CH2), F32),
            pltpu.SemaphoreType.DMA((4,)),
        ],
        cost_estimate=pl.CostEstimate(flops=50_000_000, bytes_accessed=2_000_000, transcendentals=0),
        compiler_params=pltpu.CompilerParams(vmem_limit_bytes=8 << 20),
        interpret=INTERPRET,
    )(
        *map(
            in_hbm,
            (
                jnp.transpose(conv1_w, (0, 2, 1, 3)).reshape(3, 3, CH1),
                conv2_w.reshape(9, CH1, CH2),
                conv1_b[None, :],
                conv2_b[None, :],
            ),
        )
    )


def join_kernel(*refs):
    low = 0
    for ref in refs[:-1]:
        high = low + ref.shape[0]
        refs[-1][low:high] = ref[...]
        low = high


def joined(*blocks):
    count = sum(block.shape[0] for block in blocks)
    vmem = pl.BlockSpec(memory_space=pltpu.VMEM)
    shape = (count,) + blocks[0].shape[1:]
    return pl.pallas_call(
        join_kernel,
        out_shape=jax.ShapeDtypeStruct(shape, BF),
        in_specs=[vmem] * len(blocks),
        out_specs=vmem,
        cost_estimate=pl.CostEstimate(flops=0, bytes_accessed=300_000, transcendentals=0),
        compiler_params=pltpu.CompilerParams(vmem_limit_bytes=4 << 20),
        interpret=INTERPRET,
    )(*blocks)


def trim_kernel(where_ref, blocks_ref, out_ref):
    out_ref[0:2] = blocks_ref[0:2]
    out_ref[2] = blocks_ref[2 + where_ref[2]]


def trimmed(where, blocks):
    vmem = pl.BlockSpec(memory_space=pltpu.VMEM)
    return pl.pallas_call(
        trim_kernel,
        out_shape=jax.ShapeDtypeStruct((3,) + blocks.shape[1:], BF),
        in_specs=[pl.BlockSpec(memory_space=pltpu.SMEM), vmem],
        out_specs=vmem,
        cost_estimate=pl.CostEstimate(flops=0, bytes_accessed=1_000, transcendentals=0),
        compiler_params=pltpu.CompilerParams(vmem_limit_bytes=4 << 20),
        interpret=INTERPRET,
    )(where, blocks)


def cost_kernel(z_count, where_ref, kept_q_ref, sent_q_ref, own_ref, *refs):
    *mine_refs, cross_ref, last_ref = refs[:-9]
    a_ref, b_ref, bias1_ref, bias2_ref, kept_ref, sent_ref, corr, hid, acc = refs[-9:]
    z = where_ref[1]
    toward = 2 * where_ref[2] - 1
    n = 2 * kept_q_ref.shape[0]
    corr[0, :, 0:128] = jnp.zeros((n, 128), BF)
    hid[0, :, 0:ROW1] = jnp.zeros((n, ROW1), BF)
    q = jnp.concatenate([kept_q_ref[...], sent_q_ref[...]], axis=0)

    def put(low, high, shift):
        chip = lax.rem(z + z_count + shift, z_count)
        cells = jnp.concatenate([low[0:MAP], high[0:MAP], low[MAP:], high[MAP:]], axis=0)
        got = lax.dot_general(q, cells, (((1,), (1,)), ((), ())), preferred_element_type=F32)
        got = (got * 0.0625).astype(BF)
        for side in range(2):
            part = got[:, 128 * side : 128 * (side + 1)]
            y = side * z_count + chip
            corr[y, :, 128:256] = part
            corr[y + 1, :, 0:128] = part

    put(own_ref[0], own_ref[1], 0)
    distance = 0
    for ref in mine_refs:
        for k in range(0, ref.shape[0], 2):
            distance += 1
            put(ref[k], ref[k + 1], toward * distance)
            other = 2 * distance - 2
            put(cross_ref[other], cross_ref[other + 1], -toward * distance)
    put(last_ref[0], last_ref[1], -distance - 1)
    put(last_ref[3], last_ref[4], distance + 1)
    put(last_ref[2], last_ref[5], distance + 2)

    bias1 = bias1_ref[...]
    rows1 = 8
    for t in range(HALF1 // rows1):
        lhs = corr[rows1 * t : rows1 * (t + 1)].reshape(rows1 * n, 256)
        got = jnp.dot(lhs, a_ref[...], preferred_element_type=F32)
        got = jnp.maximum(got + bias1, 0.0).astype(BF).reshape(rows1, n, ROW1)
        for s in range(rows1):
            y = rows1 * t + s
            j = y // 2
            if y % 2 == 0:
                hid[j, :, ROW1 : 2 * ROW1] = got[s]
            else:
                hid[j, :, 2 * ROW1 : 3 * ROW1] = got[s]
                hid[j + 1, :, 0:ROW1] = got[s]

    bias2 = bias2_ref[...]
    half = ROW2 // 2
    rows2 = 4
    acc[...] = jnp.zeros(acc.shape, F32)
    for t in range(HALF2 // rows2):
        tile = slice(rows2 * t, rows2 * (t + 1))
        left = jnp.zeros((rows2 * n, half), F32)
        for dy in range(3):
            k = slice(ROW1 * dy, ROW1 * dy + ROW1 // 2)
            left += jnp.dot(
                hid[tile, :, k].reshape(rows2 * n, ROW1 // 2),
                b_ref[k, 0:half],
                preferred_element_type=F32,
            )
        right = jnp.dot(
            hid[tile].reshape(rows2 * n, 3 * ROW1), b_ref[:, half:], preferred_element_type=F32
        )
        left = jnp.maximum(left + bias2[:, :half], 0.0).reshape(rows2, n, half)
        right = jnp.maximum(right + bias2[:, half:], 0.0).reshape(rows2, n, half)
        acc[:, :half] += jnp.sum(left, axis=0)
        acc[:, half:] += jnp.sum(right, axis=0)
    total = acc[:, 0:128]
    for k in range(1, ROW2 // 128):
        total = total + acc[:, 128 * k : 128 * (k + 1)]
    total = (total[:, 0:32] + total[:, 32:64]) + (total[:, 64:96] + total[:, 96:128])
    pooled = (total * (1.0 / (HALF2 * HALF2))).astype(BF)
    kept_ref[...] = pooled[: n // 2]
    sent_ref[...] = pooled[n // 2 :]


def pooled_costs(where, kept_q, sent_q, own, far, a, b, bias1, bias2):
    n = 2 * kept_q.shape[0]
    z_count = MAP // 4
    vmem = pl.BlockSpec(memory_space=pltpu.VMEM)

    return pl.pallas_call(
        functools.partial(cost_kernel, z_count),
        out_shape=(jax.ShapeDtypeStruct((n // 2, CH2), BF),) * 2,
        in_specs=[pl.BlockSpec(memory_space=pltpu.SMEM)] + [vmem] * (7 + len(far)),
        out_specs=(vmem, vmem),
        scratch_shapes=[
            pltpu.VMEM((HALF1 + 1, n, 256), BF),
            pltpu.VMEM((HALF2 + 1, n, 3 * ROW1), BF),
            pltpu.VMEM((n, ROW2), F32),
        ],
        cost_estimate=pl.CostEstimate(
            flops=5_000_000_000, bytes_accessed=4_000_000, transcendentals=0
        ),
        compiler_params=pltpu.CompilerParams(vmem_limit_bytes=28 << 20),
        interpret=INTERPRET,
    )(where, kept_q, sent_q, own, *far, a, b, bias1, bias2)


def tail_kernel(
    frame_count,
    where_ref,
    kept_ref,
    partner_ref,
    straight_ref,
    crossed_ref,
    proj_w_ref,
    proj_b_ref,
    time_w_ref,
    time_b_ref,
    out_ref,
):
    x, frame_block = where_ref[0], where_ref[3]
    first = x == 0
    kept, partner = kept_ref[...], partner_ref[...]
    straight, crossed = straight_ref[...], crossed_ref[...]
    around = [
        jnp.where(first, crossed, straight),
        jnp.where(first, kept, partner),
        jnp.where(first, partner, kept),
        jnp.where(first, straight, crossed),
    ]
    valid = [frame_block > 0, None, None, frame_block < frame_count - 1]
    wide = []
    for pooled, there in zip(around, valid):
        got = jnp.dot(pooled, proj_w_ref[...], preferred_element_type=F32) + proj_b_ref[...]
        got = got.astype(BF).astype(F32)
        if there is not None:
            got = jnp.where(there, got, 0.0)
        wide.append(got)
    for t in range(2):
        mixed = (
            time_w_ref[0:1, :] * wide[t]
            + time_w_ref[1:2, :] * wide[t + 1]
            + time_w_ref[2:3, :] * wide[t + 2]
            + time_b_ref[...]
        )
        out_ref[:, t, :] = mixed.astype(BF)


def tail(frame_count, where, pooled, proj_w, proj_b, time_w, time_b):
    count, width = pooled[0].shape[0], proj_w.shape[1]
    vmem = pl.BlockSpec(memory_space=pltpu.VMEM)
    return pl.pallas_call(
        functools.partial(tail_kernel, frame_count),
        out_shape=jax.ShapeDtypeStruct((count, 2, width), BF),
        in_specs=[pl.BlockSpec(memory_space=pltpu.SMEM)] + [vmem] * 8,
        out_specs=vmem,
        compiler_params=pltpu.CompilerParams(vmem_limit_bytes=8 << 20),
        interpret=INTERPRET,
    )(where, *pooled, proj_w, proj_b[None, :], time_w, time_b[None, :])


def one_device(
    sizes,
    frame_maps,
    query_table,
    start_frame,
    row_ids,
    conv1_w,
    conv1_b,
    conv2_w,
    conv2_b,
    proj_w,
    proj_b,
    time_w,
    time_b,
):
    xh_count, y_count, _, z_count, _ = sizes
    frame_count = xh_count * y_count
    x = lax.axis_index("xl")
    z = lax.axis_index("z")
    frame_block = lax.axis_index("xh") * y_count + lax.axis_index("y")
    where = jnp.stack([x, z, lax.axis_index("c"), frame_block]).astype(jnp.int32)
    swap = [(0, 1), (1, 0)]

    def flip(axis, count, step):
        return lambda v: lax.ppermute(v, axis, [(i, i ^ step) for i in range(count)])

    def along(block, distance):
        pairs = []
        for i in range(z_count):
            pairs.append((2 * i, 2 * ((i + distance) % z_count)))
            pairs.append((2 * i + 1, 2 * ((i - distance) % z_count) + 1))
        return lax.ppermute(block, ("z", "c"), pairs)

    def both(block):
        return lax.all_gather(block, "c", axis=0, tiled=True)

    def behind(value, earlier):
        return lax.optimization_barrier((value, earlier))[0]

    gathered = lax.all_gather(frame_maps, ("xl", "c"), axis=0)
    own = picked(where, gathered)
    queries = own_queries(where, query_table, start_frame, row_ids)
    weights = banded_weights(conv1_w, conv1_b, conv2_w, conv2_b)
    near = []
    for distance in (1, 2):
        near.append(along(own, distance))
    queries = queries + flip("y", y_count, 1)(queries)
    near = lax.optimization_barrier(near)

    ring = [joined(*near)]
    ring.append(along(ring[0], 2))
    if y_count > 2:
        queries = queries + flip("y", y_count, 2)(behind(queries, ring[0]))
    ring[1], weights = lax.optimization_barrier((ring[1], weights))

    ring.append(along(ring[1], 2))
    if xh_count > 1:
        queries = queries + flip("xh", xh_count, 1)(behind(queries, ring[1]))
    ring[2] = lax.optimization_barrier(ring[2])

    end = trimmed(where, ring[2])
    last = along(end, 2)
    sent_q = lax.ppermute(behind(queries, ring[2]), "xl", swap)
    cross = lax.ppermute(joined(*ring), "c", swap)
    last, cross, sent_q = lax.optimization_barrier((last, cross, sent_q))
    spread = ring + [cross, both(last)]

    kept, sent = pooled_costs(where, queries, sent_q, own, spread, *weights)

    def frame_pairs(cross):
        pairs = []
        for f in range(frame_count):
            before, after = (f - 1) % frame_count, (f + 1) % frame_count
            pairs.append((2 * before + 1, 2 * f + (0 if cross else 1)))
            pairs.append((2 * after, 2 * f + (1 if cross else 0)))
        return pairs

    partner = lax.ppermute(sent, "xl", swap)
    straight = lax.ppermute(kept, ("xh", "y", "xl"), frame_pairs(False))
    crossed = lax.ppermute(sent, ("xh", "y", "xl"), frame_pairs(True))
    pooled = (kept, partner, straight, crossed)
    return tail(frame_count, where, pooled, proj_w, proj_b, time_w, time_b)


def solution(mesh):

    frames, _ = mesh.devices.shape
    sizes = (frames // 4 or 1, min(frames, 4), 2, MAP // 4, 2)
    fine = Mesh(mesh.devices.reshape(sizes), ("xh", "y", "xl", "z", "c"))
    fr = ("xh", "y")
    qs = ("xl", "z", "c")
    placed = (P(fr, qs, None), P(fr, qs, None), P(qs), P(qs)) + (P(),) * 8
    return jax.shard_map(
        functools.partial(one_device, sizes),
        mesh=fine,
        in_specs=placed,
        out_specs=P(qs, fr, None),
        check_vma=False,
    )
```

```python
import functools

import jax
import jax.numpy as jnp
from jax import lax
from jax.experimental import pallas as pl
from jax.experimental.pallas import tpu as pltpu
from jax.sharding import Mesh, PartitionSpec as P


MAP = 64
CH1 = 16
CH2 = 32
HALF1 = MAP // 2
HALF2 = MAP // 4
ROW1 = HALF1 * CH1
ROW2 = HALF2 * CH2
BF = jnp.bfloat16
F32 = jnp.float32
INTERPRET = False


def iota(shape, dim):
    return lax.broadcasted_iota(jnp.int32, shape, dim)


def in_hbm(array):
    if INTERPRET:
        return array
    return pltpu.with_memory_space_constraint(array, pltpu.HBM)


def query_kernel(where_ref, table_hbm, start_hbm, rows_hbm, out_ref, table, start, rows, sems):
    frames_here = 2
    copies = [
        pltpu.make_async_copy(table_hbm, table, sems.at[0]),
        pltpu.make_async_copy(start_hbm, start, sems.at[1]),
        pltpu.make_async_copy(rows_hbm, rows, sems.at[2]),
    ]
    for copy in copies:
        copy.start()
    for copy in copies:
        copy.wait()
    low = where_ref[3] * frames_here
    owned = (start[...] >= low) & (start[...] < low + frames_here)
    row = jnp.where(owned, rows[...], -1)
    chosen = (iota((table.shape[1], row.shape[1]), 0) == row).astype(BF)
    got = lax.dot_general(chosen, table[0], (((0,), (0,)), ((), ())), preferred_element_type=F32)
    out_ref[...] = got.astype(BF)


def own_queries(where, query_table, start_frame, row_ids):
    count = start_frame.shape[0]
    hbm = pl.BlockSpec(memory_space=pltpu.HBM)
    return pl.pallas_call(
        query_kernel,
        out_shape=jax.ShapeDtypeStruct((count, query_table.shape[2]), BF),
        in_specs=[pl.BlockSpec(memory_space=pltpu.SMEM)] + [hbm] * 3,
        out_specs=pl.BlockSpec(memory_space=pltpu.VMEM),
        scratch_shapes=[
            pltpu.VMEM(query_table.shape, BF),
            pltpu.VMEM((1, count), jnp.int32),
            pltpu.VMEM((1, count), jnp.int32),
            pltpu.SemaphoreType.DMA((3,)),
        ],
        cost_estimate=pl.CostEstimate(flops=2_000_000, bytes_accessed=200_000, transcendentals=0),
        compiler_params=pltpu.CompilerParams(vmem_limit_bytes=4 << 20),
        interpret=INTERPRET,
    )(where, *map(in_hbm, (query_table, start_frame[None, :], row_ids[None, :])))


def pick_kernel(where_ref, all_ref, out_ref):
    x = where_ref[0]
    cells = all_ref.shape[2]
    for core in range(2):
        for side in range(2):
            out_ref[core, cells * side : cells * (side + 1), :] = all_ref[2 * side + core, x]


def picked(where, gathered):
    cells, channels = gathered.shape[2:]
    vmem = pl.BlockSpec(memory_space=pltpu.VMEM)
    return pl.pallas_call(
        pick_kernel,
        out_shape=jax.ShapeDtypeStruct((2, 2 * cells, channels), BF),
        in_specs=[pl.BlockSpec(memory_space=pltpu.SMEM), vmem],
        out_specs=vmem,
        cost_estimate=pl.CostEstimate(flops=0, bytes_accessed=300_000, transcendentals=0),
        compiler_params=pltpu.CompilerParams(vmem_limit_bytes=4 << 20),
        interpret=INTERPRET,
    )(where, gathered)


def weights_kernel(*refs):
    a_ref, b_ref, wide1_ref, wide2_ref, w1_ref, w2_ref, bias1_ref, bias2_ref, sems = refs[4:]
    copies = [
        pltpu.make_async_copy(refs[k], refs[8 + k], sems.at[k]) for k in range(4)
    ]
    for copy in copies:
        copy.start()
    b_ref[...] = jnp.zeros(b_ref.shape, BF)
    for copy in copies:
        copy.wait()
    spread = (iota((CH1, ROW1), 1) % CH1 == iota((CH1, ROW1), 0)).astype(BF)
    wide1_ref[...] = jnp.concatenate([bias1_ref[...]] * HALF1, axis=1)
    wide2_ref[...] = jnp.concatenate([bias2_ref[...]] * HALF2, axis=1)

    in_x = iota((MAP, ROW1), 0)
    out_x = iota((MAP, ROW1), 1) // CH1
    a_ref[0:MAP, :] = jnp.zeros((MAP, ROW1), BF)
    for dy in range(3):
        wide = jnp.dot(w1_ref[dy], spread, preferred_element_type=F32)
        block = jnp.zeros((MAP, ROW1), F32)
        for dx in range(3):
            block = jnp.where(in_x == 2 * out_x + dx - 1, wide[dx : dx + 1, :], block)
        a_ref[MAP * (dy + 1) : MAP * (dy + 2), :] = block.astype(BF)

    for dy in range(3):
        taps = jnp.concatenate([w2_ref[3 * dy + dx] for dx in range(3)], axis=0)
        taps = jnp.concatenate([taps] * (128 // CH2), axis=1)
        for out_x in range(HALF2):
            low = 2 * out_x - 1
            skip = max(0, -low)
            lane = CH2 * out_x
            part = lane % 128
            b_ref[
                ROW1 * dy + CH1 * (low + skip) : ROW1 * dy + CH1 * (low + 3), lane : lane + CH2
            ] = taps[CH1 * skip :, part : part + CH2]


def banded_weights(conv1_w, conv1_b, conv2_w, conv2_b):
    return pl.pallas_call(
        weights_kernel,
        out_shape=(
            jax.ShapeDtypeStruct((4 * MAP, ROW1), BF),
            jax.ShapeDtypeStruct((3 * ROW1, ROW2), BF),
            jax.ShapeDtypeStruct((1, ROW1), F32),
            jax.ShapeDtypeStruct((1, ROW2), F32),
        ),
        in_specs=[pl.BlockSpec(memory_space=pltpu.HBM)] * 4,
        scratch_shapes=[
            pltpu.VMEM((3, 3, CH1), BF),
            pltpu.VMEM((9, CH1, CH2), BF),
            pltpu.VMEM((1, CH1), F32),
            pltpu.VMEM((1, CH2), F32),
            pltpu.SemaphoreType.DMA((4,)),
        ],
        cost_estimate=pl.CostEstimate(flops=50_000_000, bytes_accessed=2_000_000, transcendentals=0),
        compiler_params=pltpu.CompilerParams(vmem_limit_bytes=8 << 20),
        interpret=INTERPRET,
    )(
        *map(
            in_hbm,
            (
                jnp.transpose(conv1_w, (0, 2, 1, 3)).reshape(3, 3, CH1),
                conv2_w.reshape(9, CH1, CH2),
                conv1_b[None, :],
                conv2_b[None, :],
            ),
        )
    )


def join_kernel(*refs):
    low = 0
    for ref in refs[:-1]:
        high = low + ref.shape[0]
        refs[-1][low:high] = ref[...]
        low = high


def joined(*blocks):
    count = sum(block.shape[0] for block in blocks)
    vmem = pl.BlockSpec(memory_space=pltpu.VMEM)
    shape = (count,) + blocks[0].shape[1:]
    return pl.pallas_call(
        join_kernel,
        out_shape=jax.ShapeDtypeStruct(shape, BF),
        in_specs=[vmem] * len(blocks),
        out_specs=vmem,
        cost_estimate=pl.CostEstimate(flops=0, bytes_accessed=300_000, transcendentals=0),
        compiler_params=pltpu.CompilerParams(vmem_limit_bytes=4 << 20),
        interpret=INTERPRET,
    )(*blocks)


def trim_kernel(where_ref, blocks_ref, out_ref):
    out_ref[0:2] = blocks_ref[0:2]
    out_ref[2] = blocks_ref[2 + where_ref[2]]


def trimmed(where, blocks):
    vmem = pl.BlockSpec(memory_space=pltpu.VMEM)
    return pl.pallas_call(
        trim_kernel,
        out_shape=jax.ShapeDtypeStruct((3,) + blocks.shape[1:], BF),
        in_specs=[pl.BlockSpec(memory_space=pltpu.SMEM), vmem],
        out_specs=vmem,
        cost_estimate=pl.CostEstimate(flops=0, bytes_accessed=1_000, transcendentals=0),
        compiler_params=pltpu.CompilerParams(vmem_limit_bytes=4 << 20),
        interpret=INTERPRET,
    )(where, blocks)


def cost_kernel(z_count, where_ref, kept_q_ref, sent_q_ref, own_ref, *refs):
    *mine_refs, cross_ref, last_ref = refs[:-9]
    a_ref, b_ref, bias1_ref, bias2_ref, kept_ref, sent_ref, corr, hid, acc = refs[-9:]
    z = where_ref[1]
    toward = 2 * where_ref[2] - 1
    n = 2 * kept_q_ref.shape[0]
    corr[0, :, 0:128] = jnp.zeros((n, 128), BF)
    hid[0, :, 0:ROW1] = jnp.zeros((n, ROW1), BF)
    q = jnp.concatenate([kept_q_ref[...], sent_q_ref[...]], axis=0)

    def put(low, high, shift):
        chip = lax.rem(z + z_count + shift, z_count)
        cells = jnp.concatenate([low[0:MAP], high[0:MAP], low[MAP:], high[MAP:]], axis=0)
        got = lax.dot_general(q, cells, (((1,), (1,)), ((), ())), preferred_element_type=F32)
        got = (got * 0.0625).astype(BF)
        for side in range(2):
            part = got[:, 128 * side : 128 * (side + 1)]
            y = side * z_count + chip
            corr[y, :, 128:256] = part
            corr[y + 1, :, 0:128] = part

    put(own_ref[0], own_ref[1], 0)
    distance = 0
    for ref in mine_refs:
        for k in range(0, ref.shape[0], 2):
            distance += 1
            put(ref[k], ref[k + 1], toward * distance)
            other = 2 * distance - 2
            put(cross_ref[other], cross_ref[other + 1], -toward * distance)
    put(last_ref[0], last_ref[1], -distance - 1)
    put(last_ref[3], last_ref[4], distance + 1)
    put(last_ref[2], last_ref[5], distance + 2)

    bias1 = bias1_ref[...]
    rows1 = 8
    for t in range(HALF1 // rows1):
        lhs = corr[rows1 * t : rows1 * (t + 1)].reshape(rows1 * n, 256)
        got = jnp.dot(lhs, a_ref[...], preferred_element_type=F32)
        got = jnp.maximum(got + bias1, 0.0).astype(BF).reshape(rows1, n, ROW1)
        for s in range(rows1):
            y = rows1 * t + s
            j = y // 2
            if y % 2 == 0:
                hid[j, :, ROW1 : 2 * ROW1] = got[s]
            else:
                hid[j, :, 2 * ROW1 : 3 * ROW1] = got[s]
                hid[j + 1, :, 0:ROW1] = got[s]

    bias2 = bias2_ref[...]
    half = ROW2 // 2
    rows2 = 4
    acc[...] = jnp.zeros(acc.shape, F32)
    for t in range(HALF2 // rows2):
        tile = slice(rows2 * t, rows2 * (t + 1))
        left = jnp.zeros((rows2 * n, half), F32)
        for dy in range(3):
            k = slice(ROW1 * dy, ROW1 * dy + ROW1 // 2)
            left += jnp.dot(
                hid[tile, :, k].reshape(rows2 * n, ROW1 // 2),
                b_ref[k, 0:half],
                preferred_element_type=F32,
            )
        right = jnp.dot(
            hid[tile].reshape(rows2 * n, 3 * ROW1), b_ref[:, half:], preferred_element_type=F32
        )
        left = jnp.maximum(left + bias2[:, :half], 0.0).reshape(rows2, n, half)
        right = jnp.maximum(right + bias2[:, half:], 0.0).reshape(rows2, n, half)
        acc[:, :half] += jnp.sum(left, axis=0)
        acc[:, half:] += jnp.sum(right, axis=0)
    total = acc[:, 0:128]
    for k in range(1, ROW2 // 128):
        total = total + acc[:, 128 * k : 128 * (k + 1)]
    total = (total[:, 0:32] + total[:, 32:64]) + (total[:, 64:96] + total[:, 96:128])
    pooled = (total * (1.0 / (HALF2 * HALF2))).astype(BF)
    kept_ref[...] = pooled[: n // 2]
    sent_ref[...] = pooled[n // 2 :]


def pooled_costs(where, kept_q, sent_q, own, far, a, b, bias1, bias2):
    n = 2 * kept_q.shape[0]
    z_count = MAP // 4
    vmem = pl.BlockSpec(memory_space=pltpu.VMEM)

    return pl.pallas_call(
        functools.partial(cost_kernel, z_count),
        out_shape=(jax.ShapeDtypeStruct((n // 2, CH2), BF),) * 2,
        in_specs=[pl.BlockSpec(memory_space=pltpu.SMEM)] + [vmem] * (7 + len(far)),
        out_specs=(vmem, vmem),
        scratch_shapes=[
            pltpu.VMEM((HALF1 + 1, n, 256), BF),
            pltpu.VMEM((HALF2 + 1, n, 3 * ROW1), BF),
            pltpu.VMEM((n, ROW2), F32),
        ],
        cost_estimate=pl.CostEstimate(
            flops=5_000_000_000, bytes_accessed=4_000_000, transcendentals=0
        ),
        compiler_params=pltpu.CompilerParams(vmem_limit_bytes=28 << 20),
        interpret=INTERPRET,
    )(where, kept_q, sent_q, own, *far, a, b, bias1, bias2)


def tail_kernel(
    frame_count,
    where_ref,
    kept_ref,
    partner_ref,
    straight_ref,
    crossed_ref,
    proj_w_ref,
    proj_b_ref,
    time_w_ref,
    time_b_ref,
    out_ref,
):
    x, frame_block = where_ref[0], where_ref[3]
    first = x == 0
    kept, partner = kept_ref[...], partner_ref[...]
    straight, crossed = straight_ref[...], crossed_ref[...]
    around = [
        jnp.where(first, crossed, straight),
        jnp.where(first, kept, partner),
        jnp.where(first, partner, kept),
        jnp.where(first, straight, crossed),
    ]
    valid = [frame_block > 0, None, None, frame_block < frame_count - 1]
    wide = []
    for pooled, there in zip(around, valid):
        got = jnp.dot(pooled, proj_w_ref[...], preferred_element_type=F32) + proj_b_ref[...]
        got = got.astype(BF).astype(F32)
        if there is not None:
            got = jnp.where(there, got, 0.0)
        wide.append(got)
    for t in range(2):
        mixed = (
            time_w_ref[0:1, :] * wide[t]
            + time_w_ref[1:2, :] * wide[t + 1]
            + time_w_ref[2:3, :] * wide[t + 2]
            + time_b_ref[...]
        )
        out_ref[:, t, :] = mixed.astype(BF)


def tail(frame_count, where, pooled, proj_w, proj_b, time_w, time_b):
    count, width = pooled[0].shape[0], proj_w.shape[1]
    vmem = pl.BlockSpec(memory_space=pltpu.VMEM)
    return pl.pallas_call(
        functools.partial(tail_kernel, frame_count),
        out_shape=jax.ShapeDtypeStruct((count, 2, width), BF),
        in_specs=[pl.BlockSpec(memory_space=pltpu.SMEM)] + [vmem] * 8,
        out_specs=vmem,
        compiler_params=pltpu.CompilerParams(vmem_limit_bytes=8 << 20),
        interpret=INTERPRET,
    )(where, *pooled, proj_w, proj_b[None, :], time_w, time_b[None, :])


def one_device(
    sizes,
    frame_maps,
    query_table,
    start_frame,
    row_ids,
    conv1_w,
    conv1_b,
    conv2_w,
    conv2_b,
    proj_w,
    proj_b,
    time_w,
    time_b,
):
    xh_count, y_count, _, z_count, _ = sizes
    frame_count = xh_count * y_count
    x = lax.axis_index("xl")
    z = lax.axis_index("z")
    frame_block = lax.axis_index("xh") * y_count + lax.axis_index("y")
    where = jnp.stack([x, z, lax.axis_index("c"), frame_block]).astype(jnp.int32)
    swap = [(0, 1), (1, 0)]

    def flip(axis, count, step):
        return lambda v: lax.ppermute(v, axis, [(i, i ^ step) for i in range(count)])

    def along(block, distance):
        pairs = []
        for i in range(z_count):
            pairs.append((2 * i, 2 * ((i + distance) % z_count)))
            pairs.append((2 * i + 1, 2 * ((i - distance) % z_count) + 1))
        return lax.ppermute(block, ("z", "c"), pairs)

    def both(block):
        return lax.all_gather(block, "c", axis=0, tiled=True)

    def behind(value, earlier):
        return lax.optimization_barrier((value, earlier))[0]

    gathered = lax.all_gather(frame_maps, ("xl", "c"), axis=0)
    own = picked(where, gathered)
    queries = own_queries(where, query_table, start_frame, row_ids)
    weights = banded_weights(conv1_w, conv1_b, conv2_w, conv2_b)
    near = []
    for distance in (1, 2):
        near.append(along(own, distance))
    queries = queries + flip("y", y_count, 1)(queries)
    near = lax.optimization_barrier(near)

    ring = [joined(*near)]
    ring.append(along(ring[0], 2))
    if y_count > 2:
        queries = queries + flip("y", y_count, 2)(behind(queries, ring[0]))
    ring[1], weights = lax.optimization_barrier((ring[1], weights))

    ring.append(along(ring[1], 2))
    if xh_count > 1:
        queries = queries + flip("xh", xh_count, 1)(behind(queries, ring[1]))
    ring[2] = lax.optimization_barrier(ring[2])

    end = trimmed(where, ring[2])
    last = along(end, 2)
    sent_q = lax.ppermute(behind(queries, ring[2]), "xl", swap)
    cross = lax.ppermute(joined(*ring), "c", swap)
    last, cross, sent_q = lax.optimization_barrier((last, cross, sent_q))
    spread = ring + [cross, both(last)]

    kept, sent = pooled_costs(where, queries, sent_q, own, spread, *weights)

    def frame_pairs(cross):
        pairs = []
        for f in range(frame_count):
            if f > 0:
                pairs.append((2 * (f - 1) + 1, 2 * f + (0 if cross else 1)))
            if f < frame_count - 1:
                pairs.append((2 * (f + 1), 2 * f + (1 if cross else 0)))
        return pairs

    partner = lax.ppermute(sent, "xl", swap)
    straight = lax.ppermute(kept, ("xh", "y", "xl"), frame_pairs(False))
    crossed = lax.ppermute(sent, ("xh", "y", "xl"), frame_pairs(True))
    pooled = (kept, partner, straight, crossed)
    return tail(frame_count, where, pooled, proj_w, proj_b, time_w, time_b)


def solution(mesh):

    frames, _ = mesh.devices.shape
    sizes = (frames // 4 or 1, min(frames, 4), 2, MAP // 4, 2)
    fine = Mesh(mesh.devices.reshape(sizes), ("xh", "y", "xl", "z", "c"))
    fr = ("xh", "y")
    qs = ("xl", "z", "c")
    placed = (P(fr, qs, None), P(fr, qs, None), P(qs), P(qs)) + (P(),) * 8
    return jax.shard_map(
        functools.partial(one_device, sizes),
        mesh=fine,
        in_specs=placed,
        out_specs=P(qs, fr, None),
        check_vma=False,
    )
```

```python
import functools

import jax
import jax.numpy as jnp
from jax import lax
from jax.experimental import pallas as pl
from jax.experimental.pallas import tpu as pltpu
from jax.sharding import Mesh, PartitionSpec as P


MAP = 64
CH1 = 16
CH2 = 32
HALF1 = MAP // 2
HALF2 = MAP // 4
ROW1 = HALF1 * CH1
ROW2 = HALF2 * CH2
BF = jnp.bfloat16
F32 = jnp.float32
INTERPRET = False


def iota(shape, dim):
    return lax.broadcasted_iota(jnp.int32, shape, dim)


def in_hbm(array):
    if INTERPRET:
        return array
    return pltpu.with_memory_space_constraint(array, pltpu.HBM)


def opening_kernel(
    where_ref, maps_hbm, table_hbm, start_hbm, rows_hbm, out_ref, table, start, rows, sems
):
    frames_here, cells = maps_hbm.shape[0], maps_hbm.shape[1]
    copies = [
        pltpu.make_async_copy(start_hbm, start, sems.at[0]),
        pltpu.make_async_copy(rows_hbm, rows, sems.at[1]),
        pltpu.make_async_copy(table_hbm, table, sems.at[2]),
    ]
    for f in range(frames_here):
        part = out_ref.at[pl.ds(cells * f, cells)]
        copies.append(pltpu.make_async_copy(maps_hbm.at[f], part, sems.at[3 + f]))
    for copy in copies:
        copy.start()
    for copy in copies[:3]:
        copy.wait()
    low = where_ref[2] * frames_here
    owned = (start[...] >= low) & (start[...] < low + frames_here)
    row = jnp.where(owned, rows[...], -1)
    chosen = (iota((table.shape[1], row.shape[1]), 0) == row).astype(BF)
    got = lax.dot_general(chosen, table[0], (((0,), (0,)), ((), ())), preferred_element_type=F32)
    out_ref[frames_here * cells :, :] = got.astype(BF)
    for copy in copies[3:]:
        copy.wait()


def opening(where, frame_maps, query_table, start_frame, row_ids):
    frames_here, cells, channels = frame_maps.shape
    count = start_frame.shape[0]
    hbm = pl.BlockSpec(memory_space=pltpu.HBM)
    arrays = (frame_maps, query_table, start_frame[None, :], row_ids[None, :])
    return pl.pallas_call(
        opening_kernel,
        out_shape=jax.ShapeDtypeStruct((frames_here * cells + count, channels), BF),
        in_specs=[pl.BlockSpec(memory_space=pltpu.SMEM)] + [hbm] * 4,
        out_specs=pl.BlockSpec(memory_space=pltpu.VMEM),
        scratch_shapes=[
            pltpu.VMEM(query_table.shape, BF),
            pltpu.VMEM((1, count), jnp.int32),
            pltpu.VMEM((1, count), jnp.int32),
            pltpu.SemaphoreType.DMA((5,)),
        ],
        cost_estimate=pl.CostEstimate(flops=2_000_000, bytes_accessed=200_000, transcendentals=0),
        compiler_params=pltpu.CompilerParams(vmem_limit_bytes=4 << 20),
        interpret=INTERPRET,
    )(where, *map(in_hbm, arrays))


def pick_kernel(where_ref, all_ref, block_ref, queries_ref):
    x, core = where_ref[0], where_ref[3]
    cells = block_ref.shape[1] // 2
    frame = pl.ds(pl.multiple_of(cells * x, cells), cells)
    for c in range(2):
        for side in range(2):
            block_ref[c, cells * side : cells * (side + 1), :] = all_ref[2 * side + c, frame, :]
    count = queries_ref.shape[0] // 2
    first = 2 * cells
    queries_ref[0:count, :] = all_ref[2 * x + core, first : first + count, :]
    queries_ref[count:, :] = all_ref[2 * (1 - x) + core, first : first + count, :]


def picked(where, gathered, cells):
    channels = gathered.shape[2]
    count = gathered.shape[1] - 2 * cells
    vmem = pl.BlockSpec(memory_space=pltpu.VMEM)
    return pl.pallas_call(
        pick_kernel,
        out_shape=(
            jax.ShapeDtypeStruct((2, 2 * cells, channels), BF),
            jax.ShapeDtypeStruct((2 * count, channels), BF),
        ),
        in_specs=[pl.BlockSpec(memory_space=pltpu.SMEM), vmem],
        out_specs=(vmem, vmem),
        cost_estimate=pl.CostEstimate(flops=0, bytes_accessed=300_000, transcendentals=0),
        compiler_params=pltpu.CompilerParams(vmem_limit_bytes=4 << 20),
        interpret=INTERPRET,
    )(where, gathered)


def weights_kernel(*refs):
    a_ref, b_ref, wide1_ref, wide2_ref, w1_ref, w2_ref, bias1_ref, bias2_ref, sems = refs[4:]
    copies = [
        pltpu.make_async_copy(refs[k], refs[8 + k], sems.at[k]) for k in range(4)
    ]
    for copy in copies:
        copy.start()
    b_ref[...] = jnp.zeros(b_ref.shape, BF)
    for copy in copies:
        copy.wait()
    spread = (iota((CH1, ROW1), 1) % CH1 == iota((CH1, ROW1), 0)).astype(BF)
    wide1_ref[...] = jnp.concatenate([bias1_ref[...]] * HALF1, axis=1)
    wide2_ref[...] = jnp.concatenate([bias2_ref[...]] * HALF2, axis=1)

    in_x = iota((MAP, ROW1), 0)
    out_x = iota((MAP, ROW1), 1) // CH1
    a_ref[0:MAP, :] = jnp.zeros((MAP, ROW1), BF)
    for dy in range(3):
        wide = jnp.dot(w1_ref[dy], spread, preferred_element_type=F32)
        block = jnp.zeros((MAP, ROW1), F32)
        for dx in range(3):
            block = jnp.where(in_x == 2 * out_x + dx - 1, wide[dx : dx + 1, :], block)
        a_ref[MAP * (dy + 1) : MAP * (dy + 2), :] = block.astype(BF)

    for dy in range(3):
        taps = jnp.concatenate([w2_ref[3 * dy + dx] for dx in range(3)], axis=0)
        taps = jnp.concatenate([taps] * (128 // CH2), axis=1)
        for out_x in range(HALF2):
            low = 2 * out_x - 1
            skip = max(0, -low)
            lane = CH2 * out_x
            part = lane % 128
            b_ref[
                ROW1 * dy + CH1 * (low + skip) : ROW1 * dy + CH1 * (low + 3), lane : lane + CH2
            ] = taps[CH1 * skip :, part : part + CH2]


def banded_weights(conv1_w, conv1_b, conv2_w, conv2_b):
    return pl.pallas_call(
        weights_kernel,
        out_shape=(
            jax.ShapeDtypeStruct((4 * MAP, ROW1), BF),
            jax.ShapeDtypeStruct((3 * ROW1, ROW2), BF),
            jax.ShapeDtypeStruct((1, ROW1), F32),
            jax.ShapeDtypeStruct((1, ROW2), F32),
        ),
        in_specs=[pl.BlockSpec(memory_space=pltpu.HBM)] * 4,
        scratch_shapes=[
            pltpu.VMEM((3, 3, CH1), BF),
            pltpu.VMEM((9, CH1, CH2), BF),
            pltpu.VMEM((1, CH1), F32),
            pltpu.VMEM((1, CH2), F32),
            pltpu.SemaphoreType.DMA((4,)),
        ],
        cost_estimate=pl.CostEstimate(flops=50_000_000, bytes_accessed=2_000_000, transcendentals=0),
        compiler_params=pltpu.CompilerParams(vmem_limit_bytes=8 << 20),
        interpret=INTERPRET,
    )(
        *map(
            in_hbm,
            (
                jnp.transpose(conv1_w, (0, 2, 1, 3)).reshape(3, 3, CH1),
                conv2_w.reshape(9, CH1, CH2),
                conv1_b[None, :],
                conv2_b[None, :],
            ),
        )
    )


def join_kernel(*refs):
    low = 0
    for ref in refs[:-1]:
        high = low + ref.shape[0]
        refs[-1][low:high] = ref[...]
        low = high


def joined(*blocks):
    count = sum(block.shape[0] for block in blocks)
    vmem = pl.BlockSpec(memory_space=pltpu.VMEM)
    shape = (count,) + blocks[0].shape[1:]
    return pl.pallas_call(
        join_kernel,
        out_shape=jax.ShapeDtypeStruct(shape, BF),
        in_specs=[vmem] * len(blocks),
        out_specs=vmem,
        cost_estimate=pl.CostEstimate(flops=0, bytes_accessed=300_000, transcendentals=0),
        compiler_params=pltpu.CompilerParams(vmem_limit_bytes=4 << 20),
        interpret=INTERPRET,
    )(*blocks)


def trim_kernel(where_ref, blocks_ref, out_ref):
    out_ref[0:2] = blocks_ref[0:2]
    out_ref[2] = blocks_ref[2 + where_ref[3]]


def trimmed(where, blocks):
    vmem = pl.BlockSpec(memory_space=pltpu.VMEM)
    return pl.pallas_call(
        trim_kernel,
        out_shape=jax.ShapeDtypeStruct((3,) + blocks.shape[1:], BF),
        in_specs=[pl.BlockSpec(memory_space=pltpu.SMEM), vmem],
        out_specs=vmem,
        cost_estimate=pl.CostEstimate(flops=0, bytes_accessed=300_000, transcendentals=0),
        compiler_params=pltpu.CompilerParams(vmem_limit_bytes=4 << 20),
        interpret=INTERPRET,
    )(where, blocks)


def correlate(corr, q, z, z_count, low, high, shift):
    chip = lax.rem(z + z_count + shift, z_count)
    cells = jnp.concatenate([low[0:MAP], high[0:MAP], low[MAP:], high[MAP:]], axis=0)
    got = lax.dot_general(q, cells, (((1,), (1,)), ((), ())), preferred_element_type=F32)
    got = (got * 0.0625).astype(BF)
    for side in range(2):
        part = got[:, 128 * side : 128 * (side + 1)]
        y = side * z_count + chip
        corr[y, :, 128:256] = part
        corr[y + 1, :, 0:128] = part


def corr_kernel(z_count, where_ref, q_ref, own_ref, *refs):
    *mine_refs, corr = refs
    z = where_ref[1]
    toward = 2 * where_ref[3] - 1
    q = q_ref[...]
    corr[...] = jnp.zeros(corr.shape, BF)
    correlate(corr, q, z, z_count, own_ref[0], own_ref[1], 0)
    distance = 0
    for ref in mine_refs:
        for k in range(0, ref.shape[0], 2):
            distance += 1
            correlate(corr, q, z, z_count, ref[k], ref[k + 1], toward * distance)


def partial_corr(where, queries, own, blocks):
    vmem = pl.BlockSpec(memory_space=pltpu.VMEM)
    return pl.pallas_call(
        functools.partial(corr_kernel, MAP // 4),
        out_shape=jax.ShapeDtypeStruct((HALF1 + 1, queries.shape[0], 256), BF),
        in_specs=[pl.BlockSpec(memory_space=pltpu.SMEM)] + [vmem] * (2 + len(blocks)),
        out_specs=vmem,
        cost_estimate=pl.CostEstimate(
            flops=250_000_000, bytes_accessed=4_000_000, transcendentals=0
        ),
        compiler_params=pltpu.CompilerParams(vmem_limit_bytes=12 << 20),
        interpret=INTERPRET,
    )(where, queries, own, *blocks)


def cost_kernel(z_count, where_ref, q_ref, last_ref, old_ref, cross_ref, *refs):
    del old_ref
    a_ref, b_ref, bias1_ref, bias2_ref, kept_ref, sent_ref, corr, hid, acc = refs
    z = where_ref[1]
    n = q_ref.shape[0]
    hid[0, :, 0:ROW1] = jnp.zeros((n, ROW1), BF)
    q = q_ref[...]
    away = 1 - 2 * where_ref[3]
    for k in range(0, cross_ref.shape[0], 2):
        correlate(corr, q, z, z_count, cross_ref[k], cross_ref[k + 1], away * (k // 2 + 1))
    correlate(corr, q, z, z_count, last_ref[0], last_ref[1], -7)
    correlate(corr, q, z, z_count, last_ref[3], last_ref[4], 7)
    correlate(corr, q, z, z_count, last_ref[2], last_ref[5], 8)

    bias1 = bias1_ref[...]
    rows1 = 8
    for t in range(HALF1 // rows1):
        lhs = corr[rows1 * t : rows1 * (t + 1)].reshape(rows1 * n, 256)
        got = jnp.dot(lhs, a_ref[...], preferred_element_type=F32)
        got = jnp.maximum(got + bias1, 0.0).astype(BF).reshape(rows1, n, ROW1)
        for s in range(rows1):
            y = rows1 * t + s
            j = y // 2
            if y % 2 == 0:
                hid[j, :, ROW1 : 2 * ROW1] = got[s]
            else:
                hid[j, :, 2 * ROW1 : 3 * ROW1] = got[s]
                hid[j + 1, :, 0:ROW1] = got[s]

    bias2 = bias2_ref[...]
    half = ROW2 // 2
    rows2 = 4
    acc[...] = jnp.zeros(acc.shape, F32)
    for t in range(HALF2 // rows2):
        tile = slice(rows2 * t, rows2 * (t + 1))
        left = jnp.zeros((rows2 * n, half), F32)
        for dy in range(3):
            k = slice(ROW1 * dy, ROW1 * dy + ROW1 // 2)
            left += jnp.dot(
                hid[tile, :, k].reshape(rows2 * n, ROW1 // 2),
                b_ref[k, 0:half],
                preferred_element_type=F32,
            )
        right = jnp.dot(
            hid[tile].reshape(rows2 * n, 3 * ROW1), b_ref[:, half:], preferred_element_type=F32
        )
        left = jnp.maximum(left + bias2[:, :half], 0.0).reshape(rows2, n, half)
        right = jnp.maximum(right + bias2[:, half:], 0.0).reshape(rows2, n, half)
        acc[:, :half] += jnp.sum(left, axis=0)
        acc[:, half:] += jnp.sum(right, axis=0)
    total = acc[:, 0:128]
    for k in range(1, ROW2 // 128):
        total = total + acc[:, 128 * k : 128 * (k + 1)]
    total = (total[:, 0:32] + total[:, 32:64]) + (total[:, 64:96] + total[:, 96:128])
    pooled = (total * (1.0 / (HALF2 * HALF2))).astype(BF)
    kept_ref[...] = pooled[: n // 2]
    sent_ref[...] = pooled[n // 2 :]


def pooled_costs(where, queries, last, corr, cross, a, b, bias1, bias2):
    n = queries.shape[0]
    vmem = pl.BlockSpec(memory_space=pltpu.VMEM)
    return pl.pallas_call(
        functools.partial(cost_kernel, MAP // 4),
        out_shape=(jax.ShapeDtypeStruct((n // 2, CH2), BF),) * 2
        + (jax.ShapeDtypeStruct(corr.shape, BF),),
        in_specs=[pl.BlockSpec(memory_space=pltpu.SMEM)] + [vmem] * 8,
        out_specs=(vmem,) * 3,
        scratch_shapes=[
            pltpu.VMEM((HALF2 + 1, n, 3 * ROW1), BF),
            pltpu.VMEM((n, ROW2), F32),
        ],
        input_output_aliases={3: 2},
        cost_estimate=pl.CostEstimate(
            flops=5_000_000_000, bytes_accessed=4_000_000, transcendentals=0
        ),
        compiler_params=pltpu.CompilerParams(vmem_limit_bytes=28 << 20),
        interpret=INTERPRET,
    )(where, queries, last, corr, cross, a, b, bias1, bias2)[:2]


def tail_kernel(
    frame_count,
    where_ref,
    kept_ref,
    partner_ref,
    straight_ref,
    crossed_ref,
    proj_w_ref,
    proj_b_ref,
    time_w_ref,
    time_b_ref,
    out_ref,
):
    x, frame_block = where_ref[0], where_ref[2]
    first = x == 0
    kept, partner = kept_ref[...], partner_ref[...]
    straight, crossed = straight_ref[...], crossed_ref[...]
    around = [
        jnp.where(first, crossed, straight),
        jnp.where(first, kept, partner),
        jnp.where(first, partner, kept),
        jnp.where(first, straight, crossed),
    ]
    valid = [frame_block > 0, None, None, frame_block < frame_count - 1]
    wide = []
    for pooled, there in zip(around, valid):
        got = jnp.dot(pooled, proj_w_ref[...], preferred_element_type=F32) + proj_b_ref[...]
        got = got.astype(BF).astype(F32)
        if there is not None:
            got = jnp.where(there, got, 0.0)
        wide.append(got)
    for t in range(2):
        mixed = (
            time_w_ref[0:1, :] * wide[t]
            + time_w_ref[1:2, :] * wide[t + 1]
            + time_w_ref[2:3, :] * wide[t + 2]
            + time_b_ref[...]
        )
        out_ref[:, t, :] = mixed.astype(BF)


def tail(frame_count, where, pooled, proj_w, proj_b, time_w, time_b):
    count, width = pooled[0].shape[0], proj_w.shape[1]
    vmem = pl.BlockSpec(memory_space=pltpu.VMEM)
    return pl.pallas_call(
        functools.partial(tail_kernel, frame_count),
        out_shape=jax.ShapeDtypeStruct((count, 2, width), BF),
        in_specs=[pl.BlockSpec(memory_space=pltpu.SMEM)] + [vmem] * 8,
        out_specs=vmem,
        compiler_params=pltpu.CompilerParams(vmem_limit_bytes=8 << 20),
        interpret=INTERPRET,
    )(where, *pooled, proj_w, proj_b[None, :], time_w, time_b[None, :])


def one_device(
    sizes,
    frame_maps,
    query_table,
    start_frame,
    row_ids,
    conv1_w,
    conv1_b,
    conv2_w,
    conv2_b,
    proj_w,
    proj_b,
    time_w,
    time_b,
):
    xh_count, y_count, _, z_count, _ = sizes
    frame_count = xh_count * y_count
    x = lax.axis_index("xl")
    z = lax.axis_index("z")
    frame_block = lax.axis_index("xh") * y_count + lax.axis_index("y")
    where = jnp.stack([x, z, frame_block, lax.axis_index("c")]).astype(jnp.int32)
    swap = [(0, 1), (1, 0)]

    def flip(axis, count, step):
        return lambda v: lax.ppermute(v, axis, [(i, i ^ step) for i in range(count)])

    def along(block, distance):
        pairs = []
        for i in range(z_count):
            pairs.append((2 * i, 2 * ((i + distance) % z_count)))
            pairs.append((2 * i + 1, 2 * ((i - distance) % z_count) + 1))
        return lax.ppermute(block, ("z", "c"), pairs)

    def both(block):
        return lax.all_gather(block, "c", axis=0, tiled=True)

    def behind(value, earlier):
        return lax.optimization_barrier((value, earlier))[0]

    message = opening(where, frame_maps, query_table, start_frame, row_ids)
    gathered = lax.all_gather(message, ("xl", "c"), axis=0)
    own, queries = picked(where, gathered, frame_maps.shape[1])
    weights = banded_weights(conv1_w, conv1_b, conv2_w, conv2_b)
    near = []
    for distance in (1, 2):
        near.append(along(own, distance))
    queries = queries + flip("y", y_count, 1)(queries)
    near = lax.optimization_barrier(near)

    ring = [joined(*near)]
    ring.append(along(ring[0], 2))
    if y_count > 2:
        queries = queries + flip("y", y_count, 2)(behind(queries, ring[0]))
    ring[1], weights = lax.optimization_barrier((ring[1], weights))

    ring.append(along(ring[1], 2))
    if xh_count > 1:
        queries = queries + flip("xh", xh_count, 1)(behind(queries, ring[1]))
    ring[2] = lax.optimization_barrier(ring[2])

    end = trimmed(where, ring[2])
    last = along(end, 2)
    cross = lax.ppermute(joined(*ring), "c", swap)
    corr = partial_corr(where, queries, own, ring)
    last, corr = lax.optimization_barrier((last, corr))

    kept, sent = pooled_costs(where, queries, both(last), corr, cross, *weights)

    def frame_pairs(cross):
        pairs = []
        for f in range(frame_count):
            if f > 0:
                pairs.append((2 * (f - 1) + 1, 2 * f + (0 if cross else 1)))
            if f < frame_count - 1:
                pairs.append((2 * (f + 1), 2 * f + (1 if cross else 0)))
        return pairs

    partner = lax.ppermute(sent, "xl", swap)
    straight = lax.ppermute(kept, ("xh", "y", "xl"), frame_pairs(False))
    crossed = lax.ppermute(sent, ("xh", "y", "xl"), frame_pairs(True))
    pooled = (kept, partner, straight, crossed)
    return tail(frame_count, where, pooled, proj_w, proj_b, time_w, time_b)


def solution(mesh):

    frames, _ = mesh.devices.shape
    sizes = (frames // 4 or 1, min(frames, 4), 2, MAP // 4, 2)
    fine = Mesh(mesh.devices.reshape(sizes), ("xh", "y", "xl", "z", "c"))
    fr = ("xh", "y")
    qs = ("xl", "z", "c")
    placed = (P(fr, qs, None), P(fr, qs, None), P(qs), P(qs)) + (P(),) * 8
    return jax.shard_map(
        functools.partial(one_device, sizes),
        mesh=fine,
        in_specs=placed,
        out_specs=P(qs, fr, None),
        check_vma=False,
    )
```

```python
import functools

import jax
import jax.numpy as jnp
from jax import lax
from jax.experimental import pallas as pl
from jax.experimental.pallas import tpu as pltpu
from jax.sharding import Mesh, PartitionSpec as P


MAP = 64
CH1 = 16
CH2 = 32
HALF1 = MAP // 2
HALF2 = MAP // 4
ROW1 = HALF1 * CH1
ROW2 = HALF2 * CH2
BF = jnp.bfloat16
F32 = jnp.float32
INTERPRET = False


def iota(shape, dim):
    return lax.broadcasted_iota(jnp.int32, shape, dim)


def in_hbm(array):
    if INTERPRET:
        return array
    return pltpu.with_memory_space_constraint(array, pltpu.HBM)


def opening_kernel(
    where_ref, maps_hbm, table_hbm, start_hbm, rows_hbm, out_ref, table, start, rows, sems
):
    frames_here, cells = maps_hbm.shape[0], maps_hbm.shape[1]
    copies = [
        pltpu.make_async_copy(start_hbm, start, sems.at[0]),
        pltpu.make_async_copy(rows_hbm, rows, sems.at[1]),
        pltpu.make_async_copy(table_hbm, table, sems.at[2]),
    ]
    for f in range(frames_here):
        part = out_ref.at[pl.ds(cells * f, cells)]
        copies.append(pltpu.make_async_copy(maps_hbm.at[f], part, sems.at[3 + f]))
    for copy in copies:
        copy.start()
    for copy in copies[:3]:
        copy.wait()
    low = where_ref[2] * frames_here
    owned = (start[...] >= low) & (start[...] < low + frames_here)
    row = jnp.where(owned, rows[...], -1)
    chosen = (iota((table.shape[1], row.shape[1]), 0) == row).astype(BF)
    got = lax.dot_general(chosen, table[0], (((0,), (0,)), ((), ())), preferred_element_type=F32)
    out_ref[frames_here * cells :, :] = got.astype(BF)
    for copy in copies[3:]:
        copy.wait()


def opening(where, frame_maps, query_table, start_frame, row_ids):
    frames_here, cells, channels = frame_maps.shape
    count = start_frame.shape[0]
    hbm = pl.BlockSpec(memory_space=pltpu.HBM)
    arrays = (frame_maps, query_table, start_frame[None, :], row_ids[None, :])
    return pl.pallas_call(
        opening_kernel,
        out_shape=jax.ShapeDtypeStruct((frames_here * cells + count, channels), BF),
        in_specs=[pl.BlockSpec(memory_space=pltpu.SMEM)] + [hbm] * 4,
        out_specs=pl.BlockSpec(memory_space=pltpu.VMEM),
        scratch_shapes=[
            pltpu.VMEM(query_table.shape, BF),
            pltpu.VMEM((1, count), jnp.int32),
            pltpu.VMEM((1, count), jnp.int32),
            pltpu.SemaphoreType.DMA((5,)),
        ],
        cost_estimate=pl.CostEstimate(flops=2_000_000, bytes_accessed=200_000, transcendentals=0),
        compiler_params=pltpu.CompilerParams(vmem_limit_bytes=4 << 20),
        interpret=INTERPRET,
    )(where, *map(in_hbm, arrays))


def pick_kernel(where_ref, all_ref, block_ref, queries_ref):
    x, core = where_ref[0], where_ref[3]
    cells = block_ref.shape[1] // 2
    frame = pl.ds(pl.multiple_of(cells * x, cells), cells)
    for c in range(2):
        for side in range(2):
            block_ref[c, cells * side : cells * (side + 1), :] = all_ref[2 * side + c, frame, :]
    count = queries_ref.shape[0] // 2
    first = 2 * cells
    queries_ref[0:count, :] = all_ref[2 * x + core, first : first + count, :]
    queries_ref[count:, :] = all_ref[2 * (1 - x) + core, first : first + count, :]


def picked(where, gathered, cells):
    channels = gathered.shape[2]
    count = gathered.shape[1] - 2 * cells
    vmem = pl.BlockSpec(memory_space=pltpu.VMEM)
    return pl.pallas_call(
        pick_kernel,
        out_shape=(
            jax.ShapeDtypeStruct((2, 2 * cells, channels), BF),
            jax.ShapeDtypeStruct((2 * count, channels), BF),
        ),
        in_specs=[pl.BlockSpec(memory_space=pltpu.SMEM), vmem],
        out_specs=(vmem, vmem),
        cost_estimate=pl.CostEstimate(flops=0, bytes_accessed=300_000, transcendentals=0),
        compiler_params=pltpu.CompilerParams(vmem_limit_bytes=4 << 20),
        interpret=INTERPRET,
    )(where, gathered)


def weights_kernel(*refs):
    a_ref, b_ref, wide1_ref, wide2_ref, w1_ref, w2_ref, bias1_ref, bias2_ref, sems = refs[4:]
    copies = [
        pltpu.make_async_copy(refs[k], refs[8 + k], sems.at[k]) for k in range(4)
    ]
    for copy in copies:
        copy.start()
    b_ref[...] = jnp.zeros(b_ref.shape, BF)
    for copy in copies:
        copy.wait()
    spread = (iota((CH1, ROW1), 1) % CH1 == iota((CH1, ROW1), 0)).astype(BF)
    wide1_ref[...] = jnp.concatenate([bias1_ref[...]] * HALF1, axis=1)
    wide2_ref[...] = jnp.concatenate([bias2_ref[...]] * HALF2, axis=1)

    in_x = iota((MAP, ROW1), 0)
    out_x = iota((MAP, ROW1), 1) // CH1
    a_ref[0:MAP, :] = jnp.zeros((MAP, ROW1), BF)
    for dy in range(3):
        wide = jnp.dot(w1_ref[dy], spread, preferred_element_type=F32)
        block = jnp.zeros((MAP, ROW1), F32)
        for dx in range(3):
            block = jnp.where(in_x == 2 * out_x + dx - 1, wide[dx : dx + 1, :], block)
        a_ref[MAP * (dy + 1) : MAP * (dy + 2), :] = block.astype(BF)

    for dy in range(3):
        taps = jnp.concatenate([w2_ref[3 * dy + dx] for dx in range(3)], axis=0)
        taps = jnp.concatenate([taps] * (128 // CH2), axis=1)
        for out_x in range(HALF2):
            low = 2 * out_x - 1
            skip = max(0, -low)
            lane = CH2 * out_x
            part = lane % 128
            b_ref[
                ROW1 * dy + CH1 * (low + skip) : ROW1 * dy + CH1 * (low + 3), lane : lane + CH2
            ] = taps[CH1 * skip :, part : part + CH2]


def banded_weights(conv1_w, conv1_b, conv2_w, conv2_b):
    return pl.pallas_call(
        weights_kernel,
        out_shape=(
            jax.ShapeDtypeStruct((4 * MAP, ROW1), BF),
            jax.ShapeDtypeStruct((3 * ROW1, ROW2), BF),
            jax.ShapeDtypeStruct((1, ROW1), F32),
            jax.ShapeDtypeStruct((1, ROW2), F32),
        ),
        in_specs=[pl.BlockSpec(memory_space=pltpu.HBM)] * 4,
        scratch_shapes=[
            pltpu.VMEM((3, 3, CH1), BF),
            pltpu.VMEM((9, CH1, CH2), BF),
            pltpu.VMEM((1, CH1), F32),
            pltpu.VMEM((1, CH2), F32),
            pltpu.SemaphoreType.DMA((4,)),
        ],
        cost_estimate=pl.CostEstimate(flops=50_000_000, bytes_accessed=2_000_000, transcendentals=0),
        compiler_params=pltpu.CompilerParams(vmem_limit_bytes=8 << 20),
        interpret=INTERPRET,
    )(
        *map(
            in_hbm,
            (
                jnp.transpose(conv1_w, (0, 2, 1, 3)).reshape(3, 3, CH1),
                conv2_w.reshape(9, CH1, CH2),
                conv1_b[None, :],
                conv2_b[None, :],
            ),
        )
    )


def join_kernel(*refs):
    low = 0
    for ref in refs[:-1]:
        high = low + ref.shape[0]
        refs[-1][low:high] = ref[...]
        low = high


def joined(*blocks):
    count = sum(block.shape[0] for block in blocks)
    vmem = pl.BlockSpec(memory_space=pltpu.VMEM)
    shape = (count,) + blocks[0].shape[1:]
    return pl.pallas_call(
        join_kernel,
        out_shape=jax.ShapeDtypeStruct(shape, BF),
        in_specs=[vmem] * len(blocks),
        out_specs=vmem,
        cost_estimate=pl.CostEstimate(flops=0, bytes_accessed=300_000, transcendentals=0),
        compiler_params=pltpu.CompilerParams(vmem_limit_bytes=4 << 20),
        interpret=INTERPRET,
    )(*blocks)


def trim_kernel(where_ref, blocks_ref, out_ref):
    out_ref[0:2] = blocks_ref[0:2]
    out_ref[2] = blocks_ref[2 + where_ref[3]]


def trimmed(where, blocks):
    vmem = pl.BlockSpec(memory_space=pltpu.VMEM)
    return pl.pallas_call(
        trim_kernel,
        out_shape=jax.ShapeDtypeStruct((3,) + blocks.shape[1:], BF),
        in_specs=[pl.BlockSpec(memory_space=pltpu.SMEM), vmem],
        out_specs=vmem,
        cost_estimate=pl.CostEstimate(flops=0, bytes_accessed=300_000, transcendentals=0),
        compiler_params=pltpu.CompilerParams(vmem_limit_bytes=4 << 20),
        interpret=INTERPRET,
    )(where, blocks)


def correlate(corr, q, z, z_count, low, high, shift):
    chip = lax.rem(z + z_count + shift, z_count)
    cells = jnp.concatenate([low[0:MAP], high[0:MAP], low[MAP:], high[MAP:]], axis=0)
    got = lax.dot_general(q, cells, (((1,), (1,)), ((), ())), preferred_element_type=F32)
    got = (got * 0.0625).astype(BF)
    for side in range(2):
        part = got[:, 128 * side : 128 * (side + 1)]
        y = side * z_count + chip
        corr[y, :, 128:256] = part
        corr[y + 1, :, 0:128] = part


def corr_kernel(z_count, where_ref, q_ref, own_ref, *refs):
    *mine_refs, cross_ref, corr = refs
    z = where_ref[1]
    toward = 2 * where_ref[3] - 1
    q = q_ref[...]
    corr[...] = jnp.zeros(corr.shape, BF)
    correlate(corr, q, z, z_count, own_ref[0], own_ref[1], 0)
    distance = 0
    for ref in mine_refs:
        for k in range(0, ref.shape[0], 2):
            distance += 1
            correlate(corr, q, z, z_count, ref[k], ref[k + 1], toward * distance)
            other = 2 * distance - 2
            low, high = cross_ref[other], cross_ref[other + 1]
            correlate(corr, q, z, z_count, low, high, -toward * distance)


def partial_corr(where, queries, own, blocks):
    vmem = pl.BlockSpec(memory_space=pltpu.VMEM)
    return pl.pallas_call(
        functools.partial(corr_kernel, MAP // 4),
        out_shape=jax.ShapeDtypeStruct((HALF1 + 1, queries.shape[0], 256), BF),
        in_specs=[pl.BlockSpec(memory_space=pltpu.SMEM)] + [vmem] * (2 + len(blocks)),
        out_specs=vmem,
        cost_estimate=pl.CostEstimate(
            flops=250_000_000, bytes_accessed=4_000_000, transcendentals=0
        ),
        compiler_params=pltpu.CompilerParams(vmem_limit_bytes=12 << 20),
        interpret=INTERPRET,
    )(where, queries, own, *blocks)


def cost_kernel(z_count, where_ref, q_ref, last_ref, old_ref, *refs):
    del old_ref
    a_ref, b_ref, bias1_ref, bias2_ref, kept_ref, sent_ref, corr, hid, acc = refs
    z = where_ref[1]
    n = q_ref.shape[0]
    hid[0, :, 0:ROW1] = jnp.zeros((n, ROW1), BF)
    q = q_ref[...]
    correlate(corr, q, z, z_count, last_ref[0], last_ref[1], -7)
    correlate(corr, q, z, z_count, last_ref[3], last_ref[4], 7)
    correlate(corr, q, z, z_count, last_ref[2], last_ref[5], 8)

    bias1 = bias1_ref[...]
    rows1 = 16
    for t in range(HALF1 // rows1):
        lhs = corr[rows1 * t : rows1 * (t + 1)].reshape(rows1 * n, 256)
        got = jnp.dot(lhs, a_ref[...], preferred_element_type=F32)
        got = jnp.maximum(got + bias1, 0.0).astype(BF).reshape(rows1, n, ROW1)
        for s in range(rows1):
            y = rows1 * t + s
            j = y // 2
            if y % 2 == 0:
                hid[j, :, ROW1 : 2 * ROW1] = got[s]
            else:
                hid[j, :, 2 * ROW1 : 3 * ROW1] = got[s]
                hid[j + 1, :, 0:ROW1] = got[s]

    bias2 = bias2_ref[...]
    half = ROW2 // 2
    rows2 = 8
    acc[...] = jnp.zeros(acc.shape, F32)
    for t in range(HALF2 // rows2):
        tile = slice(rows2 * t, rows2 * (t + 1))
        left = jnp.zeros((rows2 * n, half), F32)
        for dy in range(3):
            k = slice(ROW1 * dy, ROW1 * dy + ROW1 // 2)
            left += jnp.dot(
                hid[tile, :, k].reshape(rows2 * n, ROW1 // 2),
                b_ref[k, 0:half],
                preferred_element_type=F32,
            )
        right = jnp.dot(
            hid[tile].reshape(rows2 * n, 3 * ROW1), b_ref[:, half:], preferred_element_type=F32
        )
        left = jnp.maximum(left + bias2[:, :half], 0.0).reshape(rows2, n, half)
        right = jnp.maximum(right + bias2[:, half:], 0.0).reshape(rows2, n, half)
        acc[:, :half] += jnp.sum(left, axis=0)
        acc[:, half:] += jnp.sum(right, axis=0)
    total = acc[:, 0:128]
    for k in range(1, ROW2 // 128):
        total = total + acc[:, 128 * k : 128 * (k + 1)]
    total = (total[:, 0:32] + total[:, 32:64]) + (total[:, 64:96] + total[:, 96:128])
    pooled = (total * (1.0 / (HALF2 * HALF2))).astype(BF)
    kept_ref[...] = pooled[: n // 2]
    sent_ref[...] = pooled[n // 2 :]


def pooled_costs(where, queries, last, corr, a, b, bias1, bias2):
    n = queries.shape[0]
    vmem = pl.BlockSpec(memory_space=pltpu.VMEM)
    return pl.pallas_call(
        functools.partial(cost_kernel, MAP // 4),
        out_shape=(jax.ShapeDtypeStruct((n // 2, CH2), BF),) * 2
        + (jax.ShapeDtypeStruct(corr.shape, BF),),
        in_specs=[pl.BlockSpec(memory_space=pltpu.SMEM)] + [vmem] * 7,
        out_specs=(vmem,) * 3,
        scratch_shapes=[
            pltpu.VMEM((HALF2 + 1, n, 3 * ROW1), BF),
            pltpu.VMEM((n, ROW2), F32),
        ],
        input_output_aliases={3: 2},
        cost_estimate=pl.CostEstimate(
            flops=5_000_000_000, bytes_accessed=4_000_000, transcendentals=0
        ),
        compiler_params=pltpu.CompilerParams(vmem_limit_bytes=28 << 20),
        interpret=INTERPRET,
    )(where, queries, last, corr, a, b, bias1, bias2)[:2]


def tail_kernel(
    frame_count,
    where_ref,
    kept_ref,
    partner_ref,
    straight_ref,
    crossed_ref,
    proj_w_ref,
    proj_b_ref,
    time_w_ref,
    time_b_ref,
    out_ref,
):
    x, frame_block = where_ref[0], where_ref[2]
    first = x == 0
    kept, partner = kept_ref[...], partner_ref[...]
    straight, crossed = straight_ref[...], crossed_ref[...]
    around = [
        jnp.where(first, crossed, straight),
        jnp.where(first, kept, partner),
        jnp.where(first, partner, kept),
        jnp.where(first, straight, crossed),
    ]
    valid = [frame_block > 0, None, None, frame_block < frame_count - 1]
    wide = []
    for pooled, there in zip(around, valid):
        got = jnp.dot(pooled, proj_w_ref[...], preferred_element_type=F32) + proj_b_ref[...]
        got = got.astype(BF).astype(F32)
        if there is not None:
            got = jnp.where(there, got, 0.0)
        wide.append(got)
    for t in range(2):
        mixed = (
            time_w_ref[0:1, :] * wide[t]
            + time_w_ref[1:2, :] * wide[t + 1]
            + time_w_ref[2:3, :] * wide[t + 2]
            + time_b_ref[...]
        )
        out_ref[:, t, :] = mixed.astype(BF)


def tail(frame_count, where, pooled, proj_w, proj_b, time_w, time_b):
    count, width = pooled[0].shape[0], proj_w.shape[1]
    vmem = pl.BlockSpec(memory_space=pltpu.VMEM)
    return pl.pallas_call(
        functools.partial(tail_kernel, frame_count),
        out_shape=jax.ShapeDtypeStruct((count, 2, width), BF),
        in_specs=[pl.BlockSpec(memory_space=pltpu.SMEM)] + [vmem] * 8,
        out_specs=vmem,
        compiler_params=pltpu.CompilerParams(vmem_limit_bytes=8 << 20),
        interpret=INTERPRET,
    )(where, *pooled, proj_w, proj_b[None, :], time_w, time_b[None, :])


def one_device(
    sizes,
    frame_maps,
    query_table,
    start_frame,
    row_ids,
    conv1_w,
    conv1_b,
    conv2_w,
    conv2_b,
    proj_w,
    proj_b,
    time_w,
    time_b,
):
    xh_count, y_count, _, z_count, _ = sizes
    frame_count = xh_count * y_count
    x = lax.axis_index("xl")
    z = lax.axis_index("z")
    frame_block = lax.axis_index("xh") * y_count + lax.axis_index("y")
    where = jnp.stack([x, z, frame_block, lax.axis_index("c")]).astype(jnp.int32)
    swap = [(0, 1), (1, 0)]

    def flip(axis, count, step):
        return lambda v: lax.ppermute(v, axis, [(i, i ^ step) for i in range(count)])

    def along(block, distance):
        pairs = []
        for i in range(z_count):
            pairs.append((2 * i, 2 * ((i + distance) % z_count)))
            pairs.append((2 * i + 1, 2 * ((i - distance) % z_count) + 1))
        return lax.ppermute(block, ("z", "c"), pairs)

    def both(block):
        return lax.all_gather(block, "c", axis=0, tiled=True)

    def behind(value, earlier):
        return lax.optimization_barrier((value, earlier))[0]

    message = opening(where, frame_maps, query_table, start_frame, row_ids)
    gathered = lax.all_gather(message, ("xl", "c"), axis=0)
    own, queries = picked(where, gathered, frame_maps.shape[1])
    weights = banded_weights(conv1_w, conv1_b, conv2_w, conv2_b)
    near = []
    for distance in (1, 2):
        near.append(along(own, distance))
    queries = queries + flip("y", y_count, 1)(queries)
    near = lax.optimization_barrier(near)

    ring = [joined(*near)]
    ring.append(along(ring[0], 2))
    if y_count > 2:
        queries = queries + flip("y", y_count, 2)(behind(queries, ring[0]))
    ring[1], weights = lax.optimization_barrier((ring[1], weights))

    ring.append(along(ring[1], 2))
    if xh_count > 1:
        queries = queries + flip("xh", xh_count, 1)(behind(queries, ring[1]))
    ring[2] = lax.optimization_barrier(ring[2])

    end = trimmed(where, ring[2])
    last = along(end, 2)
    cross = lax.ppermute(joined(*ring), "c", swap)
    corr = partial_corr(where, queries, own, ring + [cross])
    last, corr = lax.optimization_barrier((last, corr))

    kept, sent = pooled_costs(where, queries, both(last), corr, *weights)

    def frame_pairs(cross):
        pairs = []
        for f in range(frame_count):
            if f > 0:
                pairs.append((2 * (f - 1) + 1, 2 * f + (0 if cross else 1)))
            if f < frame_count - 1:
                pairs.append((2 * (f + 1), 2 * f + (1 if cross else 0)))
        return pairs

    partner = lax.ppermute(sent, "xl", swap)
    straight = lax.ppermute(kept, ("xh", "y", "xl"), frame_pairs(False))
    crossed = lax.ppermute(sent, ("xh", "y", "xl"), frame_pairs(True))
    pooled = (kept, partner, straight, crossed)
    return tail(frame_count, where, pooled, proj_w, proj_b, time_w, time_b)


def solution(mesh):

    frames, _ = mesh.devices.shape
    sizes = (frames // 4 or 1, min(frames, 4), 2, MAP // 4, 2)
    fine = Mesh(mesh.devices.reshape(sizes), ("xh", "y", "xl", "z", "c"))
    fr = ("xh", "y")
    qs = ("xl", "z", "c")
    placed = (P(fr, qs, None), P(fr, qs, None), P(qs), P(qs)) + (P(),) * 8
    return jax.shard_map(
        functools.partial(one_device, sizes),
        mesh=fine,
        in_specs=placed,
        out_specs=P(qs, fr, None),
        check_vma=False,
    )
```
